32 devices in a mesh: section: 4 (over z), expert: 8 (over y, x, core).
Axes of the slice: x: 2, y: 2, z: 4, core: 2. Of those that a mesh axis runs over, the one named last changes fastest.
Arguments:
- tokens: bfloat16 [48, 4096], P('expert'), may hold values from -6 to 6
- expert_ids: int32 [4, 48, 1], P('section', 'expert'), may hold values from 0 to 3; in each aligned block of 6 rows (0 to 5, 6 to 11, ..., all dimensions but the last counted through in order) at most 2 rows name the same one
- gate_scale: float32 [4, 48], P('section', 'expert'), may hold values from 0.3 to 1
- norm_gain: float32 [4, 4096], P('section'), may hold values from 0.5 to 1.5
- w_gate: bfloat16 [4, 4096, 4096], P('section', None, 'expert'), may hold values from -0.09375 to 0.09375
- w_up: bfloat16 [4, 4096, 4096], P('section', None, 'expert'), may hold values from -0.09375 to 0.09375
- w_down: bfloat16 [4, 4096, 4096], P('section', 'expert'), may hold values from -0.1875 to 0.1875
Outputs:
- section_out: bfloat16 [4, 48, 4096], P('section', 'expert')
The draws below stay inside these ranges and needn't reach their ends.
Inputs may be any that keep to these rules, and one draw needn't show every extreme that they name: `expert_ids`: within each layer, the 6 tokens of one index of expert choose any one expert at most 2 times.
All inputs are finite; a program needn't handle non-finite values.
Results may differ from the reference program's by a relative error of at most 0.035.
Values may be sent and summed in bfloat16 or wider, within the bound.
No kernel may reach another device: no remote copies, remote signals or barrier semaphores. Data moves between devices by JAX's collectives and lax.ppermute only.
A program may use at most 64 MiB of HBM per device.

```python
import math
import jax
import jax.numpy as jnp
import numpy as np
from jax import lax

D = 4096
FF = 1024
EXPERTS = 4
TOP = 1
TOK_DEV = 6
CAP = 2
SECTIONS = 4
TOKENS = 48
N_EXPERT = 8


def steps_of(key, extent, cuts, low, top_value):
    def one(axis_at, shards_of):
        draws = jax.random.uniform(jax.random.fold_in(jax.random.fold_in(key, 6), axis_at), (shards_of,), jnp.float32, low / len(cuts), top_value / len(cuts))
        return jnp.repeat(jnp.exp(draws), extent[axis_at] // shards_of).reshape((-1,) + (1,) * (len(extent) - axis_at - 1))

    level = one(*cuts[0])
    for cut in cuts[1:]:
        level = level * one(*cut)
    return level


def deal_out(own_key, own, number, rows, count, top, limit, slope):
    ranking = jax.random.permutation(own_key, count)
    packed, common = load_shares(count, rows * top, limit, slope, True), load_shares(count, rows * top, limit, slope, False)
    places = jnp.arange(count)

    def named(tallies, offset_by):
        used = int((tallies > 0).sum())
        fixed = max(1, used // 4)
        passed = fixed + (places - fixed + offset_by * (used - fixed)) % max(1, count - fixed)
        return jnp.zeros((count,), jnp.int32).at[ranking[jnp.where(places < fixed, places, passed)]].set(jnp.asarray(tallies, jnp.int32))

    tallies = jnp.where(number % 4 == 0, named(packed, number // 4), named(common, number - number // 4 - 1))
    mixed = jax.random.permutation(jax.random.fold_in(own, 3), count)
    donor, taker = mixed[0:count // 2 * 2:2], mixed[1:count // 2 * 2:2]
    margin = jnp.minimum(tallies[donor] - 1, limit - tallies[taker]) // 2
    margin = jnp.where((donor == ranking[0]) | (taker == ranking[0]) | (tallies[taker] == 0), 0, jnp.maximum(margin, 0))
    passed = jax.random.randint(jax.random.fold_in(own, 4), (count // 2,), 0, 1 << 20) % (margin + 1)
    tallies = tallies.at[donor].add(-passed).at[taker].add(passed)
    labels = jnp.searchsorted(jnp.cumsum(tallies), jnp.arange(rows * top), side="right").astype(jnp.int32)
    grid = labels.reshape(top, rows).T
    grid = grid[jax.random.permutation(jax.random.fold_in(own, 1), rows)]
    offset_by = jax.random.randint(jax.random.fold_in(own, 2), (rows, 1), 0, top)
    return jnp.take_along_axis(grid, (jnp.arange(top)[None, :] + offset_by) % top, axis=1)


def load_shares(amount, total, limit, skew, full):
    weights = [(1 << 20) // math.isqrt(standing ** skew) + 1 for standing in range(1, amount + 1)]
    largest = limit if full else min(limit, max(-(-total // amount), total * weights[0] // sum(weights)))
    least = 1 if total - largest >= amount - 1 else 0
    counts, rest = [largest] + [least] * (amount - 1), total - largest - least * (amount - 1)
    while rest > 0:
        free = [i for i in range(1, amount) if counts[i] < largest] or [i for i in range(1, amount) if counts[i] < limit]
        whole, remaining = sum([weights[i] for i in free]), rest
        for i in free:
            addition = min(limit - counts[i], max(1, remaining * weights[i] // whole), rest)
            counts[i] = counts[i] + addition
            rest = rest - addition
    return np.array(counts)


def normal_values(stream_key, dims, scale, reach, split=(), kind=jnp.bfloat16):
    loudness = steps_of(stream_key, dims, split, -0.22, 0.18) if split else 1.0
    result = jax.random.normal(stream_key, dims, jnp.float32) * scale * loudness
    return jnp.minimum(jnp.maximum(result, -reach), reach).astype(kind)


def setup_inputs(seed: int = 0) -> dict:
    streams_of = jax.random.split(jax.random.key(seed), 8)
    tokens = normal_values(streams_of[0], (TOKENS, D), 1.0, 6.0, ((0, 8),))
    expert_ids_keys = jax.random.split(jax.random.fold_in(streams_of[1], 1), SECTIONS * TOKENS // TOK_DEV)
    expert_ids_turns = jax.random.permutation(jax.random.fold_in(streams_of[1], 3), SECTIONS * TOKENS // TOK_DEV)
    expert_ids = jax.vmap(lambda own, number: deal_out(jax.random.fold_in(streams_of[1], 2), own, number, TOK_DEV, EXPERTS, TOP, CAP, 2))(expert_ids_keys, expert_ids_turns).reshape((SECTIONS, TOKENS, TOP))
    gate_scale = jnp.clip(0.3 + 0.7 * jax.random.uniform(streams_of[2], (SECTIONS, TOKENS), jnp.float32) ** steps_of(streams_of[2], (SECTIONS, TOKENS), ((0, 4), (1, 8)), -0.2, 0.2), 0.3, 1.0)
    norm_gain = jnp.clip(1.0 + 0.1 * jax.random.normal(streams_of[3], (SECTIONS, D), jnp.float32), 0.5, 1.5)
    w_gate = normal_values(streams_of[4], (SECTIONS, D, EXPERTS * FF), D ** -0.5, 0.09375, ((0, 4), (2, 8)))
    w_up = normal_values(streams_of[5], (SECTIONS, D, EXPERTS * FF), D ** -0.5, 0.09375, ((0, 4), (2, 8)))
    w_down = normal_values(streams_of[6], (SECTIONS, EXPERTS * FF, D), FF ** -0.5, 0.1875, ((0, 4), (1, 8)))
    return dict(tokens=tokens, expert_ids=expert_ids, gate_scale=gate_scale, norm_gain=norm_gain, w_gate=w_gate, w_up=w_up, w_down=w_down)


def norm_rows(state, gain):
    values = state.astype(jnp.float32)
    scale = lax.rsqrt(lax.optimization_barrier(jnp.mean(values * values, axis=-1, keepdims=True)) + 1e-06)
    return (values * scale * gain.astype(jnp.float32)).astype(jnp.bfloat16)

def reference(tokens, expert_ids, gate_scale, norm_gain, w_gate, w_up, w_down):
    group = N_EXPERT // EXPERTS
    width = FF // group
    state = tokens
    results = []
    for layer in range(SECTIONS):
        normed = norm_rows(state, norm_gain[layer])
        chosen = expert_ids[layer, :, 0]
        total = jnp.zeros((TOKENS, D), jnp.float32)
        for expert in range(EXPERTS):
            first = expert * FF
            gate = jnp.dot(normed, w_gate[layer, :, first:first + FF], preferred_element_type=jnp.float32)
            upward = jnp.dot(normed, w_up[layer, :, first:first + FF], preferred_element_type=jnp.float32)
            hidden = (jax.nn.silu(gate) * upward).astype(jnp.bfloat16)
            blocks = hidden.reshape(TOKENS, group, width).astype(jnp.float32)
            downs = w_down[layer, first:first + FF, :].reshape(group, width, D).astype(jnp.float32)
            parts = jnp.einsum('tgh,ghd->tgd', blocks, downs).astype(jnp.bfloat16)
            parts = lax.optimization_barrier(parts).astype(jnp.float32)
            summed = lax.optimization_barrier(jnp.sum(parts, axis=1))
            total = total + jnp.where((chosen == expert)[:, None], summed, jnp.float32(0.0))
        state = (state.astype(jnp.float32) + gate_scale[layer][:, None] * total).astype(jnp.bfloat16)
        results.append(state)
    return jnp.stack(results)
```

```python
import functools

import jax
import jax.numpy as jnp
from jax import lax
from jax.experimental import pallas as pl
from jax.experimental.pallas import tpu as pltpu
from jax.sharding import PartitionSpec as P

EXPERTS = 4
CAP = 2
LANES = 128
BLOCKS = 4
F32 = jnp.float32
BF16 = jnp.bfloat16
VMEM = pl.BlockSpec(memory_space=pltpu.VMEM)


def call(kernel, outs, args, limit=4 << 20, scratch=(), flops=1000, name=None):
    moved = sum(a.size * a.dtype.itemsize for a in args)
    return pl.pallas_call(
        kernel,
        out_shape=outs,
        in_specs=[VMEM] * len(args),
        out_specs=jax.tree.map(lambda _: VMEM, outs),
        scratch_shapes=scratch,
        compiler_params=pltpu.CompilerParams(vmem_limit_bytes=limit),
        cost_estimate=pl.CostEstimate(flops=flops, bytes_accessed=moved, transcendentals=0),
        name=name,
    )(*args)


def shape(dims, kind=BF16):
    return jax.ShapeDtypeStruct(dims, kind)


def place(group):
    index = lax.axis_index("expert")
    return index // group, lax.rem(index, group)


def iota(dims, axis):
    return lax.broadcasted_iota(jnp.int32, dims, axis)


def slot_kernel(group, tokens, ids, scale, *outs):
    expert, _ = place(group)
    rows = tokens.shape[0]
    width = tokens.shape[1]
    ids_row = ids[...]
    ids_full = jnp.broadcast_to(ids_row, (rows, rows))
    diagonal = iota((rows, rows), 0) == iota((rows, rows), 1)
    ids_column = jnp.sum(jnp.where(diagonal, ids_full, 0), axis=1, keepdims=True)
    earlier = iota((rows, rows), 0) < iota((rows, rows), 1)
    rank = jnp.sum(jnp.where((ids_full == ids_column) & earlier, 1, 0), axis=0, keepdims=True)
    position = ids_row * CAP + rank
    slots = EXPERTS * CAP
    index = iota((slots, rows), 0)
    wanted = (expert ^ (index // CAP)) * CAP + lax.rem(index, CAP)
    chosen = jnp.where(position == wanted, 1.0, 0.0).astype(BF16)
    body = jnp.dot(chosen, tokens[...], preferred_element_type=F32)
    value = scale[...]
    first = value.astype(BF16).astype(F32)
    second = (value - first).astype(BF16).astype(F32)
    third = value - first - second
    pieces = (position.astype(F32), first, second, third)
    for i in range(EXPERTS):
        outs[i][:, 0:width] = body[i * CAP : (i + 1) * CAP, :].astype(BF16)
        outs[i][:, width:] = jnp.full((CAP, BLOCKS * LANES), -1.0, BF16)
        for n, piece in enumerate(pieces):
            at = width + n * LANES
            outs[i][:, at : at + rows] = jnp.broadcast_to(piece, (CAP, rows)).astype(BF16)


def expert_math(values, gain, w_gate, w_up, w_down, parts):
    inverse = lax.rsqrt(jnp.mean(values * values, axis=-1, keepdims=True) + 1e-06)
    normed = (values * inverse * gain[...]).astype(BF16)
    gate = jnp.dot(normed, w_gate[0], preferred_element_type=F32)
    upward = jnp.dot(normed, w_up[0], preferred_element_type=F32)
    hidden = (gate / (1.0 + jnp.exp(-gate)) * upward).astype(BF16)
    step = 512
    for at in range(0, values.shape[1], step):
        parts[:, at : at + step] = jnp.dot(
            hidden, w_down[0, :, at : at + step], preferred_element_type=F32
        )


def deal(parts, chunks, own, group):
    width = chunks[0].shape[1]
    for m in range(group):
        at = pl.multiple_of((own ^ m) * width, width)
        chunks[m][...] = parts[:, pl.ds(at, width)].astype(BF16)


def first_kernel(group, *refs):
    count = group * EXPERTS
    pieces = refs[:count]
    gain, w_gate, w_up, w_down = refs[count : count + 4]
    outs = refs[count + 4 : count + 4 + group]
    half, table, position = refs[count + 4 + group : count + 7 + group]
    block, rows, parts = refs[count + 7 + group :]
    _, own = place(group)
    slots = EXPERTS * CAP
    width = gain.shape[1]
    for m in range(group):
        for i in range(EXPERTS):
            block[i * CAP : (i + 1) * CAP, :] = pieces[m * EXPERTS + i][...].astype(F32)
        at = pl.multiple_of((own ^ m) * slots, slots)
        rows[pl.ds(at, slots), :] = block[...]
    table[...] = rows[:, width:].astype(BF16)
    position[...] = rows[:, width : width + LANES].astype(BF16)
    at = pl.multiple_of(own * half.shape[1], half.shape[1])
    half[...] = rows[:, pl.ds(at, half.shape[1])].astype(BF16)

    @pl.when(lax.axis_index("section") == 0)
    def _():
        expert_math(rows[:, 0:width], gain, w_gate, w_up, w_down, parts)
        deal(parts, outs, own, group)


def later_kernel(group, tick, *refs):
    pieces = refs[:group]
    gain, w_gate, w_up, w_down = refs[group : group + 4]
    outs = refs[group + 4 : 2 * group + 4]
    rows, parts = refs[2 * group + 4 :]
    _, own = place(group)

    @pl.when(lax.axis_index("section") == tick)
    def _():
        width = pieces[0].shape[1]
        for m in range(group):
            at = pl.multiple_of((own ^ m) * width, width)
            rows[:, pl.ds(at, width)] = pieces[m][...].astype(F32)
        expert_math(rows[...], gain, w_gate, w_up, w_down, parts)
        deal(parts, outs, own, group)


def slot_codes(expert, dims):
    return expert * CAP + lax.rem(iota(dims, 0), CAP)


def updated(group, pieces, half, table):
    expert, _ = place(group)
    rows = half.shape[0]
    position = table[:, 0:LANES].astype(F32)
    mine = position == slot_codes(expert, (rows, LANES)).astype(F32)
    scale = sum(table[:, n * LANES : (n + 1) * LANES].astype(F32) for n in range(1, BLOCKS))
    scale = jnp.sum(jnp.where(mine, scale, 0.0), axis=1, keepdims=True)
    total = pieces[0][...].astype(F32)
    for piece in pieces[1:]:
        total = total + piece[...].astype(F32)
    return half[...].astype(F32) + scale * total


def update_kernel(group, *refs):
    half, table, out = refs[group:]
    out[...] = updated(group, refs[:group], half, table).astype(BF16)


def last_update_kernel(group, saved, *refs):
    half, table = refs[group : group + 2]
    earlier = refs[group + 2 : group + 2 + saved]
    outs = refs[group + 2 + saved : 2 * group + 2 + saved]
    buffer = refs[-1]
    section = lax.axis_index("section")
    _, own = place(group)
    for n in range(saved):

        @pl.when(section == n)
        def _(n=n):
            buffer[...] = earlier[n][...].astype(F32)

    @pl.when(section == saved)
    def _():
        buffer[...] = updated(group, refs[:group], half, table)

    slots = EXPERTS * CAP
    for m in range(group):
        at = pl.multiple_of((own ^ m) * slots, slots)
        outs[m][...] = buffer[pl.ds(at, slots), :].astype(BF16)


def choice_kernel(group, current, before, out):
    expert, _ = place(group)
    rows = current.shape[0]
    span = EXPERTS * CAP
    here = current[...].astype(F32)
    there = before[...].astype(F32)
    mine = jnp.where(here == slot_codes(expert, here.shape).astype(F32), 1.0, 0.0).astype(BF16)
    a, b = iota((rows, rows), 0), iota((rows, rows), 1)
    for i in range(EXPERTS):
        codes = slot_codes(expert ^ i, there.shape).astype(F32)
        theirs = jnp.where(there == codes, 1.0, 0.0).astype(BF16)
        both = lax.dot_general(
            mine, theirs, (((1,), (1,)), ((), ())), preferred_element_type=F32
        )
        both = jnp.where(a // CAP == b // CAP, both, 0.0).astype(BF16)
        moved = (a // span) * span + (((lax.rem(a, span) // CAP) ^ i) * CAP) + lax.rem(a, CAP)
        order = jnp.where(moved == b, 1.0, 0.0).astype(BF16)
        out[i] = jnp.dot(both, order, preferred_element_type=F32).astype(BF16)


def pick_kernel(*refs):
    choice, out = refs[EXPERTS], refs[EXPERTS + 1]
    total = jnp.dot(choice[0], refs[0][...], preferred_element_type=F32)
    for i in range(1, EXPERTS):
        total = total + jnp.dot(choice[i], refs[i][...], preferred_element_type=F32)
    out[...] = total.astype(BF16)


def split_kernel(group, *refs):
    pieces, outs, rows = refs[:group], refs[group : group + EXPERTS], refs[-1]
    _, own = place(group)
    width = pieces[0].shape[1]
    for m in range(group):
        at = pl.multiple_of((own ^ m) * width, width)
        rows[:, pl.ds(at, width)] = pieces[m][...].astype(F32)
    for i in range(EXPERTS):
        outs[i][...] = rows[i * CAP : (i + 1) * CAP, :].astype(BF16)


def home_kernel(group, *refs):
    table, out, block = refs[EXPERTS:]
    expert, _ = place(group)
    slots = EXPERTS * CAP
    count = out.shape[1]
    for i in range(EXPERTS):
        block[i * CAP : (i + 1) * CAP, :] = refs[i][...].astype(F32)
    position = jnp.broadcast_to(table[0:1, :].astype(F32), (slots, LANES))
    index = iota((slots, LANES), 0)
    wanted = (expert ^ (index // CAP)) * CAP + lax.rem(index, CAP)
    chosen = jnp.where(position == wanted.astype(F32), 1.0, 0.0).astype(BF16)
    full = lax.dot_general(
        chosen, block[...].astype(BF16), (((0,), (0,)), ((), ())), preferred_element_type=F32
    )
    out[0] = full[0:count, :].astype(BF16)


def local(tokens, expert_ids, gate_scale, norm_gain, w_gate, w_up, w_down):
    peers = lax.axis_size("expert")
    sections = lax.axis_size("section")
    count, width = tokens.shape
    group = peers // EXPERTS
    chunk = width // group
    rows = peers * CAP
    slots = EXPERTS * CAP
    wide = width + BLOCKS * LANES
    weights = (norm_gain, w_gate, w_up, w_down)

    def across(value, i):
        pairs = [(d, (d // group ^ i) * group + d % group) for d in range(peers)]
        return lax.ppermute(value, "expert", pairs) if i else value

    def within(value, m):
        return lax.ppermute(value, "expert", [(d, d ^ m) for d in range(peers)])

    def onward(value, i):
        pairs = [
            (s * peers + d, (s + 1) % sections * peers + (d // group ^ i) * group + d % group)
            for s in range(sections)
            for d in range(peers)
        ]
        return lax.ppermute(value, ("section", "expert"), pairs)

    sent = call(
        functools.partial(slot_kernel, group),
        [shape((CAP, wide))] * EXPERTS,
        (tokens, expert_ids.reshape(1, count), gate_scale),
        name="slots",
    )
    arrived = [across(sent[i], i) for i in range(EXPERTS)]
    pieces = list(arrived)
    for m in range(1, group):
        pieces += [within(piece, m) for piece in arrived]
    flops = 6 * rows * width * w_gate.shape[2]
    outs = call(
        functools.partial(first_kernel, group),
        [shape((rows, chunk))] * (group + 1)
        + [shape((rows, BLOCKS * LANES)), shape((rows, LANES))],
        (*pieces, *weights),
        limit=8 << 20,
        scratch=[
            pltpu.VMEM((slots, wide), F32),
            pltpu.VMEM((rows, wide), F32),
            pltpu.VMEM((rows, width), F32),
        ],
        flops=flops,
        name="expert_first",
    )
    parts, half, table, position = outs[:group], outs[group], outs[group + 1], outs[group + 2]
    before = onward(position, 0)
    choice = call(
        functools.partial(choice_kernel, group),
        shape((EXPERTS, rows, rows)),
        (position, before),
        name="choice",
    )
    saved = []
    for tick in range(sections):
        if tick:
            gathered = [onward(saved[-1], i) for i in range(EXPERTS)]
            half = call(pick_kernel, shape((rows, chunk)), (*gathered, choice), name="pick")
            pieces = [half] + [within(half, m) for m in range(1, group)]
            parts = call(
                functools.partial(later_kernel, group, tick),
                [shape((rows, chunk))] * group,
                (*pieces, *weights),
                limit=8 << 20,
                scratch=[pltpu.VMEM((rows, width), F32), pltpu.VMEM((rows, width), F32)],
                flops=flops,
                name="expert",
            )
        terms = [parts[0]] + [within(parts[m], m) for m in range(1, group)]
        if tick < sections - 1:
            saved.append(
                call(
                    functools.partial(update_kernel, group),
                    shape((rows, chunk)),
                    (*terms, half, table),
                    name="update",
                )
            )
    blocks = call(
        functools.partial(last_update_kernel, group, len(saved)),
        [shape((slots, chunk))] * group,
        (*terms, half, table, *saved),
        scratch=[pltpu.VMEM((rows, chunk), F32)],
        name="update_last",
    )
    blocks = [blocks[0]] + [within(blocks[m], m) for m in range(1, group)]
    leaving = call(
        functools.partial(split_kernel, group),
        [shape((CAP, width))] * EXPERTS,
        tuple(blocks),
        scratch=[pltpu.VMEM((slots, width), F32)],
        name="split",
    )
    back = [across(leaving[i], i) for i in range(EXPERTS)]
    return call(
        functools.partial(home_kernel, group),
        shape((1, count, width)),
        (*back, sent[0][:, width : width + LANES]),
        scratch=[pltpu.VMEM((slots, width), F32)],
        name="home",
    )


def solution(mesh):
    return jax.shard_map(
        local,
        mesh=mesh,
        in_specs=(
            P("expert", None),
            P("section", "expert", None),
            P("section", "expert"),
            P("section", None),
            P("section", None, "expert"),
            P("section", None, "expert"),
            P("section", "expert", None),
        ),
        out_specs=P("section", "expert", None),
        check_vma=False,
    )
```

```python
import functools

import jax
import jax.numpy as jnp
from jax import lax
from jax.experimental import pallas as pl
from jax.experimental.pallas import tpu as pltpu
from jax.sharding import PartitionSpec as P

EXPERTS = 4
CAP = 2
LANES = 128
BLOCKS = 4
START_FLOPS = 10_000_000_000
F32 = jnp.float32
BF16 = jnp.bfloat16
VMEM = pl.BlockSpec(memory_space=pltpu.VMEM)


def call(kernel, outs, args, limit=2 << 20, scratch=(), flops=1000, name=None, specs=None, moved=None):
    if moved is None:
        moved = sum(a.size * a.dtype.itemsize for a in args)
    return pl.pallas_call(
        kernel,
        out_shape=outs,
        in_specs=specs or [VMEM] * len(args),
        out_specs=jax.tree.map(lambda _: VMEM, outs),
        scratch_shapes=scratch,
        compiler_params=pltpu.CompilerParams(vmem_limit_bytes=limit),
        cost_estimate=pl.CostEstimate(flops=flops, bytes_accessed=moved, transcendentals=0),
        name=name,
    )(*args)


def shape(dims, kind=BF16):
    return jax.ShapeDtypeStruct(dims, kind)


def place(group):
    index = lax.axis_index("expert")
    return index // group, lax.rem(index, group)


def iota(dims, axis):
    return lax.broadcasted_iota(jnp.int32, dims, axis)


def rank_kernel(ids, out):
    rows = ids.shape[1]
    ids_row = ids[...]
    ids_full = jnp.broadcast_to(ids_row, (rows, rows))
    diagonal = iota((rows, rows), 0) == iota((rows, rows), 1)
    ids_column = jnp.sum(jnp.where(diagonal, ids_full, 0), axis=1, keepdims=True)
    earlier = iota((rows, rows), 0) < iota((rows, rows), 1)
    rank = jnp.sum(jnp.where((ids_full == ids_column) & earlier, 1, 0), axis=0, keepdims=True)
    out[...] = jnp.full(out.shape, -1.0, F32)
    out[:, 0:rows] = jnp.broadcast_to((ids_row * CAP + rank).astype(F32), (out.shape[0], rows))


def slot_kernel(group, position, tokens, scale, *outs):
    expert, _ = place(group)
    rows = tokens.shape[0]
    width = tokens.shape[1]
    codes = position[...]
    index = iota(codes.shape, 0)
    wanted = (expert ^ (index // CAP)) * CAP + lax.rem(index, CAP)
    chosen = jnp.where(codes == wanted.astype(F32), 1.0, 0.0)[:, 0:rows].astype(BF16)
    body = jnp.dot(chosen, tokens[...], preferred_element_type=F32)
    value = scale[...]
    first = value.astype(BF16).astype(F32)
    second = (value - first).astype(BF16).astype(F32)
    third = value - first - second
    for i in range(EXPERTS):
        outs[i][:, 0:width] = body[i * CAP : (i + 1) * CAP, :].astype(BF16)
        outs[i][:, width : width + LANES] = codes[0:CAP, :].astype(BF16)
        outs[i][:, width + LANES :] = jnp.zeros((CAP, (BLOCKS - 1) * LANES), BF16)
        for n, piece in enumerate((first, second, third)):
            at = width + (n + 1) * LANES
            outs[i][:, at : at + rows] = jnp.broadcast_to(piece, (CAP, rows)).astype(BF16)


def expert_math(values, gain, w_gate, w_up, w_down, parts):
    inverse = lax.rsqrt(jnp.mean(values * values, axis=-1, keepdims=True) + 1e-06)
    normed = (values * inverse * gain[...]).astype(BF16)
    gate = jnp.dot(normed, w_gate[0], preferred_element_type=F32)
    upward = jnp.dot(normed, w_up[0], preferred_element_type=F32)
    hidden = (gate / (1.0 + jnp.exp(-gate)) * upward).astype(BF16)
    step = 512
    for at in range(0, values.shape[1], step):
        parts[:, at : at + step] = jnp.dot(
            hidden, w_down[0, :, at : at + step], preferred_element_type=F32
        )


def deal(parts, chunks, own, group):
    width = chunks[0].shape[1]
    for m in range(group):
        at = pl.multiple_of((own ^ m) * width, width)
        chunks[m][...] = parts[:, pl.ds(at, width)].astype(BF16)


def deal_rows(source, blocks, own):
    slots = blocks[0].shape[0]
    for m in range(len(blocks)):
        at = pl.multiple_of((own ^ m) * slots, slots)
        blocks[m][...] = source[pl.ds(at, slots), :].astype(BF16)


def join_kernel(group, width, *refs):
    count = group * EXPERTS
    whole, half, table, position = refs[count : count + 4]
    block, rows = refs[count + 4 :]
    _, own = place(group)
    slots = EXPERTS * CAP
    for m in range(group):
        for i in range(EXPERTS):
            block[i * CAP : (i + 1) * CAP, :] = refs[m * EXPERTS + i][...].astype(F32)
        at = pl.multiple_of((own ^ m) * slots, slots)
        rows[pl.ds(at, slots), :] = block[...]
    table[...] = rows[:, width:].astype(BF16)
    position[...] = rows[:, width : width + LANES].astype(BF16)
    at = pl.multiple_of(own * half.shape[1], half.shape[1])
    half[...] = rows[:, pl.ds(at, half.shape[1])].astype(BF16)
    whole[...] = rows[:, 0:width].astype(BF16)


def expert_kernel(group, tick, count, last, *refs):
    pieces = refs[:count]
    gain, w_gate, w_up, w_down = refs[count : count + 4]
    outs = refs[count + 4 : count + 4 + group]
    rows, parts = refs[-2:]
    _, own = place(group)

    @pl.when(lax.axis_index("section") == tick)
    def _():
        width = pieces[0].shape[1]
        for m in range(count):
            at = pl.multiple_of((own ^ m) * width, width) if count > 1 else 0
            rows[:, pl.ds(at, width)] = pieces[m][...].astype(F32)
        expert_math(rows[...], gain, w_gate, w_up, w_down, parts)
        if last:
            deal_rows(parts, outs, own)
            deal_rows(rows, refs[count + 4 + group : count + 5 + group], own)
        else:
            deal(parts, outs, own, group)


def slot_codes(expert, dims):
    return expert * CAP + lax.rem(iota(dims, 0), CAP)


def scales(expert, table):
    rows = table.shape[0]
    position = table[:, 0:LANES].astype(F32)
    mine = position == slot_codes(expert, (rows, LANES)).astype(F32)
    scale = sum(table[:, n * LANES : (n + 1) * LANES].astype(F32) for n in range(1, BLOCKS))
    return jnp.sum(jnp.where(mine, scale, 0.0), axis=1, keepdims=True)


def updated(pieces, before, scale):
    total = pieces[0][...].astype(F32)
    for piece in pieces[1:]:
        total = total + piece[...].astype(F32)
    return before[...].astype(F32) + scale * total


def update_kernel(group, *refs):
    half, table, out = refs[group], refs[group + 1], refs[-1]
    expert, _ = place(group)
    out[...] = updated(refs[:group], half, scales(expert, table)).astype(BF16)


def keep_kernel(group, saved, *refs):
    outs, buffer = refs[saved : saved + group], refs[-1]
    section = lax.axis_index("section")
    _, own = place(group)
    for n in range(saved):

        @pl.when(section == n)
        def _(n=n):
            buffer[...] = refs[n][...].astype(F32)

    deal_rows(buffer, outs, own)


def leave_kernel(group, *refs):
    before, table = refs[group : group + 2]
    kept = refs[group + 2 : 2 * group + 2]
    outs = refs[2 * group + 2 : 2 * group + 2 + EXPERTS]
    column, rows = refs[-2:]
    slots = EXPERTS * CAP
    final = lax.axis_size("section") - 1
    section = lax.axis_index("section")
    expert, own = place(group)

    @pl.when(section == final)
    def _():
        column[...] = jnp.broadcast_to(scales(expert, table), column.shape)
        at = pl.multiple_of(own * slots, slots)
        scale = column[pl.ds(at, slots), :][:, 0:1]
        rows[...] = updated(refs[:group], before, scale)

    @pl.when(section != final)
    def _():
        width = kept[0].shape[1]
        for m in range(group):
            at = pl.multiple_of((own ^ m) * width, width)
            rows[:, pl.ds(at, width)] = kept[m][...].astype(F32)

    for i in range(EXPERTS):
        outs[i][...] = rows[i * CAP : (i + 1) * CAP, :].astype(BF16)


def choice_kernel(group, current, before, out):
    expert, _ = place(group)
    rows = current.shape[0]
    span = EXPERTS * CAP
    here = current[...].astype(F32)
    there = before[...].astype(F32)
    mine = jnp.where(here == slot_codes(expert, here.shape).astype(F32), 1.0, 0.0).astype(BF16)
    a, b = iota((rows, rows), 0), iota((rows, rows), 1)
    for i in range(EXPERTS):
        codes = slot_codes(expert ^ i, there.shape).astype(F32)
        theirs = jnp.where(there == codes, 1.0, 0.0).astype(BF16)
        both = lax.dot_general(
            mine, theirs, (((1,), (1,)), ((), ())), preferred_element_type=F32
        )
        both = jnp.where(a // CAP == b // CAP, both, 0.0).astype(BF16)
        moved = (a // span) * span + (((lax.rem(a, span) // CAP) ^ i) * CAP) + lax.rem(a, CAP)
        order = jnp.where(moved == b, 1.0, 0.0).astype(BF16)
        out[i] = jnp.dot(both, order, preferred_element_type=F32).astype(BF16)


def pick_kernel(*refs):
    choice, out = refs[EXPERTS], refs[-1]
    total = jnp.dot(choice[0], refs[0][...], preferred_element_type=F32)
    for i in range(1, EXPERTS):
        total = total + jnp.dot(choice[i], refs[i][...], preferred_element_type=F32)
    out[...] = total.astype(BF16)


def home_kernel(group, *refs):
    table, out, block = refs[EXPERTS:]
    expert, _ = place(group)
    slots = EXPERTS * CAP
    count = out.shape[1]
    for i in range(EXPERTS):
        block[i * CAP : (i + 1) * CAP, :] = refs[i][...].astype(F32)
    lanes = -(-count // 16) * 16
    position = jnp.broadcast_to(table[0:1, 0:lanes].astype(F32), (slots, lanes))
    index = iota((slots, lanes), 0)
    wanted = (expert ^ (index // CAP)) * CAP + lax.rem(index, CAP)
    chosen = jnp.where(position == wanted.astype(F32), 1.0, 0.0).astype(BF16)
    full = lax.dot_general(
        chosen, block[...].astype(BF16), (((0,), (0,)), ((), ())), preferred_element_type=F32
    )
    out[0] = full[0:count, :].astype(BF16)


def local(tokens, expert_ids, gate_scale, norm_gain, w_gate, w_up, w_down):
    peers = lax.axis_size("expert")
    sections = lax.axis_size("section")
    count, width = tokens.shape
    group = peers // EXPERTS
    chunk = width // group
    rows = peers * CAP
    slots = EXPERTS * CAP
    wide = width + BLOCKS * LANES
    weights = (norm_gain, w_gate, w_up, w_down)

    def across(value, i):
        pairs = [(d, (d // group ^ i) * group + d % group) for d in range(peers)]
        return lax.ppermute(value, "expert", pairs) if i else value

    def within(value, m):
        return lax.ppermute(value, "expert", [(d, d ^ m) for d in range(peers)])

    def onward(value, hops, i):
        pairs = [
            (s * peers + d, hops[s] * peers + (d // group ^ i) * group + d % group)
            for s in range(sections)
            for d in range(peers)
        ]
        return lax.ppermute(value, ("section", "expert"), pairs)

    def cycle(tick, turn):
        hops = list(range(sections))
        others = [(tick + n) % sections for n in range(2, sections)]
        ring = [tick, tick + 1] + (others[turn : turn + 1] if turn < 2 else [])
        for n, s in enumerate(ring):
            hops[s] = ring[(n + 1) % len(ring)]
        return hops

    position = call(
        rank_kernel,
        shape((slots, LANES), F32),
        (expert_ids.reshape(1, count),),
        flops=START_FLOPS,
        name="rank",
    )
    sent = call(
        functools.partial(slot_kernel, group),
        [shape((CAP, wide))] * EXPERTS,
        (position, tokens, gate_scale),
        name="slots",
    )
    arrived = [across(sent[i], i) for i in range(EXPERTS)]
    pieces = list(arrived)
    for m in range(1, group):
        pieces += [within(piece, m) for piece in arrived]
    flops = 6 * rows * width * w_gate.shape[2]
    whole, half, table, position = call(
        functools.partial(join_kernel, group, width),
        [shape((rows, width)), shape((rows, chunk)), shape((rows, BLOCKS * LANES)), shape((rows, LANES))],
        tuple(pieces),
        scratch=[pltpu.VMEM((slots, wide), F32), pltpu.VMEM((rows, wide), F32)],
        name="join",
    )
    before = onward(position, [(s + 1) % sections for s in range(sections)], 0)
    choice = call(
        functools.partial(choice_kernel, group),
        shape((EXPERTS, rows, rows)),
        (position, before),
        name="choice",
    )
    saved = []
    pieces = [whole]
    for tick in range(sections):
        last = tick == sections - 1
        if tick:
            gathered = [
                onward(saved[-1], cycle(tick - 1, EXPERTS - 1 - i), i) for i in range(EXPERTS)
            ]
            kept = []
            if last:
                kept = call(
                    functools.partial(keep_kernel, group, len(saved)),
                    [shape((slots, chunk))] * group,
                    tuple(saved),
                    scratch=[pltpu.VMEM((rows, chunk), F32)],
                    name="keep",
                )
                kept = [kept[0]] + [within(kept[m], m) for m in range(1, group)]
            half = call(
                pick_kernel, shape((rows, chunk)), (*gathered, choice, *kept), name="pick"
            )
            pieces = [half] + [within(half, m) for m in range(1, group)]
        parts = call(
            functools.partial(expert_kernel, group, tick, len(pieces), last),
            [shape((slots, width))] * (group + 1) if last else [shape((rows, chunk))] * group,
            (*pieces, *weights),
            limit=4 << 20,
            scratch=[pltpu.VMEM((rows, width), F32), pltpu.VMEM((rows, width), F32)],
            flops=flops,
            name="expert",
        )
        terms = [parts[0]] + [within(parts[m], m) for m in range(1, group)]
        if not last:
            hold = () if tick else (choice,)
            saved.append(
                call(
                    functools.partial(update_kernel, group),
                    shape((rows, chunk)),
                    (*terms, half, table, *hold),
                    name="update",
                )
            )
    leaving = call(
        functools.partial(leave_kernel, group),
        [shape((CAP, width))] * EXPERTS,
        (*terms, parts[group], table, *kept),
        scratch=[pltpu.VMEM((rows, LANES), F32), pltpu.VMEM((slots, width), F32)],
        name="leave",
    )
    back = [across(leaving[i], i) for i in range(EXPERTS)]
    return call(
        functools.partial(home_kernel, group),
        shape((1, count, width)),
        (*back, sent[0][:, width : width + LANES]),
        scratch=[pltpu.VMEM((slots, width), F32)],
        name="home",
    )


def solution(mesh):
    return jax.shard_map(
        local,
        mesh=mesh,
        in_specs=(
            P("expert", None),
            P("section", "expert", None),
            P("section", "expert"),
            P("section", None),
            P("section", None, "expert"),
            P("section", None, "expert"),
            P("section", "expert", None),
        ),
        out_specs=P("section", "expert", None),
        check_vma=False,
    )
```

```python
import functools

import jax
import jax.numpy as jnp
from jax import lax
from jax.experimental import pallas as pl
from jax.experimental.pallas import tpu as pltpu
from jax.sharding import PartitionSpec as P


EXPERTS = 4
CAP = 2
LANES = 128
BLOCKS = 4
START_FLOPS = 10_000_000_000
F32 = jnp.float32
BF16 = jnp.bfloat16
VMEM = pl.BlockSpec(memory_space=pltpu.VMEM)


def call(kernel, outs, args, limit=2 << 20, scratch=(), flops=1000, specs=None, moved=None):
    if moved is None:
        moved = sum(a.size * a.dtype.itemsize for a in args)
    return pl.pallas_call(
        kernel,
        out_shape=outs,
        in_specs=specs or [VMEM] * len(args),
        out_specs=jax.tree.map(lambda _: VMEM, outs),
        scratch_shapes=scratch,
        compiler_params=pltpu.CompilerParams(vmem_limit_bytes=limit),
        cost_estimate=pl.CostEstimate(flops=flops, bytes_accessed=moved, transcendentals=0),
    )(*args)


def shape(dims, kind=BF16):
    return jax.ShapeDtypeStruct(dims, kind)


def place(group):
    index = lax.axis_index("expert")
    return index // group, lax.rem(index, group)


def iota(dims, axis):
    return lax.broadcasted_iota(jnp.int32, dims, axis)


def rank_kernel(ids, out):
    rows = ids.shape[1]
    ids_row = ids[...]
    ids_full = jnp.broadcast_to(ids_row, (rows, rows))
    diagonal = iota((rows, rows), 0) == iota((rows, rows), 1)
    ids_column = jnp.sum(jnp.where(diagonal, ids_full, 0), axis=1, keepdims=True)
    earlier = iota((rows, rows), 0) < iota((rows, rows), 1)
    rank = jnp.sum(jnp.where((ids_full == ids_column) & earlier, 1, 0), axis=0, keepdims=True)
    out[...] = jnp.full(out.shape, -1.0, F32)
    out[:, 0:rows] = jnp.broadcast_to((ids_row * CAP + rank).astype(F32), (out.shape[0], rows))


def slot_kernel(group, position, tokens, scale, *outs):
    expert, _ = place(group)
    rows = tokens.shape[0]
    width = tokens.shape[1]
    codes = position[...]
    index = iota(codes.shape, 0)
    wanted = (expert ^ (index // CAP)) * CAP + lax.rem(index, CAP)
    chosen = jnp.where(codes == wanted.astype(F32), 1.0, 0.0)[:, 0:rows].astype(BF16)
    body = jnp.dot(chosen, tokens[...], preferred_element_type=F32)
    value = scale[...]
    first = value.astype(BF16).astype(F32)
    second = (value - first).astype(BF16).astype(F32)
    third = value - first - second
    for i in range(EXPERTS):
        outs[i][:, 0:width] = body[i * CAP : (i + 1) * CAP, :].astype(BF16)
        outs[i][:, width : width + LANES] = codes[0:CAP, :].astype(BF16)
        outs[i][:, width + LANES :] = jnp.zeros((CAP, (BLOCKS - 1) * LANES), BF16)
        for n, piece in enumerate((first, second, third)):
            at = width + (n + 1) * LANES
            outs[i][:, at : at + rows] = jnp.broadcast_to(piece, (CAP, rows)).astype(BF16)


def expert_math(values, gain, w_gate, w_up, w_down, parts):
    inverse = lax.rsqrt(jnp.mean(values * values, axis=-1, keepdims=True) + 1e-06)
    normed = (values * inverse * gain[...]).astype(BF16)
    gate = jnp.dot(normed, w_gate[0], preferred_element_type=F32)
    upward = jnp.dot(normed, w_up[0], preferred_element_type=F32)
    hidden = (gate / (1.0 + jnp.exp(-gate)) * upward).astype(BF16)
    step = 512
    for at in range(0, values.shape[1], step):
        parts[:, at : at + step] = jnp.dot(
            hidden, w_down[0, :, at : at + step], preferred_element_type=F32
        )


def deal(parts, chunks, own, group):
    width = chunks[0].shape[1]
    for m in range(group):
        at = pl.multiple_of((own ^ m) * width, width)
        chunks[m][...] = parts[:, pl.ds(at, width)].astype(BF16)


def deal_rows(source, blocks, own):
    slots = blocks[0].shape[0]
    for m in range(len(blocks)):
        at = pl.multiple_of((own ^ m) * slots, slots)
        blocks[m][...] = source[pl.ds(at, slots), :].astype(BF16)


def join_kernel(group, width, *refs):
    count = group * EXPERTS
    whole, half, table, position = refs[count : count + 4]
    block, rows = refs[count + 4 :]
    _, own = place(group)
    slots = EXPERTS * CAP
    for m in range(group):
        for i in range(EXPERTS):
            block[i * CAP : (i + 1) * CAP, :] = refs[m * EXPERTS + i][...].astype(F32)
        at = pl.multiple_of((own ^ m) * slots, slots)
        rows[pl.ds(at, slots), :] = block[...]
    table[...] = rows[:, width:].astype(BF16)
    position[...] = rows[:, width : width + LANES].astype(BF16)
    at = pl.multiple_of(own * half.shape[1], half.shape[1])
    half[...] = rows[:, pl.ds(at, half.shape[1])].astype(BF16)
    whole[...] = rows[:, 0:width].astype(BF16)


def expert_kernel(group, tick, count, last, *refs):
    pieces = refs[:count]
    gain, w_gate, w_up, w_down = refs[count : count + 4]
    outs = refs[count + 4 : count + 4 + group]
    rows, parts = refs[-2:]
    _, own = place(group)

    @pl.when(lax.axis_index("section") == tick)
    def _():
        width = pieces[0].shape[1]
        for m in range(count):
            at = pl.multiple_of((own ^ m) * width, width) if count > 1 else 0
            rows[:, pl.ds(at, width)] = pieces[m][...].astype(F32)
        expert_math(rows[...], gain, w_gate, w_up, w_down, parts)
        if last:
            deal_rows(parts, outs, own)
            deal_rows(rows, refs[count + 4 + group : count + 5 + group], own)
        else:
            deal(parts, outs, own, group)


def slot_codes(expert, dims):
    return expert * CAP + lax.rem(iota(dims, 0), CAP)


def scales(expert, table):
    rows = table.shape[0]
    position = table[:, 0:LANES].astype(F32)
    mine = position == slot_codes(expert, (rows, LANES)).astype(F32)
    scale = sum(table[:, n * LANES : (n + 1) * LANES].astype(F32) for n in range(1, BLOCKS))
    return jnp.sum(jnp.where(mine, scale, 0.0), axis=1, keepdims=True)


def updated(pieces, before, scale):
    total = pieces[0][...].astype(F32)
    for piece in pieces[1:]:
        total = total + piece[...].astype(F32)
    return before[...].astype(F32) + scale * total


def update_kernel(group, *refs):
    half, table, out = refs[group], refs[group + 1], refs[-1]
    expert, _ = place(group)
    out[...] = updated(refs[:group], half, scales(expert, table)).astype(BF16)


def keep_kernel(group, saved, *refs):
    outs, buffer = refs[saved : saved + group], refs[-1]
    section = lax.axis_index("section")
    _, own = place(group)
    for n in range(saved):

        @pl.when(section == n)
        def _(n=n):
            buffer[...] = refs[n][...].astype(F32)

    deal_rows(buffer, outs, own)


def leave_kernel(group, *refs):
    before, table = refs[group : group + 2]
    kept = refs[group + 2 : 2 * group + 2]
    outs = refs[2 * group + 2 : 2 * group + 2 + EXPERTS]
    column, rows = refs[-2:]
    slots = EXPERTS * CAP
    final = lax.axis_size("section") - 1
    section = lax.axis_index("section")
    expert, own = place(group)

    @pl.when(section == final)
    def _():
        column[...] = jnp.broadcast_to(scales(expert, table), column.shape)
        at = pl.multiple_of(own * slots, slots)
        scale = column[pl.ds(at, slots), :][:, 0:1]
        rows[...] = updated(refs[:group], before, scale)

    @pl.when(section != final)
    def _():
        width = kept[0].shape[1]
        for m in range(group):
            at = pl.multiple_of((own ^ m) * width, width)
            rows[:, pl.ds(at, width)] = kept[m][...].astype(F32)

    for i in range(EXPERTS):
        outs[i][...] = rows[i * CAP : (i + 1) * CAP, :].astype(BF16)


def choice_kernel(group, current, before, out):
    expert, _ = place(group)
    rows = current.shape[0]
    span = EXPERTS * CAP
    here = current[...].astype(F32)
    there = before[...].astype(F32)
    mine = jnp.where(here == slot_codes(expert, here.shape).astype(F32), 1.0, 0.0).astype(BF16)
    a, b = iota((rows, rows), 0), iota((rows, rows), 1)
    for i in range(EXPERTS):
        codes = slot_codes(expert ^ i, there.shape).astype(F32)
        theirs = jnp.where(there == codes, 1.0, 0.0).astype(BF16)
        both = lax.dot_general(
            mine, theirs, (((1,), (1,)), ((), ())), preferred_element_type=F32
        )
        both = jnp.where(a // CAP == b // CAP, both, 0.0).astype(BF16)
        moved = (a // span) * span + (((lax.rem(a, span) // CAP) ^ i) * CAP) + lax.rem(a, CAP)
        order = jnp.where(moved == b, 1.0, 0.0).astype(BF16)
        out[i] = jnp.dot(both, order, preferred_element_type=F32).astype(BF16)


def pick_kernel(*refs):
    choice, out = refs[EXPERTS], refs[-1]
    total = jnp.dot(choice[0], refs[0][...], preferred_element_type=F32)
    for i in range(1, EXPERTS):
        total = total + jnp.dot(choice[i], refs[i][...], preferred_element_type=F32)
    out[...] = total.astype(BF16)


def home_kernel(group, *refs):
    table, out, block = refs[EXPERTS:]
    expert, _ = place(group)
    slots = EXPERTS * CAP
    count = out.shape[1]
    for i in range(EXPERTS):
        block[i * CAP : (i + 1) * CAP, :] = refs[i][...].astype(F32)
    lanes = -(-count // 16) * 16
    position = jnp.broadcast_to(table[0:1, 0:lanes].astype(F32), (slots, lanes))
    index = iota((slots, lanes), 0)
    wanted = (expert ^ (index // CAP)) * CAP + lax.rem(index, CAP)
    chosen = jnp.where(position == wanted.astype(F32), 1.0, 0.0).astype(BF16)
    full = lax.dot_general(
        chosen, block[...].astype(BF16), (((0,), (0,)), ((), ())), preferred_element_type=F32
    )
    out[0] = full[0:count, :].astype(BF16)


def local(tokens, expert_ids, gate_scale, norm_gain, w_gate, w_up, w_down):
    peers = lax.axis_size("expert")
    sections = lax.axis_size("section")
    count, width = tokens.shape
    group = peers // EXPERTS
    chunk = width // group
    rows = peers * CAP
    slots = EXPERTS * CAP
    wide = width + BLOCKS * LANES
    weights = (norm_gain, w_gate, w_up, w_down)

    def across(value, i):
        pairs = [(d, (d // group ^ i) * group + d % group) for d in range(peers)]
        if i == 0:
            return value
        return lax.ppermute(value, "expert", pairs)

    def within(value, m):
        return lax.ppermute(value, "expert", [(d, d ^ m) for d in range(peers)])

    def onward(value, hops, i):
        pairs = [
            (s * peers + d, hops[s] * peers + (d // group ^ i) * group + d % group)
            for s in range(sections)
            for d in range(peers)
        ]
        return lax.ppermute(value, ("section", "expert"), pairs)

    def cycle(tick, turn):
        hops = list(range(sections))
        others = [(tick + n) % sections for n in range(2, sections)]
        ring = [tick, tick + 1] + (others[turn : turn + 1] if turn < 2 else [])
        for n, s in enumerate(ring):
            hops[s] = ring[(n + 1) % len(ring)]
        return hops

    position = call(
        rank_kernel, shape((slots, LANES), F32), (expert_ids.reshape(1, count),), flops=START_FLOPS
    )
    sent = call(
        functools.partial(slot_kernel, group),
        [shape((CAP, wide))] * EXPERTS,
        (position, tokens, gate_scale),
    )
    arrived = [across(sent[i], i) for i in range(EXPERTS)]
    pieces = list(arrived)
    for m in range(1, group):
        pieces += [within(piece, m) for piece in arrived]
    flops = 6 * rows * width * w_gate.shape[2]
    whole, half, table, position = call(
        functools.partial(join_kernel, group, width),
        [shape((rows, width)), shape((rows, chunk)), shape((rows, BLOCKS * LANES)), shape((rows, LANES))],
        tuple(pieces),
        scratch=[pltpu.VMEM((slots, wide), F32), pltpu.VMEM((rows, wide), F32)],
    )
    before = onward(position, [(s + 1) % sections for s in range(sections)], 0)
    choice = call(
        functools.partial(choice_kernel, group), shape((EXPERTS, rows, rows)), (position, before)
    )
    saved = []
    pieces = [whole]
    for tick in range(sections):
        last = tick == sections - 1
        if tick:
            gathered = [
                onward(saved[-1], cycle(tick - 1, EXPERTS - 1 - i), i) for i in range(EXPERTS)
            ]
            kept = []
            if last:
                kept = call(
                    functools.partial(keep_kernel, group, len(saved)),
                    [shape((slots, chunk))] * group,
                    tuple(saved),
                    scratch=[pltpu.VMEM((rows, chunk), F32)],
                )
                kept = [kept[0]] + [within(kept[m], m) for m in range(1, group)]
            half = call(pick_kernel, shape((rows, chunk)), (*gathered, choice, *kept))
            pieces = [half] + [within(half, m) for m in range(1, group)]
        parts = call(
            functools.partial(expert_kernel, group, tick, len(pieces), last),
            [shape((slots, width))] * (group + 1) if last else [shape((rows, chunk))] * group,
            (*pieces, *weights),
            limit=4 << 20,
            scratch=[pltpu.VMEM((rows, width), F32), pltpu.VMEM((rows, width), F32)],
            flops=flops,
        )
        terms = [parts[0]] + [within(parts[m], m) for m in range(1, group)]
        if not last:
            saved.append(
                call(
                    functools.partial(update_kernel, group),
                    shape((rows, chunk)),
                    (*terms, half, table),
                )
            )
    leaving = call(
        functools.partial(leave_kernel, group),
        [shape((CAP, width))] * EXPERTS,
        (*terms, parts[group], table, *kept),
        scratch=[pltpu.VMEM((rows, LANES), F32), pltpu.VMEM((slots, width), F32)],
    )
    back = [across(leaving[i], i) for i in range(EXPERTS)]
    return call(
        functools.partial(home_kernel, group),
        shape((1, count, width)),
        (*back, sent[0][:, width : width + LANES]),
        scratch=[pltpu.VMEM((slots, width), F32)],
    )


def solution(mesh):
    return jax.shard_map(
        local,
        mesh=mesh,
        in_specs=(
            P("expert", None),
            P("section", "expert", None),
            P("section", "expert"),
            P("section", None),
            P("section", None, "expert"),
            P("section", None, "expert"),
            P("section", "expert", None),
        ),
        out_specs=P("section", "expert", None),
        check_vma=False,
    )
```

```python
import functools

import jax
import jax.numpy as jnp
from jax import lax
from jax.experimental import pallas as pl
from jax.experimental.pallas import tpu as pltpu
from jax.sharding import PartitionSpec as P


EXPERTS = 4
CAP = 2
LANES = 128
BLOCKS = 4
START_FLOPS = 10_000_000_000
F32 = jnp.float32
BF16 = jnp.bfloat16
VMEM = pl.BlockSpec(memory_space=pltpu.VMEM)


def call(kernel, outs, args, limit=4 << 20, scratch=(), flops=1000, specs=None, moved=None):
    if moved is None:
        moved = sum(a.size * a.dtype.itemsize for a in args)
    return pl.pallas_call(
        kernel,
        out_shape=outs,
        in_specs=specs or [VMEM] * len(args),
        out_specs=jax.tree.map(lambda _: VMEM, outs),
        scratch_shapes=scratch,
        compiler_params=pltpu.CompilerParams(vmem_limit_bytes=limit),
        cost_estimate=pl.CostEstimate(flops=flops, bytes_accessed=moved, transcendentals=0),
    )(*args)


def shape(dims, kind=BF16):
    return jax.ShapeDtypeStruct(dims, kind)


def place(group):
    index = lax.axis_index("expert")
    return index // group, lax.rem(index, group)


def iota(dims, axis):
    return lax.broadcasted_iota(jnp.int32, dims, axis)


def rank_kernel(ids, out):
    rows = ids.shape[1]
    ids_row = ids[...]
    ids_full = jnp.broadcast_to(ids_row, (rows, rows))
    diagonal = iota((rows, rows), 0) == iota((rows, rows), 1)
    ids_column = jnp.sum(jnp.where(diagonal, ids_full, 0), axis=1, keepdims=True)
    earlier = iota((rows, rows), 0) < iota((rows, rows), 1)
    rank = jnp.sum(jnp.where((ids_full == ids_column) & earlier, 1, 0), axis=0, keepdims=True)
    out[...] = jnp.full(out.shape, -1.0, F32)
    out[:, 0:rows] = jnp.broadcast_to((ids_row * CAP + rank).astype(F32), (out.shape[0], rows))


def slot_kernel(group, position, tokens, scale, *outs):
    expert, _ = place(group)
    rows = tokens.shape[0]
    width = tokens.shape[1]
    codes = position[...]
    index = iota(codes.shape, 0)
    wanted = (expert ^ (index // CAP)) * CAP + lax.rem(index, CAP)
    chosen = jnp.where(codes == wanted.astype(F32), 1.0, 0.0)[:, 0:rows].astype(BF16)
    body = jnp.dot(chosen, tokens[...], preferred_element_type=F32)
    value = scale[...]
    first = value.astype(BF16).astype(F32)
    second = (value - first).astype(BF16).astype(F32)
    third = value - first - second
    for i in range(EXPERTS):
        outs[i][:, 0:width] = body[i * CAP : (i + 1) * CAP, :].astype(BF16)
        outs[i][:, width : width + LANES] = codes[0:CAP, :].astype(BF16)
        outs[i][:, width + LANES :] = jnp.zeros((CAP, (BLOCKS - 1) * LANES), BF16)
        for n, piece in enumerate((first, second, third)):
            at = width + (n + 1) * LANES
            outs[i][:, at : at + rows] = jnp.broadcast_to(piece, (CAP, rows)).astype(BF16)


def hidden_of(gate, upward):
    return (gate / (1.0 + jnp.exp(-gate)) * upward).astype(BF16)


def down(hidden, w_down, first, out):
    step = min(512, out.shape[1])
    for n in range(0, out.shape[1], step):
        at = first + n if isinstance(first, int) else pl.multiple_of(first + n, step)
        out[:, n : n + step] = jnp.dot(
            hidden, w_down[0, :, pl.ds(at, step)], preferred_element_type=F32
        ).astype(out.dtype)


def active(tick):
    return pl.when(lax.axis_index("section") == tick)


def deal_rows(source, blocks, own):
    slots = blocks[0].shape[0]
    for m in range(len(blocks)):
        at = pl.multiple_of((own ^ m) * slots, slots)
        blocks[m][...] = source[pl.ds(at, slots), :].astype(BF16)


def join_kernel(group, width, *refs):
    count = group * EXPERTS
    whole, half, table, position = refs[count : count + 4]
    block, rows = refs[count + 4 :]
    _, own = place(group)
    slots = EXPERTS * CAP
    for m in range(group):
        for i in range(EXPERTS):
            block[i * CAP : (i + 1) * CAP, :] = refs[m * EXPERTS + i][...].astype(F32)
        at = pl.multiple_of((own ^ m) * slots, slots)
        rows[pl.ds(at, slots), :] = block[...]
    table[...] = rows[:, width:].astype(BF16)
    position[...] = rows[:, width : width + LANES].astype(BF16)
    at = pl.multiple_of(own * half.shape[1], half.shape[1])
    half[...] = rows[:, pl.ds(at, half.shape[1])].astype(BF16)
    whole[...] = rows[:, 0:width].astype(BF16)


def whole_kernel(group, tick, rows, gain, w_gate, w_up, w_down, *outs):
    _, own = place(group)

    @active(tick)
    def _():
        values = rows[...].astype(F32)
        inverse = lax.rsqrt(jnp.mean(values * values, axis=-1, keepdims=True) + 1e-06)
        normed = (values * inverse * gain[...]).astype(BF16)
        gate = jnp.dot(normed, w_gate[0], preferred_element_type=F32)
        upward = jnp.dot(normed, w_up[0], preferred_element_type=F32)
        hidden = hidden_of(gate, upward)
        outs[0][...] = hidden
        width = outs[1].shape[1]
        for m in range(1, group):
            down(hidden, w_down, pl.multiple_of((own ^ m) * width, width), outs[m])


def products(half, at, gain, w_gate, w_up):
    width = half.shape[1]
    values = half[...].astype(F32)
    scaled = (values * gain[:, pl.ds(at, width)]).astype(BF16)
    gate = jnp.dot(scaled, w_gate[0, pl.ds(at, width), :], preferred_element_type=F32)
    upward = jnp.dot(scaled, w_up[0, pl.ds(at, width), :], preferred_element_type=F32)
    return gate, upward, jnp.sum(values * values, axis=-1, keepdims=True)


def half_kernel(group, tick, half, gain, w_gate, w_up, gate_out, up_out, square_out):
    _, own = place(group)

    @active(tick)
    def _():
        width = half.shape[1]
        at = pl.multiple_of(own * width, width)
        gate, upward, square = products(half, at, gain, w_gate, w_up)
        gate_out[...] = gate
        up_out[...] = upward
        square_out[...] = jnp.broadcast_to(square, square_out.shape)


def rest_kernel(group, tick, last, *refs):
    halves = refs[:group]
    gate_in, up_in, square_in, gain, w_gate, w_up, w_down = refs[group : group + 7]
    outs = refs[group + 7 :]
    _, own = place(group)

    @active(tick)
    def _():
        gate, upward, square = gate_in[...], up_in[...], square_in[:, 0:1]
        width = halves[0].shape[1]
        for m in range(1, group):
            at = pl.multiple_of((own ^ m) * width, width)
            more = products(halves[m], at, gain, w_gate, w_up)
            gate, upward, square = gate + more[0], upward + more[1], square + more[2]
        inverse = lax.rsqrt(square / gain.shape[1] + 1e-06)
        hidden = hidden_of(gate * inverse, upward * inverse)
        if last:
            rows, parts = outs[-2:]
            for m in range(group):
                at = pl.multiple_of((own ^ m) * width, width)
                rows[:, pl.ds(at, width)] = halves[m][...].astype(F32)
            down(hidden, w_down, 0, parts)
            deal_rows(parts, outs[:group], own)
            deal_rows(rows, outs[group : group + 1], own)
        else:
            outs[0][...] = hidden
            for m in range(1, group):
                down(hidden, w_down, pl.multiple_of((own ^ m) * width, width), outs[m])


def own_kernel(group, tick, hidden, w_down, out):
    _, own = place(group)

    @active(tick)
    def _():
        down(hidden[...], w_down, pl.multiple_of(own * out.shape[1], out.shape[1]), out)


def slot_codes(expert, dims):
    return expert * CAP + lax.rem(iota(dims, 0), CAP)


def scales(expert, table):
    rows = table.shape[0]
    position = table[:, 0:LANES].astype(F32)
    mine = position == slot_codes(expert, (rows, LANES)).astype(F32)
    scale = sum(table[:, n * LANES : (n + 1) * LANES].astype(F32) for n in range(1, BLOCKS))
    return jnp.sum(jnp.where(mine, scale, 0.0), axis=1, keepdims=True)


def updated(pieces, before, scale):
    total = pieces[0][...].astype(F32)
    for piece in pieces[1:]:
        total = total + piece[...].astype(F32)
    return before[...].astype(F32) + scale * total


def update_kernel(group, *refs):
    half, table, out = refs[group], refs[group + 1], refs[-1]
    expert, _ = place(group)
    out[...] = updated(refs[:group], half, scales(expert, table)).astype(BF16)


def keep_kernel(group, saved, *refs):
    outs, buffer = refs[saved : saved + group], refs[-1]
    section = lax.axis_index("section")
    _, own = place(group)
    for n in range(saved):

        @pl.when(section == n)
        def _(n=n):
            buffer[...] = refs[n][...].astype(F32)

    deal_rows(buffer, outs, own)


def leave_kernel(group, *refs):
    before, table = refs[group : group + 2]
    kept = refs[group + 2 : 2 * group + 2]
    outs = refs[2 * group + 2 : 2 * group + 2 + EXPERTS]
    column, rows = refs[-2:]
    slots = EXPERTS * CAP
    final = lax.axis_size("section") - 1
    section = lax.axis_index("section")
    expert, own = place(group)

    @pl.when(section == final)
    def _():
        column[...] = jnp.broadcast_to(scales(expert, table), column.shape)
        at = pl.multiple_of(own * slots, slots)
        scale = column[pl.ds(at, slots), :][:, 0:1]
        rows[...] = updated(refs[:group], before, scale)

    @pl.when(section != final)
    def _():
        width = kept[0].shape[1]
        for m in range(group):
            at = pl.multiple_of((own ^ m) * width, width)
            rows[:, pl.ds(at, width)] = kept[m][...].astype(F32)

    for i in range(EXPERTS):
        outs[i][...] = rows[i * CAP : (i + 1) * CAP, :].astype(BF16)


def choice_kernel(group, current, before, out):
    expert, _ = place(group)
    rows = current.shape[0]
    span = EXPERTS * CAP
    here = current[...].astype(F32)
    there = before[...].astype(F32)
    mine = jnp.where(here == slot_codes(expert, here.shape).astype(F32), 1.0, 0.0).astype(BF16)
    a, b = iota((rows, rows), 0), iota((rows, rows), 1)
    for i in range(EXPERTS):
        codes = slot_codes(expert ^ i, there.shape).astype(F32)
        theirs = jnp.where(there == codes, 1.0, 0.0).astype(BF16)
        both = lax.dot_general(
            mine, theirs, (((1,), (1,)), ((), ())), preferred_element_type=F32
        )
        both = jnp.where(a // CAP == b // CAP, both, 0.0).astype(BF16)
        moved = (a // span) * span + (((lax.rem(a, span) // CAP) ^ i) * CAP) + lax.rem(a, CAP)
        order = jnp.where(moved == b, 1.0, 0.0).astype(BF16)
        out[i] = jnp.dot(both, order, preferred_element_type=F32).astype(BF16)


def pick_kernel(*refs):
    choice, out = refs[EXPERTS], refs[-1]
    total = jnp.dot(choice[0], refs[0][...], preferred_element_type=F32)
    for i in range(1, EXPERTS):
        total = total + jnp.dot(choice[i], refs[i][...], preferred_element_type=F32)
    out[...] = total.astype(BF16)


def home_kernel(group, *refs):
    table, out, block = refs[EXPERTS:]
    expert, _ = place(group)
    slots = EXPERTS * CAP
    count = out.shape[1]
    for i in range(EXPERTS):
        block[i * CAP : (i + 1) * CAP, :] = refs[i][...].astype(F32)
    lanes = -(-count // 16) * 16
    position = jnp.broadcast_to(table[0:1, 0:lanes].astype(F32), (slots, lanes))
    index = iota((slots, lanes), 0)
    wanted = (expert ^ (index // CAP)) * CAP + lax.rem(index, CAP)
    chosen = jnp.where(position == wanted.astype(F32), 1.0, 0.0).astype(BF16)
    full = lax.dot_general(
        chosen, block[...].astype(BF16), (((0,), (0,)), ((), ())), preferred_element_type=F32
    )
    out[0] = full[0:count, :].astype(BF16)


def local(tokens, expert_ids, gate_scale, norm_gain, w_gate, w_up, w_down):
    peers = lax.axis_size("expert")
    sections = lax.axis_size("section")
    count, width = tokens.shape
    group = peers // EXPERTS
    chunk = width // group
    rows = peers * CAP
    slots = EXPERTS * CAP
    wide = width + BLOCKS * LANES
    weights = (norm_gain, w_gate, w_up, w_down)

    def across(value, i):
        pairs = [(d, (d // group ^ i) * group + d % group) for d in range(peers)]
        if i == 0:
            return value
        return lax.ppermute(value, "expert", pairs)

    def within(value, m):
        return lax.ppermute(value, "expert", [(d, d ^ m) for d in range(peers)])

    def onward(value, hops, moves):
        pairs = [
            (s * peers + d, hops[s] * peers + (d // group ^ moves[s]) * group + d % group)
            for s in range(sections)
            for d in range(peers)
        ]
        return lax.ppermute(value, ("section", "expert"), pairs)

    def gather(value, tick):
        outs = []
        for i in range(EXPERTS):
            moves = [i if s == tick else 0 for s in range(sections)]
            outs.append(onward(value, cycle(tick, EXPERTS - 1 - i), moves))
        return outs

    def cycle(tick, turn):
        hops = list(range(sections))
        others = [(tick + n) % sections for n in range(2, sections)]
        ring = [tick, tick + 1] + (others[turn : turn + 1] if turn < 2 else [])
        for n, s in enumerate(ring):
            hops[s] = ring[(n + 1) % len(ring)]
        return hops

    position = call(
        rank_kernel, shape((slots, LANES), F32), (expert_ids.reshape(1, count),), flops=START_FLOPS
    )
    sent = call(
        functools.partial(slot_kernel, group),
        [shape((CAP, wide))] * EXPERTS,
        (position, tokens, gate_scale),
    )
    arrived = [across(sent[i], i) for i in range(EXPERTS)]
    pieces = list(arrived)
    for m in range(1, group):
        pieces += [within(piece, m) for piece in arrived]
    flops = 6 * rows * width * w_gate.shape[2]
    whole, half, table, position = call(
        functools.partial(join_kernel, group, width),
        [shape((rows, width)), shape((rows, chunk)), shape((rows, BLOCKS * LANES)), shape((rows, LANES))],
        tuple(pieces),
        scratch=[pltpu.VMEM((slots, wide), F32), pltpu.VMEM((rows, wide), F32)],
    )
    before = onward(position, [(s + 1) % sections for s in range(sections)], [0] * sections)
    choice = call(
        functools.partial(choice_kernel, group), shape((EXPERTS, rows, rows)), (position, before)
    )
    saved = []
    inner = w_gate.shape[2]
    for tick in range(sections):
        last = tick == sections - 1
        if tick:
            gathered = gather(saved[-1], tick - 1)
            kept = []
            if last:
                kept = call(
                    functools.partial(keep_kernel, group, len(saved)),
                    [shape((slots, chunk))] * group,
                    tuple(saved),
                    scratch=[pltpu.VMEM((rows, chunk), F32)],
                )
                kept = [kept[0]] + [within(kept[m], m) for m in range(1, group)]
            half = call(pick_kernel, shape((rows, chunk)), (*gathered, choice, *kept))
            halves = [half] + [within(half, m) for m in range(1, group)]
            begun = call(
                functools.partial(half_kernel, group, tick),
                [shape((rows, inner), F32)] * 2 + [shape((rows, LANES), F32)],
                (half, *weights[:3]),
                flops=flops // (3 * group) * 2,
            )
            outs = [shape((rows, inner))] + [shape((rows, chunk))] * (group - 1)
            scratch = []
            if last:
                outs = [shape((slots, width))] * (group + 1)
                scratch = [pltpu.VMEM((rows, width), F32)] * 2
            outs = call(
                functools.partial(rest_kernel, group, tick, last),
                outs,
                (*halves, *begun, *weights),
                scratch=scratch,
                flops=flops // 2,
            )
        else:
            outs = call(
                functools.partial(whole_kernel, group, tick),
                [shape((rows, inner))] + [shape((rows, chunk))] * (group - 1),
                (whole, *weights),
                flops=flops * 5 // 6,
            )
        terms = [within(outs[m], m) for m in range(1, group)]
        if last:
            terms = [outs[0]] + terms
        else:
            own = call(
                functools.partial(own_kernel, group, tick),
                shape((rows, chunk)),
                (outs[0], w_down),
                flops=flops // 6,
            )
            terms = [own] + terms
        if not last:
            saved.append(
                call(
                    functools.partial(update_kernel, group),
                    shape((rows, chunk)),
                    (*terms, half, table),
                )
            )
    leaving = call(
        functools.partial(leave_kernel, group),
        [shape((CAP, width))] * EXPERTS,
        (*terms, outs[group], table, *kept),
        scratch=[pltpu.VMEM((rows, LANES), F32), pltpu.VMEM((slots, width), F32)],
    )
    back = [across(leaving[i], i) for i in range(EXPERTS)]
    return call(
        functools.partial(home_kernel, group),
        shape((1, count, width)),
        (*back, sent[0][:, width : width + LANES]),
        scratch=[pltpu.VMEM((slots, width), F32)],
    )


def solution(mesh):
    return jax.shard_map(
        local,
        mesh=mesh,
        in_specs=(
            P("expert", None),
            P("section", "expert", None),
            P("section", "expert"),
            P("section", None),
            P("section", None, "expert"),
            P("section", None, "expert"),
            P("section", "expert", None),
        ),
        out_specs=P("section", "expert", None),
        check_vma=False,
    )
```

```python
import functools

import jax
import jax.numpy as jnp
from jax import lax
from jax.experimental import pallas as pl
from jax.experimental.pallas import tpu as pltpu
from jax.sharding import PartitionSpec as P


EXPERTS = 4
CAP = 2
LANES = 128
BLOCKS = 4
START_FLOPS = 10_000_000_000
F32 = jnp.float32
BF16 = jnp.bfloat16
VMEM = pl.BlockSpec(memory_space=pltpu.VMEM)


def call(kernel, outs, args, limit=4 << 20, scratch=(), flops=1000, specs=None, moved=None):
    if moved is None:
        moved = sum(a.size * a.dtype.itemsize for a in args)
    return pl.pallas_call(
        kernel,
        out_shape=outs,
        in_specs=specs or [VMEM] * len(args),
        out_specs=jax.tree.map(lambda _: VMEM, outs),
        scratch_shapes=scratch,
        compiler_params=pltpu.CompilerParams(vmem_limit_bytes=limit),
        cost_estimate=pl.CostEstimate(flops=flops, bytes_accessed=moved, transcendentals=0),
    )(*args)


def shape(dims, kind=BF16):
    return jax.ShapeDtypeStruct(dims, kind)


def place(group):
    index = lax.axis_index("expert")
    return index // group, lax.rem(index, group)


def iota(dims, axis):
    return lax.broadcasted_iota(jnp.int32, dims, axis)


def rank_kernel(ids, out):
    rows = ids.shape[1]
    ids_row = ids[...]
    ids_full = jnp.broadcast_to(ids_row, (rows, rows))
    diagonal = iota((rows, rows), 0) == iota((rows, rows), 1)
    ids_column = jnp.sum(jnp.where(diagonal, ids_full, 0), axis=1, keepdims=True)
    earlier = iota((rows, rows), 0) < iota((rows, rows), 1)
    rank = jnp.sum(jnp.where((ids_full == ids_column) & earlier, 1, 0), axis=0, keepdims=True)
    out[...] = jnp.full(out.shape, -1.0, F32)
    out[:, 0:rows] = jnp.broadcast_to((ids_row * CAP + rank).astype(F32), (out.shape[0], rows))


def slot_kernel(group, position, tokens, scale, *outs):
    expert, _ = place(group)
    rows = tokens.shape[0]
    width = tokens.shape[1]
    codes = position[...]
    index = iota(codes.shape, 0)
    wanted = (expert ^ (index // CAP)) * CAP + lax.rem(index, CAP)
    chosen = jnp.where(codes == wanted.astype(F32), 1.0, 0.0)[:, 0:rows].astype(BF16)
    body = jnp.dot(chosen, tokens[...], preferred_element_type=F32)
    value = scale[...]
    first = value.astype(BF16).astype(F32)
    second = (value - first).astype(BF16).astype(F32)
    third = value - first - second
    for i in range(EXPERTS):
        outs[i][:, 0:width] = body[i * CAP : (i + 1) * CAP, :].astype(BF16)
        outs[i][:, width : width + LANES] = codes[0:CAP, :].astype(BF16)
        outs[i][:, width + LANES :] = jnp.zeros((CAP, (BLOCKS - 1) * LANES), BF16)
        for n, piece in enumerate((first, second, third)):
            at = width + (n + 1) * LANES
            outs[i][:, at : at + rows] = jnp.broadcast_to(piece, (CAP, rows)).astype(BF16)


def hidden_of(gate, upward):
    return (gate / (1.0 + jnp.exp(-gate)) * upward).astype(BF16)


def down(hidden, w_down, first, out):
    step = min(512, out.shape[1])
    for n in range(0, out.shape[1], step):
        at = first + n if isinstance(first, int) else pl.multiple_of(first + n, step)
        out[:, n : n + step] = jnp.dot(
            hidden, w_down[0, :, pl.ds(at, step)], preferred_element_type=F32
        ).astype(out.dtype)


def active(tick):
    return pl.when(lax.axis_index("section") == tick)


def deal_rows(source, blocks, own):
    slots = blocks[0].shape[0]
    for m in range(len(blocks)):
        at = pl.multiple_of((own ^ m) * slots, slots)
        blocks[m][...] = source[pl.ds(at, slots), :].astype(BF16)


def join_kernel(group, width, *refs):
    count = group * EXPERTS
    whole, half, table, position = refs[count : count + 4]
    block, rows = refs[count + 4 :]
    _, own = place(group)
    slots = EXPERTS * CAP
    for m in range(group):
        for i in range(EXPERTS):
            block[i * CAP : (i + 1) * CAP, :] = refs[m * EXPERTS + i][...].astype(F32)
        at = pl.multiple_of((own ^ m) * slots, slots)
        rows[pl.ds(at, slots), :] = block[...]
    table[...] = rows[:, width:].astype(BF16)
    position[...] = rows[:, width : width + LANES].astype(BF16)
    at = pl.multiple_of(own * half.shape[1], half.shape[1])
    half[...] = rows[:, pl.ds(at, half.shape[1])].astype(BF16)
    whole[...] = rows[:, 0:width].astype(BF16)


def whole_kernel(group, tick, rows, gain, w_gate, w_up, w_down, *outs):
    _, own = place(group)

    @active(tick)
    def _():
        values = rows[...].astype(F32)
        inverse = lax.rsqrt(jnp.mean(values * values, axis=-1, keepdims=True) + 1e-06)
        normed = (values * inverse * gain[...]).astype(BF16)
        gate = jnp.dot(normed, w_gate[0], preferred_element_type=F32)
        upward = jnp.dot(normed, w_up[0], preferred_element_type=F32)
        hidden = hidden_of(gate, upward)
        outs[0][...] = hidden
        width = outs[1].shape[1]
        for m in range(1, group):
            down(hidden, w_down, pl.multiple_of((own ^ m) * width, width), outs[m])


def products(half, at, gain, w_gate, w_up):
    width = half.shape[1]
    values = half[...].astype(F32)
    scaled = (values * gain[:, pl.ds(at, width)]).astype(BF16)
    gate = jnp.dot(scaled, w_gate[0, pl.ds(at, width), :], preferred_element_type=F32)
    upward = jnp.dot(scaled, w_up[0, pl.ds(at, width), :], preferred_element_type=F32)
    return gate, upward, jnp.sum(values * values, axis=-1, keepdims=True)


def half_kernel(group, tick, half, gain, w_gate, w_up, gate_out, up_out, square_out):
    _, own = place(group)

    @active(tick)
    def _():
        width = half.shape[1]
        at = pl.multiple_of(own * width, width)
        gate, upward, square = products(half, at, gain, w_gate, w_up)
        gate_out[...] = gate
        up_out[...] = upward
        square_out[...] = jnp.broadcast_to(square, square_out.shape)


def rest_kernel(group, tick, last, *refs):
    halves = refs[:group]
    gate_in, up_in, square_in, gain, w_gate, w_up, w_down = refs[group : group + 7]
    outs = refs[group + 7 :]
    _, own = place(group)

    @active(tick)
    def _():
        gate, upward, square = gate_in[...], up_in[...], square_in[:, 0:1]
        width = halves[0].shape[1]
        for m in range(1, group):
            at = pl.multiple_of((own ^ m) * width, width)
            more = products(halves[m], at, gain, w_gate, w_up)
            gate, upward, square = gate + more[0], upward + more[1], square + more[2]
        inverse = lax.rsqrt(square / gain.shape[1] + 1e-06)
        hidden = hidden_of(gate * inverse, upward * inverse)
        if last:
            rows, parts = outs[-2:]
            for m in range(group):
                at = pl.multiple_of((own ^ m) * width, width)
                rows[:, pl.ds(at, width)] = halves[m][...].astype(F32)
            down(hidden, w_down, 0, parts)
            deal_rows(parts, outs[:group], own)
            deal_rows(rows, outs[group : group + 1], own)
        else:
            outs[0][...] = hidden
            for m in range(1, group):
                down(hidden, w_down, pl.multiple_of((own ^ m) * width, width), outs[m])


def own_kernel(group, tick, hidden, w_down, out):
    _, own = place(group)

    @active(tick)
    def _():
        down(hidden[...], w_down, pl.multiple_of(own * out.shape[1], out.shape[1]), out)


def slot_codes(expert, dims):
    return expert * CAP + lax.rem(iota(dims, 0), CAP)


def scales(expert, table):
    rows = table.shape[0]
    position = table[:, 0:LANES].astype(F32)
    mine = position == slot_codes(expert, (rows, LANES)).astype(F32)
    scale = sum(table[:, n * LANES : (n + 1) * LANES].astype(F32) for n in range(1, BLOCKS))
    return jnp.sum(jnp.where(mine, scale, 0.0), axis=1, keepdims=True)


def updated(pieces, before, scale):
    total = pieces[0][...].astype(F32)
    for piece in pieces[1:]:
        total = total + piece[...].astype(F32)
    return before[...].astype(F32) + scale * total


def update_kernel(group, *refs):
    half, table, out = refs[group], refs[group + 1], refs[-1]
    expert, _ = place(group)
    out[...] = updated(refs[:group], half, scales(expert, table)).astype(BF16)


def keep_kernel(group, saved, *refs):
    outs, buffer = refs[saved : saved + group], refs[-1]
    section = lax.axis_index("section")
    _, own = place(group)
    for n in range(saved):

        @pl.when(section == n)
        def _(n=n):
            buffer[...] = refs[n][...].astype(F32)

    deal_rows(buffer, outs, own)


def leave_kernel(group, *refs):
    before, table = refs[group : group + 2]
    kept = refs[group + 2 : 2 * group + 2]
    outs = refs[2 * group + 2 : 2 * group + 2 + EXPERTS]
    column, rows = refs[-2:]
    slots = EXPERTS * CAP
    final = lax.axis_size("section") - 1
    section = lax.axis_index("section")
    expert, own = place(group)

    @pl.when(section == final)
    def _():
        column[...] = jnp.broadcast_to(scales(expert, table), column.shape)
        at = pl.multiple_of(own * slots, slots)
        scale = column[pl.ds(at, slots), :][:, 0:1]
        rows[...] = updated(refs[:group], before, scale)

    @pl.when(section != final)
    def _():
        width = kept[0].shape[1]
        for m in range(group):
            at = pl.multiple_of((own ^ m) * width, width)
            rows[:, pl.ds(at, width)] = kept[m][...].astype(F32)

    for i in range(EXPERTS):
        outs[i][...] = rows[i * CAP : (i + 1) * CAP, :].astype(BF16)


def choice_kernel(group, current, before, out):
    expert, _ = place(group)
    rows = current.shape[0]
    span = EXPERTS * CAP
    here = current[...].astype(F32)
    there = before[...].astype(F32)
    mine = jnp.where(here == slot_codes(expert, here.shape).astype(F32), 1.0, 0.0).astype(BF16)
    a, b = iota((rows, rows), 0), iota((rows, rows), 1)
    for i in range(EXPERTS):
        codes = slot_codes(expert ^ i, there.shape).astype(F32)
        theirs = jnp.where(there == codes, 1.0, 0.0).astype(BF16)
        both = lax.dot_general(
            mine, theirs, (((1,), (1,)), ((), ())), preferred_element_type=F32
        )
        both = jnp.where(a // CAP == b // CAP, both, 0.0).astype(BF16)
        moved = (a // span) * span + (((lax.rem(a, span) // CAP) ^ i) * CAP) + lax.rem(a, CAP)
        order = jnp.where(moved == b, 1.0, 0.0).astype(BF16)
        out[i] = jnp.dot(both, order, preferred_element_type=F32).astype(BF16)


def pick_kernel(*refs):
    choice, out = refs[EXPERTS], refs[-1]
    total = jnp.dot(choice[0], refs[0][...], preferred_element_type=F32)
    for i in range(1, EXPERTS):
        total = total + jnp.dot(choice[i], refs[i][...], preferred_element_type=F32)
    out[...] = total.astype(BF16)


def home_kernel(group, *refs):
    table, out, block = refs[EXPERTS:]
    expert, _ = place(group)
    slots = EXPERTS * CAP
    count = out.shape[1]
    for i in range(EXPERTS):
        block[i * CAP : (i + 1) * CAP, :] = refs[i][...].astype(F32)
    lanes = -(-count // 16) * 16
    position = jnp.broadcast_to(table[0:1, 0:lanes].astype(F32), (slots, lanes))
    index = iota((slots, lanes), 0)
    wanted = (expert ^ (index // CAP)) * CAP + lax.rem(index, CAP)
    chosen = jnp.where(position == wanted.astype(F32), 1.0, 0.0).astype(BF16)
    full = lax.dot_general(
        chosen, block[...].astype(BF16), (((0,), (0,)), ((), ())), preferred_element_type=F32
    )
    out[0] = full[0:count, :].astype(BF16)


def local(tokens, expert_ids, gate_scale, norm_gain, w_gate, w_up, w_down):
    peers = lax.axis_size("expert")
    sections = lax.axis_size("section")
    count, width = tokens.shape
    group = peers // EXPERTS
    chunk = width // group
    rows = peers * CAP
    slots = EXPERTS * CAP
    wide = width + BLOCKS * LANES
    weights = (norm_gain, w_gate, w_up, w_down)

    def across(value, i):
        pairs = [(d, (d // group ^ i) * group + d % group) for d in range(peers)]
        if i == 0:
            return value
        return lax.ppermute(value, "expert", pairs)

    def within(value, m):
        return lax.ppermute(value, "expert", [(d, d ^ m) for d in range(peers)])

    def onward(value, hops, i):
        pairs = [
            (s * peers + d, hops[s] * peers + (d // group ^ i) * group + d % group)
            for s in range(sections)
            for d in range(peers)
        ]
        return lax.ppermute(value, ("section", "expert"), pairs)

    def gather(value, tick):
        return [onward(value, cycle(tick, EXPERTS - 1 - i), i) for i in range(EXPERTS)]

    def cycle(tick, turn):
        hops = list(range(sections))
        others = [(tick + n) % sections for n in range(2, sections)]
        ring = [tick, tick + 1] + (others[turn : turn + 1] if turn < 2 else [])
        for n, s in enumerate(ring):
            hops[s] = ring[(n + 1) % len(ring)]
        return hops

    position = call(
        rank_kernel, shape((slots, LANES), F32), (expert_ids.reshape(1, count),), flops=START_FLOPS
    )
    sent = call(
        functools.partial(slot_kernel, group),
        [shape((CAP, wide))] * EXPERTS,
        (position, tokens, gate_scale),
    )
    arrived = [across(sent[i], i) for i in range(EXPERTS)]
    pieces = list(arrived)
    for m in range(1, group):
        pieces += [within(piece, m) for piece in arrived]
    flops = 6 * rows * width * w_gate.shape[2]
    whole, half, table, position = call(
        functools.partial(join_kernel, group, width),
        [shape((rows, width)), shape((rows, chunk)), shape((rows, BLOCKS * LANES)), shape((rows, LANES))],
        tuple(pieces),
        scratch=[pltpu.VMEM((slots, wide), F32), pltpu.VMEM((rows, wide), F32)],
    )
    before = onward(position, [(s + 1) % sections for s in range(sections)], 0)
    choice = call(
        functools.partial(choice_kernel, group), shape((EXPERTS, rows, rows)), (position, before)
    )
    saved = []
    inner = w_gate.shape[2]
    for tick in range(sections):
        last = tick == sections - 1
        if tick:
            gathered = gather(saved[-1], tick - 1)
            kept = []
            if last:
                kept = call(
                    functools.partial(keep_kernel, group, len(saved)),
                    [shape((slots, chunk))] * group,
                    tuple(saved),
                    scratch=[pltpu.VMEM((rows, chunk), F32)],
                )
                kept = [kept[0]] + [within(kept[m], m) for m in range(1, group)]
            half = call(pick_kernel, shape((rows, chunk)), (*gathered, choice, *kept))
            halves = [half] + [within(half, m) for m in range(1, group)]
            begun = call(
                functools.partial(half_kernel, group, tick),
                [shape((rows, inner), F32)] * 2 + [shape((rows, LANES), F32)],
                (half, *weights[:3]),
                flops=flops // (3 * group) * 2,
            )
            outs = [shape((rows, inner))] + [shape((rows, chunk))] * (group - 1)
            scratch = []
            if last:
                outs = [shape((slots, width))] * (group + 1)
                scratch = [pltpu.VMEM((rows, width), F32)] * 2
            outs = call(
                functools.partial(rest_kernel, group, tick, last),
                outs,
                (*halves, *begun, *weights),
                scratch=scratch,
                flops=flops // 2,
            )
        else:
            outs = call(
                functools.partial(whole_kernel, group, tick),
                [shape((rows, inner))] + [shape((rows, chunk))] * (group - 1),
                (whole, *weights),
                flops=flops * 5 // 6,
            )
        terms = [within(outs[m], m) for m in range(1, group)]
        if last:
            terms = [outs[0]] + terms
        else:
            own = call(
                functools.partial(own_kernel, group, tick),
                shape((rows, chunk)),
                (outs[0], w_down),
                flops=flops // 6,
            )
            terms = [own] + terms
        if not last:
            saved.append(
                call(
                    functools.partial(update_kernel, group),
                    shape((rows, chunk)),
                    (*terms, half, table),
                )
            )
    leaving = call(
        functools.partial(leave_kernel, group),
        [shape((CAP, width))] * EXPERTS,
        (*terms, outs[group], table, *kept),
        scratch=[pltpu.VMEM((rows, LANES), F32), pltpu.VMEM((slots, width), F32)],
    )
    back = [across(leaving[i], i) for i in range(EXPERTS)]
    return call(
        functools.partial(home_kernel, group),
        shape((1, count, width)),
        (*back, sent[0][:, width : width + LANES]),
        scratch=[pltpu.VMEM((slots, width), F32)],
    )


def solution(mesh):
    return jax.shard_map(
        local,
        mesh=mesh,
        in_specs=(
            P("expert", None),
            P("section", "expert", None),
            P("section", "expert"),
            P("section", None),
            P("section", None, "expert"),
            P("section", None, "expert"),
            P("section", "expert", None),
        ),
        out_specs=P("section", "expert", None),
        check_vma=False,
    )
```

```python
import functools

import jax
import jax.numpy as jnp
from jax import lax
from jax.experimental import pallas as pl
from jax.experimental.pallas import tpu as pltpu
from jax.sharding import PartitionSpec as P


EXPERTS = 4
CAP = 2
LANES = 128
BLOCKS = 4
START_FLOPS = 10_000_000_000
F32 = jnp.float32
BF16 = jnp.bfloat16
VMEM = pl.BlockSpec(memory_space=pltpu.VMEM)


def call(kernel, outs, args, limit=4 << 20, scratch=(), flops=1000, specs=None, moved=None):
    if moved is None:
        moved = sum(a.size * a.dtype.itemsize for a in args)
    return pl.pallas_call(
        kernel,
        out_shape=outs,
        in_specs=specs or [VMEM] * len(args),
        out_specs=jax.tree.map(lambda _: VMEM, outs),
        scratch_shapes=scratch,
        compiler_params=pltpu.CompilerParams(vmem_limit_bytes=limit),
        cost_estimate=pl.CostEstimate(flops=flops, bytes_accessed=moved, transcendentals=0),
    )(*args)


def shape(dims, kind=BF16):
    return jax.ShapeDtypeStruct(dims, kind)


def place(group):
    index = lax.axis_index("expert")
    return index // group, lax.rem(index, group)


def iota(dims, axis):
    return lax.broadcasted_iota(jnp.int32, dims, axis)


def rank_kernel(ids, out):
    rows = ids.shape[1]
    ids_row = ids[...]
    ids_full = jnp.broadcast_to(ids_row, (rows, rows))
    diagonal = iota((rows, rows), 0) == iota((rows, rows), 1)
    ids_column = jnp.sum(jnp.where(diagonal, ids_full, 0), axis=1, keepdims=True)
    earlier = iota((rows, rows), 0) < iota((rows, rows), 1)
    rank = jnp.sum(jnp.where((ids_full == ids_column) & earlier, 1, 0), axis=0, keepdims=True)
    out[...] = jnp.full(out.shape, -1.0, F32)
    out[:, 0:rows] = jnp.broadcast_to((ids_row * CAP + rank).astype(F32), (out.shape[0], rows))


def slot_kernel(group, position, tokens, scale, *outs):
    expert, _ = place(group)
    rows = tokens.shape[0]
    width = tokens.shape[1]
    codes = position[...]
    index = iota(codes.shape, 0)
    wanted = (expert ^ (index // CAP)) * CAP + lax.rem(index, CAP)
    chosen = jnp.where(codes == wanted.astype(F32), 1.0, 0.0)[:, 0:rows].astype(BF16)
    body = jnp.dot(chosen, tokens[...], preferred_element_type=F32)
    value = scale[...]
    first = value.astype(BF16).astype(F32)
    second = (value - first).astype(BF16).astype(F32)
    third = value - first - second
    for i in range(EXPERTS):
        outs[i][:, 0:width] = body[i * CAP : (i + 1) * CAP, :].astype(BF16)
        outs[i][:, width : width + LANES] = codes[0:CAP, :].astype(BF16)
        outs[i][:, width + LANES :] = jnp.zeros((CAP, (BLOCKS - 1) * LANES), BF16)
        for n, piece in enumerate((first, second, third)):
            at = width + (n + 1) * LANES
            outs[i][:, at : at + rows] = jnp.broadcast_to(piece, (CAP, rows)).astype(BF16)


def hidden_of(gate, upward):
    return (gate / (1.0 + jnp.exp(-gate)) * upward).astype(BF16)


def down(hidden, w_down, first, out):
    step = min(512, out.shape[1])
    for n in range(0, out.shape[1], step):
        at = first + n if isinstance(first, int) else pl.multiple_of(first + n, step)
        out[:, n : n + step] = jnp.dot(
            hidden, w_down[0, :, pl.ds(at, step)], preferred_element_type=F32
        ).astype(out.dtype)


def active(tick):
    return pl.when(lax.axis_index("section") == tick)


def deal_rows(source, blocks, own):
    slots = blocks[0].shape[0]
    for m in range(len(blocks)):
        at = pl.multiple_of((own ^ m) * slots, slots)
        blocks[m][...] = source[pl.ds(at, slots), :].astype(BF16)


def join_kernel(group, width, *refs):
    count = group * EXPERTS
    whole, half, table = refs[count : count + 3]
    block, rows = refs[count + 3 :]
    _, own = place(group)
    slots = EXPERTS * CAP
    for m in range(group):
        for i in range(EXPERTS):
            block[i * CAP : (i + 1) * CAP, :] = refs[m * EXPERTS + i][...].astype(F32)
        at = pl.multiple_of((own ^ m) * slots, slots)
        rows[pl.ds(at, slots), :] = block[...]
    table[...] = rows[:, width:].astype(BF16)
    at = pl.multiple_of(own * half.shape[1], half.shape[1])
    half[...] = rows[:, pl.ds(at, half.shape[1])].astype(BF16)
    whole[...] = rows[:, 0:width].astype(BF16)


def whole_kernel(group, tick, rows, gain, w_gate, w_up, w_down, *outs):
    _, own = place(group)

    @active(tick)
    def _():
        values = rows[...].astype(F32)
        inverse = lax.rsqrt(jnp.mean(values * values, axis=-1, keepdims=True) + 1e-06)
        normed = (values * inverse * gain[...]).astype(BF16)
        gate = jnp.dot(normed, w_gate[0], preferred_element_type=F32)
        upward = jnp.dot(normed, w_up[0], preferred_element_type=F32)
        hidden = hidden_of(gate, upward)
        outs[0][...] = hidden
        width = outs[1].shape[1]
        for m in range(1, group):
            down(hidden, w_down, pl.multiple_of((own ^ m) * width, width), outs[m])


def products(half, at, gain, w_gate, w_up):
    width = half.shape[1]
    values = half[...].astype(F32)
    scaled = (values * gain[:, pl.ds(at, width)]).astype(BF16)
    gate = jnp.dot(scaled, w_gate[0, pl.ds(at, width), :], preferred_element_type=F32)
    upward = jnp.dot(scaled, w_up[0, pl.ds(at, width), :], preferred_element_type=F32)
    return gate, upward, jnp.sum(values * values, axis=-1, keepdims=True)


def half_kernel(group, tick, half, gain, w_gate, w_up, gate_out, up_out, square_out):
    _, own = place(group)

    @active(tick)
    def _():
        width = half.shape[1]
        at = pl.multiple_of(own * width, width)
        gate, upward, square = products(half, at, gain, w_gate, w_up)
        gate_out[...] = gate
        up_out[...] = upward
        square_out[...] = jnp.broadcast_to(square, square_out.shape)


def rest_kernel(group, tick, last, *refs):
    halves = refs[:group]
    gate_in, up_in, square_in, gain, w_gate, w_up, w_down = refs[group : group + 7]
    outs = refs[group + 7 :]
    _, own = place(group)

    @active(tick)
    def _():
        gate, upward, square = gate_in[...], up_in[...], square_in[:, 0:1]
        width = halves[0].shape[1]
        for m in range(1, group):
            at = pl.multiple_of((own ^ m) * width, width)
            more = products(halves[m], at, gain, w_gate, w_up)
            gate, upward, square = gate + more[0], upward + more[1], square + more[2]
        inverse = lax.rsqrt(square / gain.shape[1] + 1e-06)
        hidden = hidden_of(gate * inverse, upward * inverse)
        if last:
            rows, parts = outs[-2:]
            for m in range(group):
                at = pl.multiple_of((own ^ m) * width, width)
                rows[:, pl.ds(at, width)] = halves[m][...].astype(F32)
            down(hidden, w_down, 0, parts)
            deal_rows(parts, outs[:group], own)
            deal_rows(rows, outs[group : group + 1], own)
        else:
            outs[0][...] = hidden
            for m in range(1, group):
                down(hidden, w_down, pl.multiple_of((own ^ m) * width, width), outs[m])


def own_kernel(group, tick, hidden, w_down, out):
    _, own = place(group)

    @active(tick)
    def _():
        down(hidden[...], w_down, pl.multiple_of(own * out.shape[1], out.shape[1]), out)


def slot_codes(expert, dims):
    return expert * CAP + lax.rem(iota(dims, 0), CAP)


def scales(expert, table):
    rows = table.shape[0]
    position = table[:, 0:LANES].astype(F32)
    mine = position == slot_codes(expert, (rows, LANES)).astype(F32)
    scale = sum(table[:, n * LANES : (n + 1) * LANES].astype(F32) for n in range(1, BLOCKS))
    return jnp.sum(jnp.where(mine, scale, 0.0), axis=1, keepdims=True)


def updated(pieces, before, scale):
    total = pieces[0][...].astype(F32)
    for piece in pieces[1:]:
        total = total + piece[...].astype(F32)
    return before[...].astype(F32) + scale * total


def update_kernel(group, *refs):
    half, table, out, marked = refs[group : group + 4]
    expert, _ = place(group)
    width = out.shape[1]
    result = updated(refs[:group], half, scales(expert, table)).astype(BF16)
    out[...] = result
    marked[:, 0:width] = result
    marked[:, width:] = table[:, 0:LANES]


def keep_kernel(group, saved, *refs):
    outs, buffer = refs[saved : saved + group], refs[-1]
    section = lax.axis_index("section")
    _, own = place(group)
    for n in range(saved):

        @pl.when(section == n)
        def _(n=n):
            buffer[...] = refs[n][...].astype(F32)

    deal_rows(buffer, outs, own)


def leave_kernel(group, *refs):
    before, table = refs[group : group + 2]
    kept = refs[group + 2 : 2 * group + 2]
    outs = refs[2 * group + 2 : 2 * group + 2 + EXPERTS]
    column, rows = refs[-2:]
    slots = EXPERTS * CAP
    final = lax.axis_size("section") - 1
    section = lax.axis_index("section")
    expert, own = place(group)

    @pl.when(section == final)
    def _():
        column[...] = jnp.broadcast_to(scales(expert, table), column.shape)
        at = pl.multiple_of(own * slots, slots)
        scale = column[pl.ds(at, slots), :][:, 0:1]
        rows[...] = updated(refs[:group], before, scale)

    @pl.when(section != final)
    def _():
        width = kept[0].shape[1]
        for m in range(group):
            at = pl.multiple_of((own ^ m) * width, width)
            rows[:, pl.ds(at, width)] = kept[m][...].astype(F32)

    for i in range(EXPERTS):
        outs[i][...] = rows[i * CAP : (i + 1) * CAP, :].astype(BF16)


def choice_kernel(group, current, before, out):
    expert, _ = place(group)
    rows = current.shape[0]
    span = EXPERTS * CAP
    here = current[:, 0:LANES].astype(F32)
    there = before[:, before.shape[1] - LANES :].astype(F32)
    mine = jnp.where(here == slot_codes(expert, here.shape).astype(F32), 1.0, 0.0).astype(BF16)
    a, b = iota((rows, rows), 0), iota((rows, rows), 1)
    for i in range(EXPERTS):
        codes = slot_codes(expert ^ i, there.shape).astype(F32)
        theirs = jnp.where(there == codes, 1.0, 0.0).astype(BF16)
        both = lax.dot_general(
            mine, theirs, (((1,), (1,)), ((), ())), preferred_element_type=F32
        )
        both = jnp.where(a // CAP == b // CAP, both, 0.0).astype(BF16)
        moved = (a // span) * span + (((lax.rem(a, span) // CAP) ^ i) * CAP) + lax.rem(a, CAP)
        order = jnp.where(moved == b, 1.0, 0.0).astype(BF16)
        out[i] = jnp.dot(both, order, preferred_element_type=F32).astype(BF16)


def pick_kernel(*refs):
    choice, out = refs[EXPERTS], refs[-1]
    width = out.shape[1]
    total = jnp.dot(choice[0], refs[0][:, 0:width], preferred_element_type=F32)
    for i in range(1, EXPERTS):
        total = total + jnp.dot(choice[i], refs[i][...], preferred_element_type=F32)
    out[...] = total.astype(BF16)


def home_kernel(group, *refs):
    table, out, block = refs[EXPERTS:]
    expert, _ = place(group)
    slots = EXPERTS * CAP
    count = out.shape[1]
    for i in range(EXPERTS):
        block[i * CAP : (i + 1) * CAP, :] = refs[i][...].astype(F32)
    lanes = -(-count // 16) * 16
    position = jnp.broadcast_to(table[0:1, 0:lanes].astype(F32), (slots, lanes))
    index = iota((slots, lanes), 0)
    wanted = (expert ^ (index // CAP)) * CAP + lax.rem(index, CAP)
    chosen = jnp.where(position == wanted.astype(F32), 1.0, 0.0).astype(BF16)
    full = lax.dot_general(
        chosen, block[...].astype(BF16), (((0,), (0,)), ((), ())), preferred_element_type=F32
    )
    out[0] = full[0:count, :].astype(BF16)


def local(tokens, expert_ids, gate_scale, norm_gain, w_gate, w_up, w_down):
    peers = lax.axis_size("expert")
    sections = lax.axis_size("section")
    count, width = tokens.shape
    group = peers // EXPERTS
    chunk = width // group
    rows = peers * CAP
    slots = EXPERTS * CAP
    wide = width + BLOCKS * LANES
    weights = (norm_gain, w_gate, w_up, w_down)

    def across(value, i):
        pairs = [(d, (d // group ^ i) * group + d % group) for d in range(peers)]
        if i == 0:
            return value
        return lax.ppermute(value, "expert", pairs)

    def within(value, m):
        return lax.ppermute(value, "expert", [(d, d ^ m) for d in range(peers)])

    def onward(value, hops, i):
        pairs = [
            (s * peers + d, hops[s] * peers + (d // group ^ i) * group + d % group)
            for s in range(sections)
            for d in range(peers)
        ]
        return lax.ppermute(value, ("section", "expert"), pairs)

    def gather(value, marked, tick):
        outs = []
        for i in range(EXPERTS):
            hops = list(range(sections))
            third = [tick + 2 if tick + 2 < sections else 0] if i == EXPERTS - 1 else []
            ring = [tick, tick + 1] + third
            for n, s in enumerate(ring):
                hops[s] = ring[(n + 1) % len(ring)]
            outs.append(onward(value if i else marked, hops, i))
        return outs

    position = call(
        rank_kernel, shape((slots, LANES), F32), (expert_ids.reshape(1, count),), flops=START_FLOPS
    )
    sent = call(
        functools.partial(slot_kernel, group),
        [shape((CAP, wide))] * EXPERTS,
        (position, tokens, gate_scale),
    )
    arrived = [across(sent[i], i) for i in range(EXPERTS)]
    pieces = list(arrived)
    for m in range(1, group):
        pieces += [within(piece, m) for piece in arrived]
    flops = 6 * rows * width * w_gate.shape[2]
    whole, half, table = call(
        functools.partial(join_kernel, group, width),
        [shape((rows, width)), shape((rows, chunk)), shape((rows, BLOCKS * LANES))],
        tuple(pieces),
        scratch=[pltpu.VMEM((slots, wide), F32), pltpu.VMEM((rows, wide), F32)],
    )
    saved = []
    inner = w_gate.shape[2]
    for tick in range(sections):
        last = tick == sections - 1
        if tick:
            gathered = gather(saved[-1], marked, tick - 1)
            choice = call(
                functools.partial(choice_kernel, group),
                shape((EXPERTS, rows, rows)),
                (table, gathered[0]),
            )
            kept = []
            if last:
                kept = call(
                    functools.partial(keep_kernel, group, len(saved)),
                    [shape((slots, chunk))] * group,
                    tuple(saved),
                    scratch=[pltpu.VMEM((rows, chunk), F32)],
                )
                kept = [kept[0]] + [within(kept[m], m) for m in range(1, group)]
            half = call(pick_kernel, shape((rows, chunk)), (*gathered, choice, *kept))
            halves = [half] + [within(half, m) for m in range(1, group)]
            begun = call(
                functools.partial(half_kernel, group, tick),
                [shape((rows, inner), F32)] * 2 + [shape((rows, LANES), F32)],
                (half, *weights[:3]),
                flops=flops // (3 * group) * 2,
            )
            outs = [shape((rows, inner))] + [shape((rows, chunk))] * (group - 1)
            scratch = []
            if last:
                outs = [shape((slots, width))] * (group + 1)
                scratch = [pltpu.VMEM((rows, width), F32)] * 2
            outs = call(
                functools.partial(rest_kernel, group, tick, last),
                outs,
                (*halves, *begun, *weights),
                scratch=scratch,
                flops=flops // 2,
            )
        else:
            outs = call(
                functools.partial(whole_kernel, group, tick),
                [shape((rows, inner))] + [shape((rows, chunk))] * (group - 1),
                (whole, *weights),
                flops=flops * 5 // 6,
            )
        terms = [within(outs[m], m) for m in range(1, group)]
        if last:
            terms = [outs[0]] + terms
        else:
            own = call(
                functools.partial(own_kernel, group, tick),
                shape((rows, chunk)),
                (outs[0], w_down),
                flops=flops // 6,
            )
            terms = [own] + terms
        if not last:
            latest, marked = call(
                functools.partial(update_kernel, group),
                [shape((rows, chunk)), shape((rows, chunk + LANES))],
                (*terms, half, table),
            )
            saved.append(latest)
    leaving = call(
        functools.partial(leave_kernel, group),
        [shape((CAP, width))] * EXPERTS,
        (*terms, outs[group], table, *kept),
        scratch=[pltpu.VMEM((rows, LANES), F32), pltpu.VMEM((slots, width), F32)],
    )
    back = [across(leaving[i], i) for i in range(EXPERTS)]
    return call(
        functools.partial(home_kernel, group),
        shape((1, count, width)),
        (*back, sent[0][:, width : width + LANES]),
        scratch=[pltpu.VMEM((slots, width), F32)],
    )


def solution(mesh):
    return jax.shard_map(
        local,
        mesh=mesh,
        in_specs=(
            P("expert", None),
            P("section", "expert", None),
            P("section", "expert"),
            P("section", None),
            P("section", None, "expert"),
            P("section", None, "expert"),
            P("section", "expert", None),
        ),
        out_specs=P("section", "expert", None),
        check_vma=False,
    )
```

```python
import functools

import jax
import jax.numpy as jnp
from jax import lax
from jax.experimental import pallas as pl
from jax.experimental.pallas import tpu as pltpu
from jax.sharding import PartitionSpec as P


EXPERTS = 4
CAP = 2
LANES = 128
BLOCKS = 4
START_FLOPS = 10_000_000_000
F32 = jnp.float32
BF16 = jnp.bfloat16
VMEM = pl.BlockSpec(memory_space=pltpu.VMEM)


def call(kernel, outs, args, limit=4 << 20, scratch=(), flops=1000, specs=None, moved=None):
    if moved is None:
        moved = sum(a.size * a.dtype.itemsize for a in args)
    return pl.pallas_call(
        kernel,
        out_shape=outs,
        in_specs=specs or [VMEM] * len(args),
        out_specs=jax.tree.map(lambda _: VMEM, outs),
        scratch_shapes=scratch,
        compiler_params=pltpu.CompilerParams(vmem_limit_bytes=limit),
        cost_estimate=pl.CostEstimate(flops=flops, bytes_accessed=moved, transcendentals=0),
    )(*args)


def shape(dims, kind=BF16):
    return jax.ShapeDtypeStruct(dims, kind)


def place(group):
    index = lax.axis_index("expert")
    return index // group, lax.rem(index, group)


def iota(dims, axis):
    return lax.broadcasted_iota(jnp.int32, dims, axis)


def rank_kernel(ids, out):
    rows = ids.shape[1]
    ids_row = ids[...]
    ids_full = jnp.broadcast_to(ids_row, (rows, rows))
    diagonal = iota((rows, rows), 0) == iota((rows, rows), 1)
    ids_column = jnp.sum(jnp.where(diagonal, ids_full, 0), axis=1, keepdims=True)
    earlier = iota((rows, rows), 0) < iota((rows, rows), 1)
    rank = jnp.sum(jnp.where((ids_full == ids_column) & earlier, 1, 0), axis=0, keepdims=True)
    out[...] = jnp.full(out.shape, -1.0, F32)
    out[:, 0:rows] = jnp.broadcast_to((ids_row * CAP + rank).astype(F32), (out.shape[0], rows))


def slot_kernel(group, position, tokens, scale, *outs):
    expert, _ = place(group)
    rows = tokens.shape[0]
    width = tokens.shape[1]
    codes = position[...]
    index = iota(codes.shape, 0)
    wanted = (expert ^ (index // CAP)) * CAP + lax.rem(index, CAP)
    chosen = jnp.where(codes == wanted.astype(F32), 1.0, 0.0)[:, 0:rows].astype(BF16)
    body = jnp.dot(chosen, tokens[...], preferred_element_type=F32)
    value = scale[...]
    first = value.astype(BF16).astype(F32)
    second = (value - first).astype(BF16).astype(F32)
    third = value - first - second
    for i in range(EXPERTS):
        outs[i][:, 0:width] = body[i * CAP : (i + 1) * CAP, :].astype(BF16)
        outs[i][:, width : width + LANES] = codes[0:CAP, :].astype(BF16)
        outs[i][:, width + LANES :] = jnp.zeros((CAP, (BLOCKS - 1) * LANES), BF16)
        for n, piece in enumerate((first, second, third)):
            at = width + (n + 1) * LANES
            outs[i][:, at : at + rows] = jnp.broadcast_to(piece, (CAP, rows)).astype(BF16)


def hidden_of(gate, upward):
    return (gate / (1.0 + jnp.exp(-gate)) * upward).astype(BF16)


def down(hidden, w_down, first, out):
    step = min(512, out.shape[1])
    for n in range(0, out.shape[1], step):
        at = first + n if isinstance(first, int) else pl.multiple_of(first + n, step)
        out[:, n : n + step] = jnp.dot(
            hidden, w_down[0, :, pl.ds(at, step)], preferred_element_type=F32
        ).astype(out.dtype)


def active(tick):
    return pl.when(lax.axis_index("section") == tick)


def deal_rows(source, blocks, own):
    slots = blocks[0].shape[0]
    for m in range(len(blocks)):
        at = pl.multiple_of((own ^ m) * slots, slots)
        blocks[m][...] = source[pl.ds(at, slots), :].astype(BF16)


def join_kernel(group, width, *refs):
    count = group * EXPERTS
    whole, half, table = refs[count : count + 3]
    block, rows = refs[count + 3 :]
    _, own = place(group)
    slots = EXPERTS * CAP
    for m in range(group):
        for i in range(EXPERTS):
            block[i * CAP : (i + 1) * CAP, :] = refs[m * EXPERTS + i][...].astype(F32)
        at = pl.multiple_of((own ^ m) * slots, slots)
        rows[pl.ds(at, slots), :] = block[...]
    table[...] = rows[:, width:].astype(BF16)
    at = pl.multiple_of(own * half.shape[1], half.shape[1])
    half[...] = rows[:, pl.ds(at, half.shape[1])].astype(BF16)
    whole[...] = rows[:, 0:width].astype(BF16)


def whole_kernel(group, tick, rows, gain, w_gate, w_up, w_down, *outs):
    _, own = place(group)

    @active(tick)
    def _():
        values = rows[...].astype(F32)
        inverse = lax.rsqrt(jnp.mean(values * values, axis=-1, keepdims=True) + 1e-06)
        normed = (values * inverse * gain[...]).astype(BF16)
        gate = jnp.dot(normed, w_gate[0], preferred_element_type=F32)
        upward = jnp.dot(normed, w_up[0], preferred_element_type=F32)
        hidden = hidden_of(gate, upward)
        outs[0][...] = hidden
        width = outs[1].shape[1]
        for m in range(1, group):
            down(hidden, w_down, pl.multiple_of((own ^ m) * width, width), outs[m])


def products(half, at, gain, w_gate, w_up):
    width = half.shape[1]
    values = half[...].astype(F32)
    scaled = (values * gain[:, pl.ds(at, width)]).astype(BF16)
    gate = jnp.dot(scaled, w_gate[0, pl.ds(at, width), :], preferred_element_type=F32)
    upward = jnp.dot(scaled, w_up[0, pl.ds(at, width), :], preferred_element_type=F32)
    return gate, upward, jnp.sum(values * values, axis=-1, keepdims=True)


def half_kernel(group, tick, half, gain, w_gate, w_up, gate_out, up_out, square_out):
    _, own = place(group)

    @active(tick)
    def _():
        width = half.shape[1]
        at = pl.multiple_of(own * width, width)
        gate, upward, square = products(half, at, gain, w_gate, w_up)
        gate_out[...] = gate
        up_out[...] = upward
        square_out[...] = jnp.broadcast_to(square, square_out.shape)


def rest_kernel(group, tick, last, *refs):
    halves = refs[:group]
    gate_in, up_in, square_in, gain, w_gate, w_up, w_down = refs[group : group + 7]
    outs = refs[group + 7 :]
    _, own = place(group)

    @active(tick)
    def _():
        gate, upward, square = gate_in[...], up_in[...], square_in[:, 0:1]
        width = halves[0].shape[1]
        for m in range(1, group):
            at = pl.multiple_of((own ^ m) * width, width)
            more = products(halves[m], at, gain, w_gate, w_up)
            gate, upward, square = gate + more[0], upward + more[1], square + more[2]
        inverse = lax.rsqrt(square / gain.shape[1] + 1e-06)
        hidden = hidden_of(gate * inverse, upward * inverse)
        if last:
            rows, parts = outs[-2:]
            for m in range(group):
                at = pl.multiple_of((own ^ m) * width, width)
                rows[:, pl.ds(at, width)] = halves[m][...].astype(F32)
            down(hidden, w_down, 0, parts)
            deal_rows(parts, outs[:group], own)
            deal_rows(rows, outs[group : group + 1], own)
        else:
            outs[0][...] = hidden
            for m in range(1, group):
                down(hidden, w_down, pl.multiple_of((own ^ m) * width, width), outs[m])


def own_kernel(group, tick, hidden, w_down, out):
    _, own = place(group)

    @active(tick)
    def _():
        down(hidden[...], w_down, pl.multiple_of(own * out.shape[1], out.shape[1]), out)


def slot_codes(expert, dims):
    return expert * CAP + lax.rem(iota(dims, 0), CAP)


def scales(expert, table):
    rows = table.shape[0]
    position = table[:, 0:LANES].astype(F32)
    mine = position == slot_codes(expert, (rows, LANES)).astype(F32)
    scale = sum(table[:, n * LANES : (n + 1) * LANES].astype(F32) for n in range(1, BLOCKS))
    return jnp.sum(jnp.where(mine, scale, 0.0), axis=1, keepdims=True)


def updated(pieces, before, scale):
    total = pieces[0][...].astype(F32)
    for piece in pieces[1:]:
        total = total + piece[...].astype(F32)
    return before[...].astype(F32) + scale * total


def update_kernel(group, *refs):
    half, table, out, marked = refs[group : group + 4]
    expert, _ = place(group)
    width = out.shape[1]
    result = updated(refs[:group], half, scales(expert, table)).astype(BF16)
    out[...] = result
    marked[:, 0:width] = result
    marked[:, width:] = table[:, 0:LANES]


def keep_kernel(group, saved, *refs):
    outs, buffer = refs[saved : saved + group], refs[-1]
    section = lax.axis_index("section")
    _, own = place(group)
    for n in range(saved):

        @pl.when(section == n)
        def _(n=n):
            buffer[...] = refs[n][...].astype(F32)

    deal_rows(buffer, outs, own)


def leave_kernel(group, *refs):
    before, table = refs[group : group + 2]
    kept = refs[group + 2 : 2 * group + 2]
    outs = refs[2 * group + 2 : 2 * group + 2 + EXPERTS]
    column, rows = refs[-2:]
    slots = EXPERTS * CAP
    final = lax.axis_size("section") - 1
    section = lax.axis_index("section")
    expert, own = place(group)

    @pl.when(section == final)
    def _():
        column[...] = jnp.broadcast_to(scales(expert, table), column.shape)
        at = pl.multiple_of(own * slots, slots)
        scale = column[pl.ds(at, slots), :][:, 0:1]
        rows[...] = updated(refs[:group], before, scale)

    @pl.when(section != final)
    def _():
        width = kept[0].shape[1]
        for m in range(group):
            at = pl.multiple_of((own ^ m) * width, width)
            rows[:, pl.ds(at, width)] = kept[m][...].astype(F32)

    for i in range(EXPERTS):
        outs[i][...] = rows[i * CAP : (i + 1) * CAP, :].astype(BF16)


def choice_kernel(group, current, before, out):
    expert, _ = place(group)
    rows = current.shape[0]
    span = EXPERTS * CAP
    here = current[:, 0:LANES].astype(F32)
    there = before[:, before.shape[1] - LANES :].astype(F32)
    mine = jnp.where(here == slot_codes(expert, here.shape).astype(F32), 1.0, 0.0).astype(BF16)
    a, b = iota((rows, rows), 0), iota((rows, rows), 1)
    for i in range(EXPERTS):
        codes = slot_codes(expert ^ i, there.shape).astype(F32)
        theirs = jnp.where(there == codes, 1.0, 0.0).astype(BF16)
        both = lax.dot_general(
            mine, theirs, (((1,), (1,)), ((), ())), preferred_element_type=F32
        )
        both = jnp.where(a // CAP == b // CAP, both, 0.0).astype(BF16)
        moved = (a // span) * span + (((lax.rem(a, span) // CAP) ^ i) * CAP) + lax.rem(a, CAP)
        order = jnp.where(moved == b, 1.0, 0.0).astype(BF16)
        out[i] = jnp.dot(both, order, preferred_element_type=F32).astype(BF16)


def pick_kernel(*refs):
    choice, out = refs[EXPERTS], refs[-1]
    width = out.shape[1]
    total = jnp.dot(choice[0], refs[0][:, 0:width], preferred_element_type=F32)
    for i in range(1, EXPERTS):
        total = total + jnp.dot(choice[i], refs[i][...], preferred_element_type=F32)
    out[...] = total.astype(BF16)


def home_kernel(group, *refs):
    table, out, block = refs[EXPERTS:]
    expert, _ = place(group)
    slots = EXPERTS * CAP
    count = out.shape[1]
    for i in range(EXPERTS):
        block[i * CAP : (i + 1) * CAP, :] = refs[i][...].astype(F32)
    lanes = -(-count // 16) * 16
    position = jnp.broadcast_to(table[0:1, 0:lanes].astype(F32), (slots, lanes))
    index = iota((slots, lanes), 0)
    wanted = (expert ^ (index // CAP)) * CAP + lax.rem(index, CAP)
    chosen = jnp.where(position == wanted.astype(F32), 1.0, 0.0).astype(BF16)
    full = lax.dot_general(
        chosen, block[...].astype(BF16), (((0,), (0,)), ((), ())), preferred_element_type=F32
    )
    out[0] = full[0:count, :].astype(BF16)


def local(tokens, expert_ids, gate_scale, norm_gain, w_gate, w_up, w_down):
    peers = lax.axis_size("expert")
    sections = lax.axis_size("section")
    count, width = tokens.shape
    group = peers // EXPERTS
    chunk = width // group
    rows = peers * CAP
    slots = EXPERTS * CAP
    wide = width + BLOCKS * LANES
    weights = (norm_gain, w_gate, w_up, w_down)

    def across(value, i):
        pairs = [(d, (d // group ^ i) * group + d % group) for d in range(peers)]
        if i == 0:
            return value
        return lax.ppermute(value, "expert", pairs)

    def within(value, m):
        return lax.ppermute(value, "expert", [(d, d ^ m) for d in range(peers)])

    def gather(value, marked, tick):
        hops = list(range(sections))
        ring = [tick, tick + 1, tick + 2 if tick + 2 < sections else 0]
        for n, s in enumerate(ring):
            hops[s] = ring[(n + 1) % 3]
        pairs = [(s * peers + d, hops[s] * peers + d) for s in range(sections) for d in range(peers)]
        outs = []
        for i in range(EXPERTS):
            if i:
                pairs = [
                    (tick * peers + d, (tick + 1) * peers + (d // group ^ i) * group + d % group)
                    for d in range(peers)
                ]
            outs.append(lax.ppermute(value if i else marked, ("section", "expert"), pairs))
        return outs

    position = call(
        rank_kernel, shape((slots, LANES), F32), (expert_ids.reshape(1, count),), flops=START_FLOPS
    )
    sent = call(
        functools.partial(slot_kernel, group),
        [shape((CAP, wide))] * EXPERTS,
        (position, tokens, gate_scale),
    )
    arrived = [across(sent[i], i) for i in range(EXPERTS)]
    pieces = list(arrived)
    for m in range(1, group):
        pieces += [within(piece, m) for piece in arrived]
    flops = 6 * rows * width * w_gate.shape[2]
    whole, half, table = call(
        functools.partial(join_kernel, group, width),
        [shape((rows, width)), shape((rows, chunk)), shape((rows, BLOCKS * LANES))],
        tuple(pieces),
        scratch=[pltpu.VMEM((slots, wide), F32), pltpu.VMEM((rows, wide), F32)],
    )
    saved = []
    inner = w_gate.shape[2]
    for tick in range(sections):
        last = tick == sections - 1
        if tick:
            gathered = gather(saved[-1], marked, tick - 1)
            choice = call(
                functools.partial(choice_kernel, group),
                shape((EXPERTS, rows, rows)),
                (table, gathered[0]),
            )
            kept = []
            if last:
                kept = call(
                    functools.partial(keep_kernel, group, len(saved)),
                    [shape((slots, chunk))] * group,
                    tuple(saved),
                    scratch=[pltpu.VMEM((rows, chunk), F32)],
                )
                kept = [kept[0]] + [within(kept[m], m) for m in range(1, group)]
            half = call(pick_kernel, shape((rows, chunk)), (*gathered, choice, *kept))
            halves = [half] + [within(half, m) for m in range(1, group)]
            begun = call(
                functools.partial(half_kernel, group, tick),
                [shape((rows, inner), F32)] * 2 + [shape((rows, LANES), F32)],
                (half, *weights[:3]),
                flops=flops // (3 * group) * 2,
            )
            outs = [shape((rows, inner))] + [shape((rows, chunk))] * (group - 1)
            scratch = []
            if last:
                outs = [shape((slots, width))] * (group + 1)
                scratch = [pltpu.VMEM((rows, width), F32)] * 2
            outs = call(
                functools.partial(rest_kernel, group, tick, last),
                outs,
                (*halves, *begun, *weights),
                scratch=scratch,
                flops=flops // 2,
            )
        else:
            outs = call(
                functools.partial(whole_kernel, group, tick),
                [shape((rows, inner))] + [shape((rows, chunk))] * (group - 1),
                (whole, *weights),
                flops=flops * 5 // 6,
            )
        terms = [within(outs[m], m) for m in range(1, group)]
        if last:
            terms = [outs[0]] + terms
        else:
            own = call(
                functools.partial(own_kernel, group, tick),
                shape((rows, chunk)),
                (outs[0], w_down),
                flops=flops // 6,
            )
            terms = [own] + terms
        if not last:
            latest, marked = call(
                functools.partial(update_kernel, group),
                [shape((rows, chunk)), shape((rows, chunk + LANES))],
                (*terms, half, table),
            )
            saved.append(latest)
    leaving = call(
        functools.partial(leave_kernel, group),
        [shape((CAP, width))] * EXPERTS,
        (*terms, outs[group], table, *kept),
        scratch=[pltpu.VMEM((rows, LANES), F32), pltpu.VMEM((slots, width), F32)],
    )
    back = [across(leaving[i], i) for i in range(EXPERTS)]
    return call(
        functools.partial(home_kernel, group),
        shape((1, count, width)),
        (*back, sent[0][:, width : width + LANES]),
        scratch=[pltpu.VMEM((slots, width), F32)],
    )


def solution(mesh):
    return jax.shard_map(
        local,
        mesh=mesh,
        in_specs=(
            P("expert", None),
            P("section", "expert", None),
            P("section", "expert"),
            P("section", None),
            P("section", None, "expert"),
            P("section", None, "expert"),
            P("section", "expert", None),
        ),
        out_specs=P("section", "expert", None),
        check_vma=False,
    )
```

```python
import functools

import jax
import jax.numpy as jnp
from jax import lax
from jax.experimental import pallas as pl
from jax.experimental.pallas import tpu as pltpu
from jax.sharding import PartitionSpec as P


EXPERTS = 4
CAP = 2
LANES = 128
BLOCKS = 4
START_FLOPS = 10_000_000_000
F32 = jnp.float32
BF16 = jnp.bfloat16
VMEM = pl.BlockSpec(memory_space=pltpu.VMEM)


def call(kernel, outs, args, limit=4 << 20, scratch=(), flops=1000, specs=None, moved=None):
    if moved is None:
        moved = sum(a.size * a.dtype.itemsize for a in args)
    return pl.pallas_call(
        kernel,
        out_shape=outs,
        in_specs=specs or [VMEM] * len(args),
        out_specs=jax.tree.map(lambda _: VMEM, outs),
        scratch_shapes=scratch,
        compiler_params=pltpu.CompilerParams(vmem_limit_bytes=limit),
        cost_estimate=pl.CostEstimate(flops=flops, bytes_accessed=moved, transcendentals=0),
    )(*args)


def shape(dims, kind=BF16):
    return jax.ShapeDtypeStruct(dims, kind)


def place(group):
    index = lax.axis_index("expert")
    return index // group, lax.rem(index, group)


def iota(dims, axis):
    return lax.broadcasted_iota(jnp.int32, dims, axis)


def code_kernel(group, out):
    expert, _ = place(group)
    index = iota(out.shape, 0)
    out[...] = ((expert ^ (index // CAP)) * CAP + lax.rem(index, CAP)).astype(F32)


def slot_kernel(wanted, tokens, ids, scale, *outs):
    rows = tokens.shape[0]
    width = tokens.shape[1]
    ids_row = ids[...]
    ids_full = jnp.broadcast_to(ids_row, (rows, rows))
    diagonal = iota((rows, rows), 0) == iota((rows, rows), 1)
    ids_column = jnp.sum(jnp.where(diagonal, ids_full, 0), axis=1, keepdims=True)
    earlier = iota((rows, rows), 0) < iota((rows, rows), 1)
    rank = jnp.sum(jnp.where((ids_full == ids_column) & earlier, 1, 0), axis=0, keepdims=True)
    position = (ids_row * CAP + rank).astype(F32)
    chosen = jnp.where(position == wanted[:, 0:rows], 1.0, 0.0).astype(BF16)
    body = jnp.dot(chosen, tokens[...], preferred_element_type=F32)
    value = scale[...]
    first = value.astype(BF16).astype(F32)
    second = (value - first).astype(BF16).astype(F32)
    third = value - first - second
    for i in range(EXPERTS):
        outs[i][:, 0:width] = body[i * CAP : (i + 1) * CAP, :].astype(BF16)
        outs[i][:, width:] = jnp.full((CAP, BLOCKS * LANES), -1.0, BF16)
        for n, piece in enumerate((position, first, second, third)):
            at = width + n * LANES
            outs[i][:, at : at + rows] = jnp.broadcast_to(piece, (CAP, rows)).astype(BF16)


def hidden_of(gate, upward):
    return (gate / (1.0 + jnp.exp(-gate)) * upward).astype(BF16)


def down(hidden, w_down, first, out):
    step = min(512, out.shape[1])
    for n in range(0, out.shape[1], step):
        at = first + n if isinstance(first, int) else pl.multiple_of(first + n, step)
        out[:, n : n + step] = jnp.dot(
            hidden, w_down[0, :, pl.ds(at, step)], preferred_element_type=F32
        ).astype(out.dtype)


def active(tick):
    return pl.when(lax.axis_index("section") == tick)


def deal_rows(source, blocks, own):
    slots = blocks[0].shape[0]
    for m in range(len(blocks)):
        at = pl.multiple_of((own ^ m) * slots, slots)
        blocks[m][...] = source[pl.ds(at, slots), :].astype(BF16)


def join_kernel(group, width, *refs):
    count = group * EXPERTS
    whole, half, table = refs[count : count + 3]
    block, rows = refs[count + 3 :]
    _, own = place(group)
    slots = EXPERTS * CAP
    for m in range(group):
        for i in range(EXPERTS):
            block[i * CAP : (i + 1) * CAP, :] = refs[m * EXPERTS + i][...].astype(F32)
        at = pl.multiple_of((own ^ m) * slots, slots)
        rows[pl.ds(at, slots), :] = block[...]
    table[...] = rows[:, width:].astype(BF16)
    at = pl.multiple_of(own * half.shape[1], half.shape[1])
    half[...] = rows[:, pl.ds(at, half.shape[1])].astype(BF16)
    whole[...] = rows[:, 0:width].astype(BF16)


def whole_kernel(group, tick, rows, gain, w_gate, w_up, w_down, *outs):
    _, own = place(group)

    @active(tick)
    def _():
        values = rows[...].astype(F32)
        inverse = lax.rsqrt(jnp.mean(values * values, axis=-1, keepdims=True) + 1e-06)
        normed = (values * inverse * gain[...]).astype(BF16)
        gate = jnp.dot(normed, w_gate[0], preferred_element_type=F32)
        upward = jnp.dot(normed, w_up[0], preferred_element_type=F32)
        hidden = hidden_of(gate, upward)
        outs[0][...] = hidden
        width = outs[1].shape[1]
        for m in range(1, group):
            down(hidden, w_down, pl.multiple_of((own ^ m) * width, width), outs[m])


def products(half, at, gain, w_gate, w_up):
    width = half.shape[1]
    values = half[...].astype(F32)
    scaled = (values * gain[:, pl.ds(at, width)]).astype(BF16)
    gate = jnp.dot(scaled, w_gate[0, pl.ds(at, width), :], preferred_element_type=F32)
    upward = jnp.dot(scaled, w_up[0, pl.ds(at, width), :], preferred_element_type=F32)
    return gate, upward, jnp.sum(values * values, axis=-1, keepdims=True)


def half_kernel(group, tick, half, gain, w_gate, w_up, gate_out, up_out, square_out):
    _, own = place(group)

    @active(tick)
    def _():
        width = half.shape[1]
        at = pl.multiple_of(own * width, width)
        gate, upward, square = products(half, at, gain, w_gate, w_up)
        gate_out[...] = gate
        up_out[...] = upward
        square_out[...] = jnp.broadcast_to(square, square_out.shape)


def rest_kernel(group, tick, last, *refs):
    halves = refs[:group]
    gate_in, up_in, square_in, gain, w_gate, w_up, w_down = refs[group : group + 7]
    outs = refs[group + 7 :]
    _, own = place(group)

    @active(tick)
    def _():
        gate, upward, square = gate_in[...], up_in[...], square_in[:, 0:1]
        width = halves[0].shape[1]
        for m in range(1, group):
            at = pl.multiple_of((own ^ m) * width, width)
            more = products(halves[m], at, gain, w_gate, w_up)
            gate, upward, square = gate + more[0], upward + more[1], square + more[2]
        inverse = lax.rsqrt(square / gain.shape[1] + 1e-06)
        hidden = hidden_of(gate * inverse, upward * inverse)
        if last:
            rows, parts = outs[-2:]
            for m in range(group):
                at = pl.multiple_of((own ^ m) * width, width)
                rows[:, pl.ds(at, width)] = halves[m][...].astype(F32)
            down(hidden, w_down, 0, parts)
            deal_rows(parts, outs[:group], own)
            deal_rows(rows, outs[group : group + 1], own)
        else:
            outs[0][...] = hidden
            for m in range(1, group):
                down(hidden, w_down, pl.multiple_of((own ^ m) * width, width), outs[m])


def own_kernel(group, tick, hidden, w_down, out):
    _, own = place(group)

    @active(tick)
    def _():
        down(hidden[...], w_down, pl.multiple_of(own * out.shape[1], out.shape[1]), out)


def slot_codes(expert, dims):
    return expert * CAP + lax.rem(iota(dims, 0), CAP)


def scales(expert, table):
    rows = table.shape[0]
    position = table[:, 0:LANES].astype(F32)
    mine = position == slot_codes(expert, (rows, LANES)).astype(F32)
    scale = sum(table[:, n * LANES : (n + 1) * LANES].astype(F32) for n in range(1, BLOCKS))
    return jnp.sum(jnp.where(mine, scale, 0.0), axis=1, keepdims=True)


def updated(pieces, before, scale):
    total = pieces[0][...].astype(F32)
    for piece in pieces[1:]:
        total = total + piece[...].astype(F32)
    return before[...].astype(F32) + scale * total


def update_kernel(group, *refs):
    half, table, out, marked = refs[group : group + 4]
    expert, _ = place(group)
    width = out.shape[1]
    result = updated(refs[:group], half, scales(expert, table)).astype(BF16)
    out[...] = result
    marked[:, 0:width] = result
    marked[:, width:] = table[:, 0:LANES]


def keep_kernel(group, saved, *refs):
    outs, buffer = refs[saved : saved + group], refs[-1]
    section = lax.axis_index("section")
    _, own = place(group)
    for n in range(saved):

        @pl.when(section == n)
        def _(n=n):
            buffer[...] = refs[n][...].astype(F32)

    deal_rows(buffer, outs, own)


def leave_kernel(group, *refs):
    before, table = refs[group : group + 2]
    kept = refs[group + 2 : 2 * group + 2]
    outs = refs[2 * group + 2 : 2 * group + 2 + EXPERTS]
    column, rows = refs[-2:]
    slots = EXPERTS * CAP
    final = lax.axis_size("section") - 1
    section = lax.axis_index("section")
    expert, own = place(group)

    @pl.when(section == final)
    def _():
        column[...] = jnp.broadcast_to(scales(expert, table), column.shape)
        at = pl.multiple_of(own * slots, slots)
        scale = column[pl.ds(at, slots), :][:, 0:1]
        rows[...] = updated(refs[:group], before, scale)

    @pl.when(section != final)
    def _():
        width = kept[0].shape[1]
        for m in range(group):
            at = pl.multiple_of((own ^ m) * width, width)
            rows[:, pl.ds(at, width)] = kept[m][...].astype(F32)

    for i in range(EXPERTS):
        outs[i][...] = rows[i * CAP : (i + 1) * CAP, :].astype(BF16)


def choice_kernel(group, current, before, out):
    expert, _ = place(group)
    rows = current.shape[0]
    span = EXPERTS * CAP
    here = current[:, 0:LANES].astype(F32)
    there = before[:, before.shape[1] - LANES :].astype(F32)
    mine = jnp.where(here == slot_codes(expert, here.shape).astype(F32), 1.0, 0.0).astype(BF16)
    a, b = iota((rows, rows), 0), iota((rows, rows), 1)
    for i in range(EXPERTS):
        codes = slot_codes(expert ^ i, there.shape).astype(F32)
        theirs = jnp.where(there == codes, 1.0, 0.0).astype(BF16)
        both = lax.dot_general(
            mine, theirs, (((1,), (1,)), ((), ())), preferred_element_type=F32
        )
        both = jnp.where(a // CAP == b // CAP, both, 0.0).astype(BF16)
        moved = (a // span) * span + (((lax.rem(a, span) // CAP) ^ i) * CAP) + lax.rem(a, CAP)
        order = jnp.where(moved == b, 1.0, 0.0).astype(BF16)
        out[i] = jnp.dot(both, order, preferred_element_type=F32).astype(BF16)


def pick_kernel(*refs):
    choice, out = refs[EXPERTS], refs[-1]
    width = out.shape[1]
    total = jnp.dot(choice[0], refs[0][:, 0:width], preferred_element_type=F32)
    for i in range(1, EXPERTS):
        total = total + jnp.dot(choice[i], refs[i][...], preferred_element_type=F32)
    out[...] = total.astype(BF16)


def home_kernel(group, *refs):
    table, out, block = refs[EXPERTS:]
    expert, _ = place(group)
    slots = EXPERTS * CAP
    count = out.shape[1]
    for i in range(EXPERTS):
        block[i * CAP : (i + 1) * CAP, :] = refs[i][...].astype(F32)
    lanes = -(-count // 16) * 16
    position = jnp.broadcast_to(table[0:1, 0:lanes].astype(F32), (slots, lanes))
    index = iota((slots, lanes), 0)
    wanted = (expert ^ (index // CAP)) * CAP + lax.rem(index, CAP)
    chosen = jnp.where(position == wanted.astype(F32), 1.0, 0.0).astype(BF16)
    full = lax.dot_general(
        chosen, block[...].astype(BF16), (((0,), (0,)), ((), ())), preferred_element_type=F32
    )
    out[0] = full[0:count, :].astype(BF16)


def local(tokens, expert_ids, gate_scale, norm_gain, w_gate, w_up, w_down):
    peers = lax.axis_size("expert")
    sections = lax.axis_size("section")
    count, width = tokens.shape
    group = peers // EXPERTS
    chunk = width // group
    rows = peers * CAP
    slots = EXPERTS * CAP
    wide = width + BLOCKS * LANES
    weights = (norm_gain, w_gate, w_up, w_down)

    def across(value, i):
        pairs = [(d, (d // group ^ i) * group + d % group) for d in range(peers)]
        if i == 0:
            return value
        return lax.ppermute(value, "expert", pairs)

    def within(value, m):
        return lax.ppermute(value, "expert", [(d, d ^ m) for d in range(peers)])

    def gather(value, marked, tick):
        outs = []
        for i in range(EXPERTS):
            ring = [tick, tick + 1]
            if i == EXPERTS - 1 and sections > 2:
                ring.append(tick - 1 if tick else 2)
            pairs = []
            for s in range(sections):
                to, move = s, lambda d: d ^ 1
                if s in ring:
                    to = ring[(ring.index(s) + 1) % len(ring)]
                    move = lambda d: d
                if s == tick:
                    move = lambda d: (d // group ^ i) * group + d % group
                pairs += [(s * peers + d, to * peers + move(d)) for d in range(peers)]
            outs.append(lax.ppermute(value if i else marked, ("section", "expert"), pairs))
        return outs

    wanted = call(
        functools.partial(code_kernel, group), shape((slots, LANES), F32), (), flops=START_FLOPS
    )
    sent = call(
        slot_kernel,
        [shape((CAP, wide))] * EXPERTS,
        (wanted, tokens, expert_ids.reshape(1, count), gate_scale),
    )
    arrived = [across(sent[i], i) for i in range(EXPERTS)]
    pieces = list(arrived)
    for m in range(1, group):
        pieces += [within(piece, m) for piece in arrived]
    flops = 6 * rows * width * w_gate.shape[2]
    whole, half, table = call(
        functools.partial(join_kernel, group, width),
        [shape((rows, width)), shape((rows, chunk)), shape((rows, BLOCKS * LANES))],
        tuple(pieces),
        scratch=[pltpu.VMEM((slots, wide), F32), pltpu.VMEM((rows, wide), F32)],
    )
    saved = []
    inner = w_gate.shape[2]
    for tick in range(sections):
        last = tick == sections - 1
        if tick:
            gathered = gather(saved[-1], marked, tick - 1)
            choice = call(
                functools.partial(choice_kernel, group),
                shape((EXPERTS, rows, rows)),
                (table, gathered[0]),
            )
            kept = []
            if last:
                kept = call(
                    functools.partial(keep_kernel, group, len(saved)),
                    [shape((slots, chunk))] * group,
                    tuple(saved),
                    scratch=[pltpu.VMEM((rows, chunk), F32)],
                )
                kept = [kept[0]] + [within(kept[m], m) for m in range(1, group)]
            half = call(pick_kernel, shape((rows, chunk)), (*gathered, choice, *kept))
            halves = [half] + [within(half, m) for m in range(1, group)]
            begun = call(
                functools.partial(half_kernel, group, tick),
                [shape((rows, inner), F32)] * 2 + [shape((rows, LANES), F32)],
                (half, *weights[:3]),
                flops=flops // (3 * group) * 2,
            )
            outs = [shape((rows, inner))] + [shape((rows, chunk))] * (group - 1)
            scratch = []
            if last:
                outs = [shape((slots, width))] * (group + 1)
                scratch = [pltpu.VMEM((rows, width), F32)] * 2
            outs = call(
                functools.partial(rest_kernel, group, tick, last),
                outs,
                (*halves, *begun, *weights),
                scratch=scratch,
                flops=flops // 2,
            )
        else:
            outs = call(
                functools.partial(whole_kernel, group, tick),
                [shape((rows, inner))] + [shape((rows, chunk))] * (group - 1),
                (whole, *weights),
                flops=flops * 5 // 6,
            )
        terms = [within(outs[m], m) for m in range(1, group)]
        if last:
            terms = [outs[0]] + terms
        else:
            own = call(
                functools.partial(own_kernel, group, tick),
                shape((rows, chunk)),
                (outs[0], w_down),
                flops=flops // 6,
            )
            terms = [own] + terms
        if not last:
            latest, marked = call(
                functools.partial(update_kernel, group),
                [shape((rows, chunk)), shape((rows, chunk + LANES))],
                (*terms, half, table),
            )
            saved.append(latest)
    leaving = call(
        functools.partial(leave_kernel, group),
        [shape((CAP, width))] * EXPERTS,
        (*terms, outs[group], table, *kept),
        scratch=[pltpu.VMEM((rows, LANES), F32), pltpu.VMEM((slots, width), F32)],
    )
    back = [across(leaving[i], i) for i in range(EXPERTS)]
    return call(
        functools.partial(home_kernel, group),
        shape((1, count, width)),
        (*back, sent[0][:, width : width + LANES]),
        scratch=[pltpu.VMEM((slots, width), F32)],
    )


def solution(mesh):
    return jax.shard_map(
        local,
        mesh=mesh,
        in_specs=(
            P("expert", None),
            P("section", "expert", None),
            P("section", "expert"),
            P("section", None),
            P("section", None, "expert"),
            P("section", None, "expert"),
            P("section", "expert", None),
        ),
        out_specs=P("section", "expert", None),
        check_vma=False,
    )
```

```python
import functools

import jax
import jax.numpy as jnp
from jax import lax
from jax.experimental import pallas as pl
from jax.experimental.pallas import tpu as pltpu
from jax.sharding import PartitionSpec as P


EXPERTS = 4
CAP = 2
LANES = 128
BLOCKS = 4
START_FLOPS = 10_000_000_000
F32 = jnp.float32
BF16 = jnp.bfloat16
VMEM = pl.BlockSpec(memory_space=pltpu.VMEM)


def call(kernel, outs, args, limit=4 << 20, scratch=(), flops=1000, specs=None, moved=None):
    if moved is None:
        moved = sum(a.size * a.dtype.itemsize for a in args)
    return pl.pallas_call(
        kernel,
        out_shape=outs,
        in_specs=specs or [VMEM] * len(args),
        out_specs=jax.tree.map(lambda _: VMEM, outs),
        scratch_shapes=scratch,
        compiler_params=pltpu.CompilerParams(vmem_limit_bytes=limit),
        cost_estimate=pl.CostEstimate(flops=flops, bytes_accessed=moved, transcendentals=0),
    )(*args)


def shape(dims, kind=BF16):
    return jax.ShapeDtypeStruct(dims, kind)


def place(group):
    index = lax.axis_index("expert")
    return index // group, lax.rem(index, group)


def iota(dims, axis):
    return lax.broadcasted_iota(jnp.int32, dims, axis)


def code_kernel(group, out):
    expert, _ = place(group)
    index = iota(out.shape, 0)
    out[...] = ((expert ^ (index // CAP)) * CAP + lax.rem(index, CAP)).astype(F32)


def slot_kernel(wanted, tokens, ids, scale, *outs):
    rows = tokens.shape[0]
    width = tokens.shape[1]
    ids_row = ids[...]
    ids_full = jnp.broadcast_to(ids_row, (rows, rows))
    diagonal = iota((rows, rows), 0) == iota((rows, rows), 1)
    ids_column = jnp.sum(jnp.where(diagonal, ids_full, 0), axis=1, keepdims=True)
    earlier = iota((rows, rows), 0) < iota((rows, rows), 1)
    rank = jnp.sum(jnp.where((ids_full == ids_column) & earlier, 1, 0), axis=0, keepdims=True)
    position = (ids_row * CAP + rank).astype(F32)
    chosen = jnp.where(position == wanted[:, 0:rows], 1.0, 0.0).astype(BF16)
    body = jnp.dot(chosen, tokens[...], preferred_element_type=F32)
    value = scale[...]
    first = value.astype(BF16).astype(F32)
    second = (value - first).astype(BF16).astype(F32)
    third = value - first - second
    for i in range(EXPERTS):
        outs[i][:, 0:width] = body[i * CAP : (i + 1) * CAP, :].astype(BF16)
        outs[i][:, width:] = jnp.full((CAP, BLOCKS * LANES), -1.0, BF16)
        for n, piece in enumerate((position, first, second, third)):
            at = width + n * LANES
            outs[i][:, at : at + rows] = jnp.broadcast_to(piece, (CAP, rows)).astype(BF16)


def hidden_of(gate, upward):
    return (gate / (1.0 + jnp.exp(-gate)) * upward).astype(BF16)


def down(hidden, w_down, first, out):
    step = min(512, out.shape[1])
    for n in range(0, out.shape[1], step):
        at = first + n if isinstance(first, int) else pl.multiple_of(first + n, step)
        out[:, n : n + step] = jnp.dot(
            hidden, w_down[0, :, pl.ds(at, step)], preferred_element_type=F32
        ).astype(out.dtype)


def active(tick):
    return pl.when(lax.axis_index("section") == tick)


def deal_rows(source, blocks, own):
    slots = blocks[0].shape[0]
    for m in range(len(blocks)):
        at = pl.multiple_of((own ^ m) * slots, slots)
        blocks[m][...] = source[pl.ds(at, slots), :].astype(BF16)


def join_kernel(group, width, *refs):
    count = group * EXPERTS
    whole, half, table, scale = refs[count : count + 4]
    block, rows = refs[count + 4 :]
    expert, own = place(group)
    slots = EXPERTS * CAP
    for m in range(group):
        for i in range(EXPERTS):
            block[i * CAP : (i + 1) * CAP, :] = refs[m * EXPERTS + i][...].astype(F32)
        at = pl.multiple_of((own ^ m) * slots, slots)
        rows[pl.ds(at, slots), :] = block[...]
    table[...] = rows[:, width : width + LANES].astype(BF16)
    scale[...] = scales(expert, rows[:, width:])
    at = pl.multiple_of(own * half.shape[1], half.shape[1])
    half[...] = rows[:, pl.ds(at, half.shape[1])].astype(BF16)
    whole[...] = rows[:, 0:width].astype(BF16)


def whole_kernel(group, tick, rows, gain, w_gate, w_up, w_down, *outs):
    _, own = place(group)

    @active(tick)
    def _():
        values = rows[...].astype(F32)
        inverse = lax.rsqrt(jnp.mean(values * values, axis=-1, keepdims=True) + 1e-06)
        normed = (values * inverse * gain[...]).astype(BF16)
        gate = jnp.dot(normed, w_gate[0], preferred_element_type=F32)
        upward = jnp.dot(normed, w_up[0], preferred_element_type=F32)
        hidden = hidden_of(gate, upward)
        outs[0][...] = hidden
        width = outs[1].shape[1]
        for m in range(1, group):
            down(hidden, w_down, pl.multiple_of((own ^ m) * width, width), outs[m])


def products(half, at, gain, w_gate, w_up):
    width = half.shape[1]
    values = half[...].astype(F32)
    scaled = (values * gain[:, pl.ds(at, width)]).astype(BF16)
    gate = jnp.dot(scaled, w_gate[0, pl.ds(at, width), :], preferred_element_type=F32)
    upward = jnp.dot(scaled, w_up[0, pl.ds(at, width), :], preferred_element_type=F32)
    return gate, upward, jnp.sum(values * values, axis=-1, keepdims=True)


def half_kernel(group, tick, half, gain, w_gate, w_up, gate_out, up_out, square_out):
    _, own = place(group)

    @active(tick)
    def _():
        width = half.shape[1]
        at = pl.multiple_of(own * width, width)
        gate, upward, square = products(half, at, gain, w_gate, w_up)
        gate_out[...] = gate
        up_out[...] = upward
        square_out[...] = jnp.broadcast_to(square, square_out.shape)


def rest_kernel(group, tick, last, *refs):
    halves = refs[:group]
    gate_in, up_in, square_in, gain, w_gate, w_up, w_down = refs[group : group + 7]
    outs = refs[group + 7 :]
    _, own = place(group)

    @active(tick)
    def _():
        gate, upward, square = gate_in[...], up_in[...], square_in[:, 0:1]
        width = halves[0].shape[1]
        for m in range(1, group):
            at = pl.multiple_of((own ^ m) * width, width)
            more = products(halves[m], at, gain, w_gate, w_up)
            gate, upward, square = gate + more[0], upward + more[1], square + more[2]
        inverse = lax.rsqrt(square / gain.shape[1] + 1e-06)
        hidden = hidden_of(gate * inverse, upward * inverse)
        if last:
            rows, parts = outs[-2:]
            for m in range(group):
                at = pl.multiple_of((own ^ m) * width, width)
                rows[:, pl.ds(at, width)] = halves[m][...].astype(F32)
            down(hidden, w_down, 0, parts)
            deal_rows(parts, outs[:group], own)
            deal_rows(rows, outs[group : group + 1], own)
        else:
            outs[0][...] = hidden
            for m in range(1, group):
                down(hidden, w_down, pl.multiple_of((own ^ m) * width, width), outs[m])


def own_kernel(group, tick, hidden, w_down, out):
    _, own = place(group)

    @active(tick)
    def _():
        down(hidden[...], w_down, pl.multiple_of(own * out.shape[1], out.shape[1]), out)


def slot_codes(expert, dims):
    return expert * CAP + lax.rem(iota(dims, 0), CAP)


def scales(expert, table):
    rows = table.shape[0]
    mine = table[:, 0:LANES] == slot_codes(expert, (rows, LANES)).astype(F32)
    scale = sum(table[:, n * LANES : (n + 1) * LANES] for n in range(1, BLOCKS))
    scale = jnp.sum(jnp.where(mine, scale, 0.0), axis=1, keepdims=True)
    return jnp.broadcast_to(scale, (rows, LANES))


def updated(pieces, before, scale):
    total = pieces[0][...].astype(F32)
    for piece in pieces[1:]:
        total = total + piece[...].astype(F32)
    return before[...].astype(F32) + scale * total


def update_kernel(group, *refs):
    half, table, scale, out, marked = refs[group : group + 5]
    width = out.shape[1]
    result = updated(refs[:group], half, scale[:, 0:1]).astype(BF16)
    out[...] = result
    marked[:, 0:width] = result
    marked[:, width:] = table[...]


def keep_kernel(group, saved, *refs):
    outs, buffer = refs[saved : saved + group], refs[-1]
    section = lax.axis_index("section")
    _, own = place(group)
    for n in range(saved):

        @pl.when(section == n)
        def _(n=n):
            buffer[...] = refs[n][...].astype(F32)

    deal_rows(buffer, outs, own)


def leave_kernel(group, *refs):
    before, scale = refs[group : group + 2]
    kept = refs[group + 2 : 2 * group + 2]
    outs = refs[2 * group + 2 : 2 * group + 2 + EXPERTS]
    rows = refs[-1]
    slots = EXPERTS * CAP
    final = lax.axis_size("section") - 1
    section = lax.axis_index("section")
    _, own = place(group)

    @pl.when(section == final)
    def _():
        at = pl.multiple_of(own * slots, slots)
        rows[...] = updated(refs[:group], before, scale[pl.ds(at, slots), :][:, 0:1])

    @pl.when(section != final)
    def _():
        width = kept[0].shape[1]
        for m in range(group):
            at = pl.multiple_of((own ^ m) * width, width)
            rows[:, pl.ds(at, width)] = kept[m][...].astype(F32)

    for i in range(EXPERTS):
        outs[i][...] = rows[i * CAP : (i + 1) * CAP, :].astype(BF16)


def choice_kernel(group, current, before, out):
    expert, _ = place(group)
    rows = current.shape[0]
    span = EXPERTS * CAP
    here = current[...].astype(F32)
    there = before[:, before.shape[1] - LANES :].astype(F32)
    mine = jnp.where(here == slot_codes(expert, here.shape).astype(F32), 1.0, 0.0).astype(BF16)
    a, b = iota((rows, rows), 0), iota((rows, rows), 1)
    for i in range(EXPERTS):
        codes = slot_codes(expert ^ i, there.shape).astype(F32)
        theirs = jnp.where(there == codes, 1.0, 0.0).astype(BF16)
        both = lax.dot_general(
            mine, theirs, (((1,), (1,)), ((), ())), preferred_element_type=F32
        )
        both = jnp.where(a // CAP == b // CAP, both, 0.0).astype(BF16)
        moved = (a // span) * span + (((lax.rem(a, span) // CAP) ^ i) * CAP) + lax.rem(a, CAP)
        order = jnp.where(moved == b, 1.0, 0.0).astype(BF16)
        out[i] = jnp.dot(both, order, preferred_element_type=F32).astype(BF16)


def early_kernel(turns, *refs):
    choice, out = refs[-2], refs[-1]
    width = out.shape[1]
    total = 0.0
    for n, i in enumerate(turns):
        total = total + jnp.dot(choice[i], refs[n][:, 0:width], preferred_element_type=F32)
    out[...] = total


def pick_kernel(i, *refs):
    sofar, last, choice, out = refs[0], refs[1], refs[2], refs[-1]
    total = sofar[...] + jnp.dot(choice[i], last[...], preferred_element_type=F32)
    out[...] = total.astype(BF16)


def home_kernel(group, *refs):
    table, out, block = refs[EXPERTS:]
    expert, _ = place(group)
    slots = EXPERTS * CAP
    count = out.shape[1]
    for i in range(EXPERTS):
        block[i * CAP : (i + 1) * CAP, :] = refs[i][...].astype(F32)
    lanes = -(-count // 16) * 16
    position = jnp.broadcast_to(table[0:1, 0:lanes].astype(F32), (slots, lanes))
    index = iota((slots, lanes), 0)
    wanted = (expert ^ (index // CAP)) * CAP + lax.rem(index, CAP)
    chosen = jnp.where(position == wanted.astype(F32), 1.0, 0.0).astype(BF16)
    full = lax.dot_general(
        chosen, block[...].astype(BF16), (((0,), (0,)), ((), ())), preferred_element_type=F32
    )
    out[0] = full[0:count, :].astype(BF16)


def local(tokens, expert_ids, gate_scale, norm_gain, w_gate, w_up, w_down):
    peers = lax.axis_size("expert")
    sections = lax.axis_size("section")
    count, width = tokens.shape
    group = peers // EXPERTS
    chunk = width // group
    rows = peers * CAP
    slots = EXPERTS * CAP
    wide = width + BLOCKS * LANES
    weights = (norm_gain, w_gate, w_up, w_down)

    def across(value, i):
        pairs = [(d, (d // group ^ i) * group + d % group) for d in range(peers)]
        if i == 0:
            return value
        return lax.ppermute(value, "expert", pairs)

    def within(value, m):
        return lax.ppermute(value, "expert", [(d, d ^ m) for d in range(peers)])

    def gather(value, marked, tick):
        outs = []
        for i in range(EXPERTS):
            ring = [tick, tick + 1]
            if i == EXPERTS - 1 and sections > 2:
                ring.append(tick - 1 if tick else 2)
            pairs = []
            for s in range(sections):
                to, move = s, lambda d: d ^ 1
                if s in ring:
                    to = ring[(ring.index(s) + 1) % len(ring)]
                    move = lambda d: d
                if s == tick:
                    move = lambda d: (d // group ^ i) * group + d % group
                pairs += [(s * peers + d, to * peers + move(d)) for d in range(peers)]
            outs.append(lax.ppermute(value if i else marked, ("section", "expert"), pairs))
        return outs

    wanted = call(
        functools.partial(code_kernel, group),
        shape((slots, LANES), F32),
        (),
        flops=START_FLOPS,
    )
    sent = call(
        slot_kernel,
        [shape((CAP, wide))] * EXPERTS,
        (wanted, tokens, expert_ids.reshape(1, count), gate_scale),
    )
    arrived = [across(sent[i], i) for i in range(EXPERTS)]
    pieces = list(arrived)
    for m in range(1, group):
        for piece in arrived:
            pieces.append(within(piece, m))
    flops = 6 * rows * width * w_gate.shape[2]
    whole, half, table, scale = call(
        functools.partial(join_kernel, group, width),
        [
            shape((rows, width)),
            shape((rows, chunk)),
            shape((rows, LANES)),
            shape((rows, LANES), F32),
        ],
        tuple(pieces),
        scratch=[pltpu.VMEM((slots, wide), F32), pltpu.VMEM((rows, wide), F32)],
    )
    saved = []
    inner = w_gate.shape[2]
    for tick in range(sections):
        last = tick == sections - 1
        if tick:
            gathered = gather(saved[-1], marked, tick - 1)
            choice = call(
                functools.partial(choice_kernel, group),
                shape((EXPERTS, rows, rows)),
                (table, gathered[0]),
            )
            kept = []
            if last:
                kept = call(
                    functools.partial(keep_kernel, group, len(saved)),
                    [shape((slots, chunk))] * group,
                    tuple(saved),
                    scratch=[pltpu.VMEM((rows, chunk), F32)],
                )
                kept = [kept[0]] + [within(kept[m], m) for m in range(1, group)]
            turns = [EXPERTS - 1, *range(EXPERTS - 2)]
            sofar = call(
                functools.partial(early_kernel, turns),
                shape((rows, chunk), F32),
                (*[gathered[i] for i in turns], choice),
                flops=2 * rows * rows * EXPERTS * chunk,
            )
            half = call(
                functools.partial(pick_kernel, EXPERTS - 2),
                shape((rows, chunk)),
                (sofar, gathered[EXPERTS - 2], choice, *kept),
            )
            halves = [half] + [within(half, m) for m in range(1, group)]
            begun = call(
                functools.partial(half_kernel, group, tick),
                [shape((rows, inner), F32)] * 2 + [shape((rows, LANES), F32)],
                (half, *weights[:3]),
                flops=flops // (3 * group) * 2,
            )
            outs = [shape((rows, inner))] + [shape((rows, chunk))] * (group - 1)
            scratch = []
            if last:
                outs = [shape((slots, width))] * (group + 1)
                scratch = [pltpu.VMEM((rows, width), F32)] * 2
            outs = call(
                functools.partial(rest_kernel, group, tick, last),
                outs,
                (*halves, *begun, *weights),
                scratch=scratch,
                flops=flops // 2,
            )
        else:
            outs = call(
                functools.partial(whole_kernel, group, tick),
                [shape((rows, inner))] + [shape((rows, chunk))] * (group - 1),
                (whole, *weights),
                flops=flops * 5 // 6,
            )
        terms = [within(outs[m], m) for m in range(1, group)]
        if last:
            terms = [outs[0]] + terms
        else:
            own = call(
                functools.partial(own_kernel, group, tick),
                shape((rows, chunk)),
                (outs[0], w_down),
                flops=flops // 6,
            )
            terms = [own] + terms
        if not last:
            latest, marked = call(
                functools.partial(update_kernel, group),
                [shape((rows, chunk)), shape((rows, chunk + LANES))],
                (*terms, half, table, scale),
            )
            saved.append(latest)
    leaving = call(
        functools.partial(leave_kernel, group),
        [shape((CAP, width))] * EXPERTS,
        (*terms, outs[group], scale, *kept),
        scratch=[pltpu.VMEM((slots, width), F32)],
    )
    back = [across(leaving[i], i) for i in range(EXPERTS)]
    return call(
        functools.partial(home_kernel, group),
        shape((1, count, width)),
        (*back, sent[0][:, width : width + LANES]),
        scratch=[pltpu.VMEM((slots, width), F32)],
    )


def solution(mesh):
    return jax.shard_map(
        local,
        mesh=mesh,
        in_specs=(
            P("expert", None),
            P("section", "expert", None),
            P("section", "expert"),
            P("section", None),
            P("section", None, "expert"),
            P("section", None, "expert"),
            P("section", "expert", None),
        ),
        out_specs=P("section", "expert", None),
        check_vma=False,
    )
```

```python
import functools

import jax
import jax.numpy as jnp
from jax import lax
from jax.experimental import pallas as pl
from jax.experimental.pallas import tpu as pltpu
from jax.sharding import PartitionSpec as P


EXPERTS = 4
CAP = 2
LANES = 128
BLOCKS = 4
RELAYED = (0,)
START_FLOPS = 10_000_000_000
F32 = jnp.float32
BF16 = jnp.bfloat16
VMEM = pl.BlockSpec(memory_space=pltpu.VMEM)


def call(kernel, outs, args, limit=4 << 20, scratch=(), flops=1000, specs=None, moved=None):
    if moved is None:
        moved = sum(a.size * a.dtype.itemsize for a in args)
    return pl.pallas_call(
        kernel,
        out_shape=outs,
        in_specs=specs or [VMEM] * len(args),
        out_specs=jax.tree.map(lambda _: VMEM, outs),
        scratch_shapes=scratch,
        compiler_params=pltpu.CompilerParams(vmem_limit_bytes=limit),
        cost_estimate=pl.CostEstimate(flops=flops, bytes_accessed=moved, transcendentals=0),
    )(*args)


def shape(dims, kind=BF16):
    return jax.ShapeDtypeStruct(dims, kind)


def place(group):
    index = lax.axis_index("expert")
    return index // group, lax.rem(index, group)


def iota(dims, axis):
    return lax.broadcasted_iota(jnp.int32, dims, axis)


def code_kernel(group, out):
    expert, _ = place(group)
    index = iota(out.shape, 0)
    out[...] = ((expert ^ (index // CAP)) * CAP + lax.rem(index, CAP)).astype(F32)


def slot_kernel(wanted, tokens, ids, scale, *outs):
    rows = tokens.shape[0]
    width = tokens.shape[1]
    ids_row = ids[...]
    ids_full = jnp.broadcast_to(ids_row, (rows, rows))
    diagonal = iota((rows, rows), 0) == iota((rows, rows), 1)
    ids_column = jnp.sum(jnp.where(diagonal, ids_full, 0), axis=1, keepdims=True)
    earlier = iota((rows, rows), 0) < iota((rows, rows), 1)
    rank = jnp.sum(jnp.where((ids_full == ids_column) & earlier, 1, 0), axis=0, keepdims=True)
    position = (ids_row * CAP + rank).astype(F32)
    chosen = jnp.where(position == wanted[:, 0:rows], 1.0, 0.0).astype(BF16)
    body = jnp.dot(chosen, tokens[...], preferred_element_type=F32)
    value = scale[...]
    first = value.astype(BF16).astype(F32)
    second = (value - first).astype(BF16).astype(F32)
    third = value - first - second
    for i in range(EXPERTS):
        outs[i][:, 0:width] = body[i * CAP : (i + 1) * CAP, :].astype(BF16)
        outs[i][:, width:] = jnp.full((CAP, BLOCKS * LANES), -1.0, BF16)
        for n, piece in enumerate((position, first, second, third)):
            at = width + n * LANES
            outs[i][:, at : at + rows] = jnp.broadcast_to(piece, (CAP, rows)).astype(BF16)


def hidden_of(gate, upward):
    return (gate / (1.0 + jnp.exp(-gate)) * upward).astype(BF16)


def down(hidden, w_down, first, out):
    step = min(512, out.shape[1])
    for n in range(0, out.shape[1], step):
        at = first + n if isinstance(first, int) else pl.multiple_of(first + n, step)
        out[:, n : n + step] = jnp.dot(
            hidden, w_down[0, :, pl.ds(at, step)], preferred_element_type=F32
        ).astype(out.dtype)


def active(tick):
    return pl.when(lax.axis_index("section") == tick)


def deal_rows(source, blocks, own):
    slots = blocks[0].shape[0]
    for m in range(len(blocks)):
        at = pl.multiple_of((own ^ m) * slots, slots)
        blocks[m][...] = source[pl.ds(at, slots), :].astype(BF16)


def join_kernel(group, width, *refs):
    count = group * EXPERTS
    whole, half, table, scale = refs[count : count + 4]
    block, rows = refs[count + 4 :]
    expert, own = place(group)
    slots = EXPERTS * CAP
    for m in range(group):
        for i in range(EXPERTS):
            block[i * CAP : (i + 1) * CAP, :] = refs[m * EXPERTS + i][...].astype(F32)
        at = pl.multiple_of((own ^ m) * slots, slots)
        rows[pl.ds(at, slots), :] = block[...]
    table[...] = rows[:, width : width + LANES].astype(BF16)
    scale[...] = scales(expert, rows[:, width:])
    at = pl.multiple_of(own * half.shape[1], half.shape[1])
    half[...] = rows[:, pl.ds(at, half.shape[1])].astype(BF16)
    whole[...] = rows[:, 0:width].astype(BF16)


def whole_kernel(group, tick, rows, gain, w_gate, w_up, w_down, *outs):
    _, own = place(group)

    @active(tick)
    def _():
        values = rows[...].astype(F32)
        inverse = lax.rsqrt(jnp.mean(values * values, axis=-1, keepdims=True) + 1e-06)
        normed = (values * inverse * gain[...]).astype(BF16)
        gate = jnp.dot(normed, w_gate[0], preferred_element_type=F32)
        upward = jnp.dot(normed, w_up[0], preferred_element_type=F32)
        hidden = hidden_of(gate, upward)
        outs[0][...] = hidden
        width = outs[1].shape[1]
        for m in range(1, group):
            down(hidden, w_down, pl.multiple_of((own ^ m) * width, width), outs[m])


def products(half, at, gain, w_gate, w_up):
    width = half.shape[1]
    values = half[...].astype(F32)
    scaled = (values * gain[:, pl.ds(at, width)]).astype(BF16)
    gate = jnp.dot(scaled, w_gate[0, pl.ds(at, width), :], preferred_element_type=F32)
    upward = jnp.dot(scaled, w_up[0, pl.ds(at, width), :], preferred_element_type=F32)
    return gate, upward, jnp.sum(values * values, axis=-1, keepdims=True)


def half_kernel(group, tick, half, gain, w_gate, w_up, gate_out, up_out, square_out):
    _, own = place(group)

    @active(tick)
    def _():
        width = half.shape[1]
        at = pl.multiple_of(own * width, width)
        gate, upward, square = products(half, at, gain, w_gate, w_up)
        gate_out[...] = gate
        up_out[...] = upward
        square_out[...] = jnp.broadcast_to(square, square_out.shape)


def rest_kernel(group, tick, last, *refs):
    halves = refs[:group]
    gate_in, up_in, square_in, gain, w_gate, w_up, w_down = refs[group : group + 7]
    outs = refs[group + 7 :]
    _, own = place(group)

    @active(tick)
    def _():
        gate, upward, square = gate_in[...], up_in[...], square_in[:, 0:1]
        width = halves[0].shape[1]
        for m in range(1, group):
            at = pl.multiple_of((own ^ m) * width, width)
            more = products(halves[m], at, gain, w_gate, w_up)
            gate, upward, square = gate + more[0], upward + more[1], square + more[2]
        inverse = lax.rsqrt(square / gain.shape[1] + 1e-06)
        hidden = hidden_of(gate * inverse, upward * inverse)
        if last:
            rows, parts = outs[-2:]
            for m in range(group):
                at = pl.multiple_of((own ^ m) * width, width)
                rows[:, pl.ds(at, width)] = halves[m][...].astype(F32)
            down(hidden, w_down, 0, parts)
            deal_rows(parts, outs[:group], own)
            deal_rows(rows, outs[group : group + 1], own)
        else:
            outs[0][...] = hidden
            for m in range(1, group):
                down(hidden, w_down, pl.multiple_of((own ^ m) * width, width), outs[m])


def own_kernel(group, tick, hidden, w_down, out):
    _, own = place(group)

    @active(tick)
    def _():
        down(hidden[...], w_down, pl.multiple_of(own * out.shape[1], out.shape[1]), out)


def slot_codes(expert, dims):
    return expert * CAP + lax.rem(iota(dims, 0), CAP)


def scales(expert, table):
    rows = table.shape[0]
    mine = table[:, 0:LANES] == slot_codes(expert, (rows, LANES)).astype(F32)
    scale = sum(table[:, n * LANES : (n + 1) * LANES] for n in range(1, BLOCKS))
    scale = jnp.sum(jnp.where(mine, scale, 0.0), axis=1, keepdims=True)
    return jnp.broadcast_to(scale, (rows, LANES))


def updated(pieces, before, scale):
    total = pieces[0][...].astype(F32)
    for piece in pieces[1:]:
        total = total + piece[...].astype(F32)
    return before[...].astype(F32) + scale * total


def update_kernel(group, *refs):
    half, table, scale, out, marked = refs[group : group + 5]
    width = out.shape[1]
    result = updated(refs[:group], half, scale[:, 0:1]).astype(BF16)
    out[...] = result
    marked[:, 0:width] = result
    marked[:, width:] = table[...]


def keep_kernel(group, saved, *refs):
    outs, buffer = refs[saved : saved + group], refs[-1]
    section = lax.axis_index("section")
    _, own = place(group)
    for n in range(saved):

        @pl.when(section == n)
        def _(n=n):
            buffer[...] = refs[n][...].astype(F32)

    deal_rows(buffer, outs, own)


def leave_kernel(group, *refs):
    before, scale = refs[group : group + 2]
    kept = refs[group + 2 : 2 * group + 2]
    outs = refs[2 * group + 2 : 2 * group + 2 + EXPERTS]
    rows = refs[-1]
    slots = EXPERTS * CAP
    final = lax.axis_size("section") - 1
    section = lax.axis_index("section")
    _, own = place(group)

    @pl.when(section == final)
    def _():
        at = pl.multiple_of(own * slots, slots)
        rows[...] = updated(refs[:group], before, scale[pl.ds(at, slots), :][:, 0:1])

    @pl.when(section != final)
    def _():
        width = kept[0].shape[1]
        for m in range(group):
            at = pl.multiple_of((own ^ m) * width, width)
            rows[:, pl.ds(at, width)] = kept[m][...].astype(F32)

    for i in range(EXPERTS):
        outs[i][...] = rows[i * CAP : (i + 1) * CAP, :].astype(BF16)


def choice_kernel(group, current, before, out):
    expert, _ = place(group)
    rows = current.shape[0]
    span = EXPERTS * CAP
    here = current[...].astype(F32)
    there = before[:, before.shape[1] - LANES :].astype(F32)
    mine = jnp.where(here == slot_codes(expert, here.shape).astype(F32), 1.0, 0.0).astype(BF16)
    a, b = iota((rows, rows), 0), iota((rows, rows), 1)
    for i in range(EXPERTS):
        codes = slot_codes(expert ^ i, there.shape).astype(F32)
        theirs = jnp.where(there == codes, 1.0, 0.0).astype(BF16)
        both = lax.dot_general(
            mine, theirs, (((1,), (1,)), ((), ())), preferred_element_type=F32
        )
        both = jnp.where(a // CAP == b // CAP, both, 0.0).astype(BF16)
        moved = (a // span) * span + (((lax.rem(a, span) // CAP) ^ i) * CAP) + lax.rem(a, CAP)
        order = jnp.where(moved == b, 1.0, 0.0).astype(BF16)
        out[i] = jnp.dot(both, order, preferred_element_type=F32).astype(BF16)


def early_kernel(turns, *refs):
    choice, out = refs[-2], refs[-1]
    width = out.shape[1]
    total = 0.0
    for n, i in enumerate(turns):
        total = total + jnp.dot(choice[i], refs[n][:, 0:width], preferred_element_type=F32)
    out[...] = total


def pick_kernel(i, *refs):
    sofar, last, choice, out = refs[0], refs[1], refs[2], refs[-1]
    piece = last[:, 0 : out.shape[1]]
    total = sofar[...] + jnp.dot(choice[i], piece, preferred_element_type=F32)
    out[...] = total.astype(BF16)


def home_kernel(group, *refs):
    table, out, block = refs[EXPERTS:]
    expert, _ = place(group)
    slots = EXPERTS * CAP
    count = out.shape[1]
    for i in range(EXPERTS):
        block[i * CAP : (i + 1) * CAP, :] = refs[i][...].astype(F32)
    lanes = -(-count // 16) * 16
    position = jnp.broadcast_to(table[0:1, 0:lanes].astype(F32), (slots, lanes))
    index = iota((slots, lanes), 0)
    wanted = (expert ^ (index // CAP)) * CAP + lax.rem(index, CAP)
    chosen = jnp.where(position == wanted.astype(F32), 1.0, 0.0).astype(BF16)
    full = lax.dot_general(
        chosen, block[...].astype(BF16), (((0,), (0,)), ((), ())), preferred_element_type=F32
    )
    out[0] = full[0:count, :].astype(BF16)


def local(tokens, expert_ids, gate_scale, norm_gain, w_gate, w_up, w_down):
    peers = lax.axis_size("expert")
    sections = lax.axis_size("section")
    count, width = tokens.shape
    group = peers // EXPERTS
    chunk = width // group
    rows = peers * CAP
    slots = EXPERTS * CAP
    wide = width + BLOCKS * LANES
    weights = (norm_gain, w_gate, w_up, w_down)

    def across(value, i):
        pairs = [(d, (d // group ^ i) * group + d % group) for d in range(peers)]
        if i == 0:
            return value
        return lax.ppermute(value, "expert", pairs)

    def within(value, m):
        return lax.ppermute(value, "expert", [(d, d ^ m) for d in range(peers)])

    def gather(value, marked, tick):
        outs = {}
        turns = gather_turns(tick)
        for i in turns:
            ring = [tick, tick + 1]
            if i == turns[0] and sections > 2:
                ring.append((tick + 2) % sections if tick else min(3, sections - 1))
            pairs = []
            for s in range(sections):
                to, move = s, lambda d: d ^ 1
                if s in ring:
                    to = ring[(ring.index(s) + 1) % len(ring)]
                    move = lambda d: d
                if s == tick:
                    move = lambda d: (d // group ^ i) * group + d % group
                pairs += [(s * peers + d, to * peers + move(d)) for d in range(peers)]
            outs[i] = lax.ppermute(value if i else marked, ("section", "expert"), pairs)
        if 1 not in outs:
            outs[1] = across(outs[0], 1)
            turns = [*turns, 1]
        return outs, turns

    wanted = call(
        functools.partial(code_kernel, group),
        shape((slots, LANES), F32),
        (),
        flops=START_FLOPS,
    )
    sent = call(
        slot_kernel,
        [shape((CAP, wide))] * EXPERTS,
        (wanted, tokens, expert_ids.reshape(1, count), gate_scale),
    )
    arrived = [across(sent[i], i) for i in range(EXPERTS)]
    pieces = list(arrived)
    for m in range(1, group):
        for piece in arrived:
            pieces.append(within(piece, m))
    flops = 6 * rows * width * w_gate.shape[2]
    whole, half, table, scale = call(
        functools.partial(join_kernel, group, width),
        [
            shape((rows, width)),
            shape((rows, chunk)),
            shape((rows, LANES)),
            shape((rows, LANES), F32),
        ],
        tuple(pieces),
        scratch=[pltpu.VMEM((slots, wide), F32), pltpu.VMEM((rows, wide), F32)],
    )
    saved = []
    inner = w_gate.shape[2]
    for tick in range(sections):
        last = tick == sections - 1
        if tick:
            gathered, turns = gather(saved[-1], marked, tick - 1)
            choice = call(
                functools.partial(choice_kernel, group),
                shape((EXPERTS, rows, rows)),
                (table, gathered[0]),
            )
            kept = []
            if last:
                kept = call(
                    functools.partial(keep_kernel, group, len(saved)),
                    [shape((slots, chunk))] * group,
                    tuple(saved),
                    scratch=[pltpu.VMEM((rows, chunk), F32)],
                )
                kept = [kept[0]] + [within(kept[m], m) for m in range(1, group)]
            sofar = call(
                functools.partial(early_kernel, turns[:-1]),
                shape((rows, chunk), F32),
                (*[gathered[i] for i in turns[:-1]], choice),
                flops=2 * rows * rows * EXPERTS * chunk,
            )
            half = call(
                functools.partial(pick_kernel, turns[-1]),
                shape((rows, chunk)),
                (sofar, gathered[turns[-1]], choice, *kept),
            )
            halves = [half] + [within(half, m) for m in range(1, group)]
            begun = call(
                functools.partial(half_kernel, group, tick),
                [shape((rows, inner), F32)] * 2 + [shape((rows, LANES), F32)],
                (half, *weights[:3]),
                flops=flops // (3 * group) * 2,
            )
            outs = [shape((rows, inner))] + [shape((rows, chunk))] * (group - 1)
            scratch = []
            if last:
                outs = [shape((slots, width))] * (group + 1)
                scratch = [pltpu.VMEM((rows, width), F32)] * 2
            outs = call(
                functools.partial(rest_kernel, group, tick, last),
                outs,
                (*halves, *begun, *weights),
                scratch=scratch,
                flops=flops // 2,
            )
        else:
            outs = call(
                functools.partial(whole_kernel, group, tick),
                [shape((rows, inner))] + [shape((rows, chunk))] * (group - 1),
                (whole, *weights),
                flops=flops * 5 // 6,
            )
        terms = [within(outs[m], m) for m in range(1, group)]
        if last:
            terms = [outs[0]] + terms
        else:
            own = call(
                functools.partial(own_kernel, group, tick),
                shape((rows, chunk)),
                (outs[0], w_down),
                flops=flops // 6,
            )
            terms = [own] + terms
        if not last:
            latest, marked = call(
                functools.partial(update_kernel, group),
                [shape((rows, chunk)), shape((rows, chunk + LANES))],
                (*terms, half, table, scale),
            )
            saved.append(latest)
    leaving = call(
        functools.partial(leave_kernel, group),
        [shape((CAP, width))] * EXPERTS,
        (*terms, outs[group], scale, *kept),
        scratch=[pltpu.VMEM((slots, width), F32)],
    )
    back = [across(leaving[i], i) for i in range(EXPERTS)]
    return call(
        functools.partial(home_kernel, group),
        shape((1, count, width)),
        (*back, sent[0][:, width : width + LANES]),
        scratch=[pltpu.VMEM((slots, width), F32)],
    )


def gather_turns(tick):
    far = EXPERTS - 1
    return [0, far, *range(2, far)] if tick in RELAYED else [far, *range(far)]


def solution(mesh):
    return jax.shard_map(
        local,
        mesh=mesh,
        in_specs=(
            P("expert", None),
            P("section", "expert", None),
            P("section", "expert"),
            P("section", None),
            P("section", None, "expert"),
            P("section", None, "expert"),
            P("section", "expert", None),
        ),
        out_specs=P("section", "expert", None),
        check_vma=False,
    )
```

```python
import functools

import jax
import jax.numpy as jnp
from jax import lax
from jax.experimental import pallas as pl
from jax.experimental.pallas import tpu as pltpu
from jax.sharding import PartitionSpec as P


EXPERTS = 4
CAP = 2
LANES = 128
BLOCKS = 4
RELAYED = (0,)
START_FLOPS = 10_000_000_000
F32 = jnp.float32
BF16 = jnp.bfloat16
VMEM = pl.BlockSpec(memory_space=pltpu.VMEM)


def call(kernel, outs, args, limit=4 << 20, scratch=(), flops=1000, specs=None, moved=None):
    if moved is None:
        moved = sum(a.size * a.dtype.itemsize for a in args)
    return pl.pallas_call(
        kernel,
        out_shape=outs,
        in_specs=specs or [VMEM] * len(args),
        out_specs=jax.tree.map(lambda _: VMEM, outs),
        scratch_shapes=scratch,
        compiler_params=pltpu.CompilerParams(vmem_limit_bytes=limit),
        cost_estimate=pl.CostEstimate(flops=flops, bytes_accessed=moved, transcendentals=0),
    )(*args)


def shape(dims, kind=BF16):
    return jax.ShapeDtypeStruct(dims, kind)


def place(group):
    index = lax.axis_index("expert")
    return index // group, lax.rem(index, group)


def iota(dims, axis):
    return lax.broadcasted_iota(jnp.int32, dims, axis)


def code_kernel(group, out):
    expert, _ = place(group)
    index = iota(out.shape, 0)
    out[...] = ((expert ^ (index // CAP)) * CAP + lax.rem(index, CAP)).astype(F32)


def slot_kernel(wanted, tokens, ids, scale, *outs):
    rows = tokens.shape[0]
    width = tokens.shape[1]
    ids_row = ids[...]
    ids_full = jnp.broadcast_to(ids_row, (rows, rows))
    diagonal = iota((rows, rows), 0) == iota((rows, rows), 1)
    ids_column = jnp.sum(jnp.where(diagonal, ids_full, 0), axis=1, keepdims=True)
    earlier = iota((rows, rows), 0) < iota((rows, rows), 1)
    rank = jnp.sum(jnp.where((ids_full == ids_column) & earlier, 1, 0), axis=0, keepdims=True)
    position = (ids_row * CAP + rank).astype(F32)
    chosen = jnp.where(position == wanted[:, 0:rows], 1.0, 0.0).astype(BF16)
    body = jnp.dot(chosen, tokens[...], preferred_element_type=F32)
    value = scale[...]
    first = value.astype(BF16).astype(F32)
    second = (value - first).astype(BF16).astype(F32)
    third = value - first - second
    for i in range(EXPERTS):
        outs[i][:, 0:width] = body[i * CAP : (i + 1) * CAP, :].astype(BF16)
        outs[i][:, width:] = jnp.full((CAP, BLOCKS * LANES), -1.0, BF16)
        for n, piece in enumerate((position, first, second, third)):
            at = width + n * LANES
            outs[i][:, at : at + rows] = jnp.broadcast_to(piece, (CAP, rows)).astype(BF16)


def hidden_of(gate, upward):
    return (gate / (1.0 + jnp.exp(-gate)) * upward).astype(BF16)


def down(hidden, w_down, first, out):
    step = min(512, out.shape[1])
    for n in range(0, out.shape[1], step):
        at = first + n if isinstance(first, int) else pl.multiple_of(first + n, step)
        out[:, n : n + step] = jnp.dot(
            hidden, w_down[0, :, pl.ds(at, step)], preferred_element_type=F32
        ).astype(out.dtype)


def active(tick):
    return pl.when(lax.axis_index("section") == tick)


def deal_rows(source, blocks, own):
    slots = blocks[0].shape[0]
    for m in range(len(blocks)):
        at = pl.multiple_of((own ^ m) * slots, slots)
        blocks[m][...] = source[pl.ds(at, slots), :].astype(BF16)


def join_kernel(group, width, *refs):
    count = group * EXPERTS
    whole, half, table, scale = refs[count : count + 4]
    block, rows = refs[count + 4 :]
    expert, own = place(group)
    slots = EXPERTS * CAP
    for m in range(group):
        for i in range(EXPERTS):
            block[i * CAP : (i + 1) * CAP, :] = refs[m * EXPERTS + i][...].astype(F32)
        at = pl.multiple_of((own ^ m) * slots, slots)
        rows[pl.ds(at, slots), :] = block[...]
    table[...] = rows[:, width : width + LANES].astype(BF16)
    scale[...] = scales(expert, rows[:, width:])
    at = pl.multiple_of(own * half.shape[1], half.shape[1])
    half[...] = rows[:, pl.ds(at, half.shape[1])].astype(BF16)
    whole[...] = rows[:, 0:width].astype(BF16)


def whole_kernel(group, tick, rows, gain, w_gate, w_up, w_down, *outs):
    _, own = place(group)

    @active(tick)
    def _():
        values = rows[...].astype(F32)
        inverse = lax.rsqrt(jnp.mean(values * values, axis=-1, keepdims=True) + 1e-06)
        normed = (values * inverse * gain[...]).astype(BF16)
        gate = jnp.dot(normed, w_gate[0], preferred_element_type=F32)
        upward = jnp.dot(normed, w_up[0], preferred_element_type=F32)
        hidden = hidden_of(gate, upward)
        outs[0][...] = hidden
        width = outs[1].shape[1]
        for m in range(1, group):
            down(hidden, w_down, pl.multiple_of((own ^ m) * width, width), outs[m])


def products(half, at, gain, w_gate, w_up):
    width = half.shape[1]
    values = half[...].astype(F32)
    scaled = (values * gain[:, pl.ds(at, width)]).astype(BF16)
    gate = jnp.dot(scaled, w_gate[0, pl.ds(at, width), :], preferred_element_type=F32)
    upward = jnp.dot(scaled, w_up[0, pl.ds(at, width), :], preferred_element_type=F32)
    return gate, upward, jnp.sum(values * values, axis=-1, keepdims=True)


def half_kernel(group, tick, half, gain, w_gate, w_up, gate_out, up_out, square_out):
    _, own = place(group)

    @active(tick)
    def _():
        width = half.shape[1]
        at = pl.multiple_of(own * width, width)
        gate, upward, square = products(half, at, gain, w_gate, w_up)
        gate_out[...] = gate
        up_out[...] = upward
        square_out[...] = jnp.broadcast_to(square, square_out.shape)


def rest_kernel(group, tick, last, *refs):
    halves = refs[:group]
    gate_in, up_in, square_in, gain, w_gate, w_up, w_down = refs[group : group + 7]
    outs = refs[group + 7 :]
    _, own = place(group)

    @active(tick)
    def _():
        gate, upward, square = gate_in[...], up_in[...], square_in[:, 0:1]
        width = halves[0].shape[1]
        for m in range(1, group):
            at = pl.multiple_of((own ^ m) * width, width)
            more = products(halves[m], at, gain, w_gate, w_up)
            gate, upward, square = gate + more[0], upward + more[1], square + more[2]
        inverse = lax.rsqrt(square / gain.shape[1] + 1e-06)
        hidden = hidden_of(gate * inverse, upward * inverse)
        if last:
            rows, parts = outs[-2:]
            for m in range(group):
                at = pl.multiple_of((own ^ m) * width, width)
                rows[:, pl.ds(at, width)] = halves[m][...].astype(F32)
            down(hidden, w_down, 0, parts)
            deal_rows(parts, outs[:group], own)
            deal_rows(rows, outs[group : group + 1], own)
        else:
            outs[0][...] = hidden
            for m in range(1, group):
                down(hidden, w_down, pl.multiple_of((own ^ m) * width, width), outs[m])


def own_kernel(group, tick, hidden, w_down, out):
    _, own = place(group)

    @active(tick)
    def _():
        down(hidden[...], w_down, pl.multiple_of(own * out.shape[1], out.shape[1]), out)


def slot_codes(expert, dims):
    return expert * CAP + lax.rem(iota(dims, 0), CAP)


def scales(expert, table):
    rows = table.shape[0]
    mine = table[:, 0:LANES] == slot_codes(expert, (rows, LANES)).astype(F32)
    scale = sum(table[:, n * LANES : (n + 1) * LANES] for n in range(1, BLOCKS))
    scale = jnp.sum(jnp.where(mine, scale, 0.0), axis=1, keepdims=True)
    return jnp.broadcast_to(scale, (rows, LANES))


def updated(pieces, before, scale):
    total = pieces[0][...].astype(F32)
    for piece in pieces[1:]:
        total = total + piece[...].astype(F32)
    return before[...].astype(F32) + scale * total


def update_kernel(group, *refs):
    half, table, scale, out, marked = refs[group : group + 5]
    width = out.shape[1]
    result = updated(refs[:group], half, scale[:, 0:1]).astype(BF16)
    out[...] = result
    marked[:, 0:width] = result
    marked[:, width:] = table[...]


def keep_kernel(group, saved, *refs):
    outs, buffer = refs[saved : saved + group], refs[-1]
    section = lax.axis_index("section")
    _, own = place(group)
    for n in range(saved):

        @pl.when(section == n)
        def _(n=n):
            buffer[...] = refs[n][...].astype(F32)

    deal_rows(buffer, outs, own)


def leave_kernel(group, *refs):
    before, scale = refs[group : group + 2]
    kept = refs[group + 2 : 2 * group + 2]
    outs = refs[2 * group + 2 : 2 * group + 2 + EXPERTS]
    rows = refs[-1]
    slots = EXPERTS * CAP
    final = lax.axis_size("section") - 1
    section = lax.axis_index("section")
    _, own = place(group)

    @pl.when(section == final)
    def _():
        at = pl.multiple_of(own * slots, slots)
        rows[...] = updated(refs[:group], before, scale[pl.ds(at, slots), :][:, 0:1])

    @pl.when(section != final)
    def _():
        width = kept[0].shape[1]
        for m in range(group):
            at = pl.multiple_of((own ^ m) * width, width)
            rows[:, pl.ds(at, width)] = kept[m][...].astype(F32)

    for i in range(EXPERTS):
        outs[i][...] = rows[i * CAP : (i + 1) * CAP, :].astype(BF16)


def choice_kernel(group, current, before, out):
    expert, _ = place(group)
    rows = current.shape[0]
    span = EXPERTS * CAP
    here = current[...].astype(F32)
    there = before[:, before.shape[1] - LANES :].astype(F32)
    mine = jnp.where(here == slot_codes(expert, here.shape).astype(F32), 1.0, 0.0).astype(BF16)
    a, b = iota((rows, rows), 0), iota((rows, rows), 1)
    for i in range(EXPERTS):
        codes = slot_codes(expert ^ i, there.shape).astype(F32)
        theirs = jnp.where(there == codes, 1.0, 0.0).astype(BF16)
        both = lax.dot_general(
            mine, theirs, (((1,), (1,)), ((), ())), preferred_element_type=F32
        )
        both = jnp.where(a // CAP == b // CAP, both, 0.0).astype(BF16)
        moved = (a // span) * span + (((lax.rem(a, span) // CAP) ^ i) * CAP) + lax.rem(a, CAP)
        order = jnp.where(moved == b, 1.0, 0.0).astype(BF16)
        out[i] = jnp.dot(both, order, preferred_element_type=F32).astype(BF16)


def early_kernel(turns, *refs):
    choice, out = refs[-2], refs[-1]
    width = out.shape[1]
    total = 0.0
    for n, i in enumerate(turns):
        total = total + jnp.dot(choice[i], refs[n][:, 0:width], preferred_element_type=F32)
    out[...] = total


def pick_kernel(i, *refs):
    sofar, last, choice, out = refs[0], refs[1], refs[2], refs[-1]
    piece = last[:, 0 : out.shape[1]]
    total = sofar[...] + jnp.dot(choice[i], piece, preferred_element_type=F32)
    out[...] = total.astype(BF16)


def home_kernel(group, *refs):
    table, out, block = refs[EXPERTS:]
    expert, _ = place(group)
    slots = EXPERTS * CAP
    count = out.shape[1]
    for i in range(EXPERTS):
        block[i * CAP : (i + 1) * CAP, :] = refs[i][...].astype(F32)
    lanes = -(-count // 16) * 16
    position = jnp.broadcast_to(table[0:1, 0:lanes].astype(F32), (slots, lanes))
    index = iota((slots, lanes), 0)
    wanted = (expert ^ (index // CAP)) * CAP + lax.rem(index, CAP)
    chosen = jnp.where(position == wanted.astype(F32), 1.0, 0.0).astype(BF16)
    full = lax.dot_general(
        chosen, block[...].astype(BF16), (((0,), (0,)), ((), ())), preferred_element_type=F32
    )
    out[0] = full[0:count, :].astype(BF16)


def local(tokens, expert_ids, gate_scale, norm_gain, w_gate, w_up, w_down):
    peers = lax.axis_size("expert")
    sections = lax.axis_size("section")
    count, width = tokens.shape
    group = peers // EXPERTS
    chunk = width // group
    rows = peers * CAP
    slots = EXPERTS * CAP
    wide = width + BLOCKS * LANES
    weights = (norm_gain, w_gate, w_up, w_down)

    def across(value, i):
        pairs = [(d, (d // group ^ i) * group + d % group) for d in range(peers)]
        if i == 0:
            return value
        return lax.ppermute(value, "expert", pairs)

    def within(value, m):
        return lax.ppermute(value, "expert", [(d, d ^ m) for d in range(peers)])

    def gather(value, marked, tick):
        outs = {}
        turns = gather_turns(tick)
        for i in turns:
            ring = [tick, tick + 1]
            if i == turns[0] and sections > 2:
                ring.append((tick + 2) % sections)
            pairs = []
            for s in range(sections):
                to, move = s, lambda d: d ^ 1
                if s in ring:
                    to = ring[(ring.index(s) + 1) % len(ring)]
                    move = lambda d: d
                if s == tick:
                    move = lambda d: (d // group ^ i) * group + d % group
                pairs += [(s * peers + d, to * peers + move(d)) for d in range(peers)]
            outs[i] = lax.ppermute(value if i else marked, ("section", "expert"), pairs)
        if 1 not in outs:
            pairs = [
                (s * peers + d, s * peers + ((d // group ^ 1) * group + d % group if s == tick + 1 else d ^ 1))
                for s in range(sections)
                for d in range(peers)
            ]
            outs[1] = lax.ppermute(outs[0], ("section", "expert"), pairs)
            turns = [*turns, 1]
        return outs, turns

    wanted = call(
        functools.partial(code_kernel, group), shape((slots, LANES), F32), (), flops=START_FLOPS
    )
    sent = call(
        slot_kernel,
        [shape((CAP, wide))] * EXPERTS,
        (wanted, tokens, expert_ids.reshape(1, count), gate_scale),
    )
    arrived = [across(sent[i], i) for i in range(EXPERTS)]
    pieces = list(arrived)
    for m in range(1, group):
        for piece in arrived:
            pieces.append(within(piece, m))
    flops = 6 * rows * width * w_gate.shape[2]
    whole, half, table, scale = call(
        functools.partial(join_kernel, group, width),
        [
            shape((rows, width)),
            shape((rows, chunk)),
            shape((rows, LANES)),
            shape((rows, LANES), F32),
        ],
        tuple(pieces),
        scratch=[pltpu.VMEM((slots, wide), F32), pltpu.VMEM((rows, wide), F32)],
    )
    saved = []
    inner = w_gate.shape[2]
    for tick in range(sections):
        last = tick == sections - 1
        if tick:
            gathered, turns = gather(saved[-1], marked, tick - 1)
            choice = call(
                functools.partial(choice_kernel, group),
                shape((EXPERTS, rows, rows)),
                (table, gathered[0]),
            )
            kept = []
            if last:
                kept = call(
                    functools.partial(keep_kernel, group, len(saved)),
                    [shape((slots, chunk))] * group,
                    tuple(saved),
                    scratch=[pltpu.VMEM((rows, chunk), F32)],
                )
                kept = [kept[0]] + [within(kept[m], m) for m in range(1, group)]
            sofar = call(
                functools.partial(early_kernel, turns[:-1]),
                shape((rows, chunk), F32),
                (*[gathered[i] for i in turns[:-1]], choice),
                flops=2 * rows * rows * EXPERTS * chunk,
            )
            half = call(
                functools.partial(pick_kernel, turns[-1]),
                shape((rows, chunk)),
                (sofar, gathered[turns[-1]], choice, *kept),
            )
            halves = [half] + [within(half, m) for m in range(1, group)]
            begun = call(
                functools.partial(half_kernel, group, tick),
                [shape((rows, inner), F32)] * 2 + [shape((rows, LANES), F32)],
                (half, *weights[:3]),
                flops=flops // (3 * group) * 2,
            )
            outs = [shape((rows, inner))] + [shape((rows, chunk))] * (group - 1)
            scratch = []
            if last:
                outs = [shape((slots, width))] * (group + 1)
                scratch = [pltpu.VMEM((rows, width), F32)] * 2
            outs = call(
                functools.partial(rest_kernel, group, tick, last),
                outs,
                (*halves, *begun, *weights),
                scratch=scratch,
                flops=flops // 2,
            )
        else:
            outs = call(
                functools.partial(whole_kernel, group, tick),
                [shape((rows, inner))] + [shape((rows, chunk))] * (group - 1),
                (whole, *weights),
                flops=flops * 5 // 6,
            )
        terms = [within(outs[m], m) for m in range(1, group)]
        if last:
            terms = [outs[0]] + terms
        else:
            own = call(
                functools.partial(own_kernel, group, tick),
                shape((rows, chunk)),
                (outs[0], w_down),
                flops=flops // 6,
            )
            terms = [own] + terms
        if not last:
            latest, marked = call(
                functools.partial(update_kernel, group),
                [shape((rows, chunk)), shape((rows, chunk + LANES))],
                (*terms, half, table, scale),
            )
            saved.append(latest)
    leaving = call(
        functools.partial(leave_kernel, group),
        [shape((CAP, width))] * EXPERTS,
        (*terms, outs[group], scale, *kept),
        scratch=[pltpu.VMEM((slots, width), F32)],
    )
    back = [across(leaving[i], i) for i in range(EXPERTS)]
    return call(
        functools.partial(home_kernel, group),
        shape((1, count, width)),
        (*back, sent[0][:, width : width + LANES]),
        scratch=[pltpu.VMEM((slots, width), F32)],
    )


def gather_turns(tick):
    far = EXPERTS - 1
    return [0, far, *range(2, far)] if tick in RELAYED else [far, *range(far)]


def solution(mesh):
    return jax.shard_map(
        local,
        mesh=mesh,
        in_specs=(
            P("expert", None),
            P("section", "expert", None),
            P("section", "expert"),
            P("section", None),
            P("section", None, "expert"),
            P("section", None, "expert"),
            P("section", "expert", None),
        ),
        out_specs=P("section", "expert", None),
        check_vma=False,
    )
```

```python
import functools

import jax
import jax.numpy as jnp
from jax import lax
from jax.experimental import pallas as pl
from jax.experimental.pallas import tpu as pltpu
from jax.sharding import PartitionSpec as P


EXPERTS = 4
CAP = 2
LANES = 128
BLOCKS = 4
RELAYED = (0,)
START_FLOPS = 10_000_000_000
F32 = jnp.float32
BF16 = jnp.bfloat16
VMEM = pl.BlockSpec(memory_space=pltpu.VMEM)


def call(kernel, outs, args, limit=4 << 20, scratch=(), flops=1000, specs=None, moved=None):
    if moved is None:
        moved = sum(a.size * a.dtype.itemsize for a in args)
    return pl.pallas_call(
        kernel,
        out_shape=outs,
        in_specs=specs or [VMEM] * len(args),
        out_specs=jax.tree.map(lambda _: VMEM, outs),
        scratch_shapes=scratch,
        compiler_params=pltpu.CompilerParams(vmem_limit_bytes=limit),
        cost_estimate=pl.CostEstimate(flops=flops, bytes_accessed=moved, transcendentals=0),
    )(*args)


def shape(dims, kind=BF16):
    return jax.ShapeDtypeStruct(dims, kind)


def place(group):
    index = lax.axis_index("expert")
    return index // group, lax.rem(index, group)


def iota(dims, axis):
    return lax.broadcasted_iota(jnp.int32, dims, axis)


def code_kernel(group, out):
    expert, _ = place(group)
    index = iota(out.shape, 0)
    out[...] = ((expert ^ (index // CAP)) * CAP + lax.rem(index, CAP)).astype(F32)


def slot_kernel(wanted, tokens, ids, scale, *outs):
    rows = tokens.shape[0]
    width = tokens.shape[1]
    ids_row = ids[...]
    ids_full = jnp.broadcast_to(ids_row, (rows, rows))
    diagonal = iota((rows, rows), 0) == iota((rows, rows), 1)
    ids_column = jnp.sum(jnp.where(diagonal, ids_full, 0), axis=1, keepdims=True)
    earlier = iota((rows, rows), 0) < iota((rows, rows), 1)
    rank = jnp.sum(jnp.where((ids_full == ids_column) & earlier, 1, 0), axis=0, keepdims=True)
    position = (ids_row * CAP + rank).astype(F32)
    chosen = jnp.where(position == wanted[:, 0:rows], 1.0, 0.0).astype(BF16)
    body = jnp.dot(chosen, tokens[...], preferred_element_type=F32)
    value = scale[...]
    first = value.astype(BF16).astype(F32)
    second = (value - first).astype(BF16).astype(F32)
    third = value - first - second
    for i in range(EXPERTS):
        outs[i][:, 0:width] = body[i * CAP : (i + 1) * CAP, :].astype(BF16)
        outs[i][:, width:] = jnp.full((CAP, BLOCKS * LANES), -1.0, BF16)
        for n, piece in enumerate((position, first, second, third)):
            at = width + n * LANES
            outs[i][:, at : at + rows] = jnp.broadcast_to(piece, (CAP, rows)).astype(BF16)


def hidden_of(gate, upward):
    return (gate / (1.0 + jnp.exp(-gate)) * upward).astype(BF16)


def down(hidden, w_down, first, out):
    step = min(512, out.shape[1])
    for n in range(0, out.shape[1], step):
        at = first + n if isinstance(first, int) else pl.multiple_of(first + n, step)
        out[:, n : n + step] = jnp.dot(
            hidden, w_down[0, :, pl.ds(at, step)], preferred_element_type=F32
        ).astype(out.dtype)


def active(tick):
    return pl.when(lax.axis_index("section") == tick)


def deal_rows(source, blocks, own):
    slots = blocks[0].shape[0]
    for m in range(len(blocks)):
        at = pl.multiple_of((own ^ m) * slots, slots)
        blocks[m][...] = source[pl.ds(at, slots), :].astype(BF16)


def join_kernel(group, width, *refs):
    count = group * EXPERTS
    whole, half, table, scale = refs[count : count + 4]
    block, rows = refs[count + 4 :]
    expert, own = place(group)
    slots = EXPERTS * CAP
    for m in range(group):
        for i in range(EXPERTS):
            block[i * CAP : (i + 1) * CAP, :] = refs[m * EXPERTS + i][...].astype(F32)
        at = pl.multiple_of((own ^ m) * slots, slots)
        rows[pl.ds(at, slots), :] = block[...]
    table[...] = rows[:, width : width + LANES].astype(BF16)
    scale[...] = scales(expert, rows[:, width:])
    at = pl.multiple_of(own * half.shape[1], half.shape[1])
    half[...] = rows[:, pl.ds(at, half.shape[1])].astype(BF16)
    whole[...] = rows[:, 0:width].astype(BF16)


def whole_kernel(group, tick, rows, gain, w_gate, w_up, w_down, *outs):
    _, own = place(group)

    @active(tick)
    def _():
        values = rows[...].astype(F32)
        inverse = lax.rsqrt(jnp.mean(values * values, axis=-1, keepdims=True) + 1e-06)
        normed = (values * inverse * gain[...]).astype(BF16)
        gate = jnp.dot(normed, w_gate[0], preferred_element_type=F32)
        upward = jnp.dot(normed, w_up[0], preferred_element_type=F32)
        hidden = hidden_of(gate, upward)
        outs[0][...] = hidden
        width = outs[1].shape[1]
        for m in range(1, group):
            down(hidden, w_down, pl.multiple_of((own ^ m) * width, width), outs[m])


def products(half, at, gain, w_gate, w_up):
    width = half.shape[1]
    values = half[...].astype(F32)
    scaled = (values * gain[:, pl.ds(at, width)]).astype(BF16)
    gate = jnp.dot(scaled, w_gate[0, pl.ds(at, width), :], preferred_element_type=F32)
    upward = jnp.dot(scaled, w_up[0, pl.ds(at, width), :], preferred_element_type=F32)
    return gate, upward, jnp.sum(values * values, axis=-1, keepdims=True)


def half_kernel(group, tick, half, gain, w_gate, w_up, gate_out, up_out, square_out):
    _, own = place(group)

    @active(tick)
    def _():
        width = half.shape[1]
        at = pl.multiple_of(own * width, width)
        gate, upward, square = products(half, at, gain, w_gate, w_up)
        gate_out[...] = gate
        up_out[...] = upward
        square_out[...] = jnp.broadcast_to(square, square_out.shape)


def rest_kernel(group, tick, last, *refs):
    halves = refs[:group]
    gate_in, up_in, square_in, gain, w_gate, w_up, w_down = refs[group : group + 7]
    outs = refs[group + 7 :]
    _, own = place(group)

    @active(tick)
    def _():
        gate, upward, square = gate_in[...], up_in[...], square_in[:, 0:1]
        width = halves[0].shape[1]
        for m in range(1, group):
            at = pl.multiple_of((own ^ m) * width, width)
            more = products(halves[m], at, gain, w_gate, w_up)
            gate, upward, square = gate + more[0], upward + more[1], square + more[2]
        inverse = lax.rsqrt(square / gain.shape[1] + 1e-06)
        hidden = hidden_of(gate * inverse, upward * inverse)
        if last:
            rows, parts = outs[-2:]
            for m in range(group):
                at = pl.multiple_of((own ^ m) * width, width)
                rows[:, pl.ds(at, width)] = halves[m][...].astype(F32)
            down(hidden, w_down, 0, parts)
            deal_rows(parts, outs[:group], own)
            deal_rows(rows, outs[group : group + 1], own)
        else:
            outs[0][...] = hidden
            for m in range(1, group):
                down(hidden, w_down, pl.multiple_of((own ^ m) * width, width), outs[m])


def own_kernel(group, tick, hidden, w_down, out):
    _, own = place(group)

    @active(tick)
    def _():
        down(hidden[...], w_down, pl.multiple_of(own * out.shape[1], out.shape[1]), out)


def slot_codes(expert, dims):
    return expert * CAP + lax.rem(iota(dims, 0), CAP)


def scales(expert, table):
    rows = table.shape[0]
    mine = table[:, 0:LANES] == slot_codes(expert, (rows, LANES)).astype(F32)
    scale = sum(table[:, n * LANES : (n + 1) * LANES] for n in range(1, BLOCKS))
    scale = jnp.sum(jnp.where(mine, scale, 0.0), axis=1, keepdims=True)
    return jnp.broadcast_to(scale, (rows, LANES))


def updated(pieces, before, scale):
    total = pieces[0][...].astype(F32)
    for piece in pieces[1:]:
        total = total + piece[...].astype(F32)
    return before[...].astype(F32) + scale * total


def update_kernel(group, *refs):
    half, table, scale, out, marked = refs[group : group + 5]
    width = out.shape[1]
    result = updated(refs[:group], half, scale[:, 0:1]).astype(BF16)
    out[...] = result
    marked[:, 0:width] = result
    marked[:, width:] = table[...]


def keep_kernel(group, saved, *refs):
    outs, buffer = refs[saved : saved + group], refs[-1]
    section = lax.axis_index("section")
    _, own = place(group)
    for n in range(saved):

        @pl.when(section == n)
        def _(n=n):
            buffer[...] = refs[n][...].astype(F32)

    deal_rows(buffer, outs, own)


def leave_kernel(group, *refs):
    before, scale = refs[group : group + 2]
    kept = refs[group + 2 : 2 * group + 2]
    outs = refs[2 * group + 2 : 2 * group + 2 + EXPERTS]
    rows = refs[-1]
    slots = EXPERTS * CAP
    final = lax.axis_size("section") - 1
    section = lax.axis_index("section")
    _, own = place(group)

    @pl.when(section == final)
    def _():
        at = pl.multiple_of(own * slots, slots)
        rows[...] = updated(refs[:group], before, scale[pl.ds(at, slots), :][:, 0:1])

    @pl.when(section != final)
    def _():
        width = kept[0].shape[1]
        for m in range(group):
            at = pl.multiple_of((own ^ m) * width, width)
            rows[:, pl.ds(at, width)] = kept[m][...].astype(F32)

    for i in range(EXPERTS):
        outs[i][...] = rows[i * CAP : (i + 1) * CAP, :].astype(BF16)


def choice_kernel(group, current, before, out):
    expert, _ = place(group)
    rows = current.shape[0]
    span = EXPERTS * CAP
    here = current[...].astype(F32)
    there = before[:, before.shape[1] - LANES :].astype(F32)
    mine = jnp.where(here == slot_codes(expert, here.shape).astype(F32), 1.0, 0.0).astype(BF16)
    a, b = iota((rows, rows), 0), iota((rows, rows), 1)
    for i in range(EXPERTS):
        codes = slot_codes(expert ^ i, there.shape).astype(F32)
        theirs = jnp.where(there == codes, 1.0, 0.0).astype(BF16)
        both = lax.dot_general(
            mine, theirs, (((1,), (1,)), ((), ())), preferred_element_type=F32
        )
        both = jnp.where(a // CAP == b // CAP, both, 0.0).astype(BF16)
        moved = (a // span) * span + (((lax.rem(a, span) // CAP) ^ i) * CAP) + lax.rem(a, CAP)
        order = jnp.where(moved == b, 1.0, 0.0).astype(BF16)
        out[i] = jnp.dot(both, order, preferred_element_type=F32).astype(BF16)


def early_kernel(turns, *refs):
    choice, out = refs[-2], refs[-1]
    width = out.shape[1]
    total = 0.0
    for n, i in enumerate(turns):
        total = total + jnp.dot(choice[i], refs[n][:, 0:width], preferred_element_type=F32)
    out[...] = total


def pick_kernel(i, *refs):
    sofar, last, choice, out = refs[0], refs[1], refs[2], refs[-1]
    piece = last[:, 0 : out.shape[1]]
    total = sofar[...] + jnp.dot(choice[i], piece, preferred_element_type=F32)
    out[...] = total.astype(BF16)


def home_kernel(group, *refs):
    table, out, block = refs[EXPERTS:]
    expert, _ = place(group)
    slots = EXPERTS * CAP
    count = out.shape[1]
    for i in range(EXPERTS):
        block[i * CAP : (i + 1) * CAP, :] = refs[i][...].astype(F32)
    lanes = -(-count // 16) * 16
    position = jnp.broadcast_to(table[0:1, 0:lanes].astype(F32), (slots, lanes))
    index = iota((slots, lanes), 0)
    wanted = (expert ^ (index // CAP)) * CAP + lax.rem(index, CAP)
    chosen = jnp.where(position == wanted.astype(F32), 1.0, 0.0).astype(BF16)
    full = lax.dot_general(
        chosen, block[...].astype(BF16), (((0,), (0,)), ((), ())), preferred_element_type=F32
    )
    out[0] = full[0:count, :].astype(BF16)


def local(tokens, expert_ids, gate_scale, norm_gain, w_gate, w_up, w_down):
    peers = lax.axis_size("expert")
    sections = lax.axis_size("section")
    count, width = tokens.shape
    group = peers // EXPERTS
    chunk = width // group
    rows = peers * CAP
    slots = EXPERTS * CAP
    wide = width + BLOCKS * LANES
    weights = (norm_gain, w_gate, w_up, w_down)

    def across(value, i):
        pairs = [(d, (d // group ^ i) * group + d % group) for d in range(peers)]
        if i == 0:
            return value
        return lax.ppermute(value, "expert", pairs)

    def within(value, m):
        return lax.ppermute(value, "expert", [(d, d ^ m) for d in range(peers)])

    def gather(value, marked, tick):
        outs = {}
        turns = gather_turns(tick)
        for i in turns:
            ring = [tick, tick + 1]
            if i == turns[0] and sections > 2:
                ring.append((tick + 2) % sections)
            pairs = []
            for s in range(sections):
                to, move = s, lambda d: d ^ 1
                if s in ring:
                    to = ring[(ring.index(s) + 1) % len(ring)]
                    move = lambda d: d
                if s == tick:
                    move = lambda d: (d // group ^ i) * group + d % group
                pairs += [(s * peers + d, to * peers + move(d)) for d in range(peers)]
            outs[i] = lax.ppermute(value if i else marked, ("section", "expert"), pairs)
        if 1 not in outs:
            pairs = [
                (s * peers + d, s * peers + ((d // group ^ 1) * group + d % group if s == tick + 1 else d ^ 1))
                for s in range(sections)
                for d in range(peers)
            ]
            outs[1] = lax.ppermute(outs[0], ("section", "expert"), pairs)
            turns = [*turns, 1]
        return outs, turns

    wanted = call(
        functools.partial(code_kernel, group), shape((slots, LANES), F32), (), flops=START_FLOPS
    )
    sent = call(
        slot_kernel,
        [shape((CAP, wide))] * EXPERTS,
        (wanted, tokens, expert_ids.reshape(1, count), gate_scale),
    )
    arrived = [across(sent[i], i) for i in range(EXPERTS)]
    pieces = list(arrived)
    for m in range(1, group):
        for i, piece in enumerate(arrived):
            if i == EXPERTS - 2:
                pairs = [
                    (d, (d // group ^ i) * group + (d % group ^ m)) for d in range(peers)
                ]
                pieces.append(lax.ppermute(sent[i], "expert", pairs))
            else:
                pieces.append(within(piece, m))
    flops = 6 * rows * width * w_gate.shape[2]
    whole, half, table, scale = call(
        functools.partial(join_kernel, group, width),
        [
            shape((rows, width)),
            shape((rows, chunk)),
            shape((rows, LANES)),
            shape((rows, LANES), F32),
        ],
        tuple(pieces),
        scratch=[pltpu.VMEM((slots, wide), F32), pltpu.VMEM((rows, wide), F32)],
    )
    saved = []
    inner = w_gate.shape[2]
    for tick in range(sections):
        last = tick == sections - 1
        if tick:
            gathered, turns = gather(saved[-1], marked, tick - 1)
            choice = call(
                functools.partial(choice_kernel, group),
                shape((EXPERTS, rows, rows)),
                (table, gathered[0]),
            )
            kept = []
            if last:
                kept = call(
                    functools.partial(keep_kernel, group, len(saved)),
                    [shape((slots, chunk))] * group,
                    tuple(saved),
                    scratch=[pltpu.VMEM((rows, chunk), F32)],
                )
                kept = [kept[0]] + [within(kept[m], m) for m in range(1, group)]
            sofar = call(
                functools.partial(early_kernel, turns[:-1]),
                shape((rows, chunk), F32),
                (*[gathered[i] for i in turns[:-1]], choice),
                flops=2 * rows * rows * EXPERTS * chunk,
            )
            half = call(
                functools.partial(pick_kernel, turns[-1]),
                shape((rows, chunk)),
                (sofar, gathered[turns[-1]], choice, *kept),
            )
            halves = [half] + [within(half, m) for m in range(1, group)]
            begun = call(
                functools.partial(half_kernel, group, tick),
                [shape((rows, inner), F32)] * 2 + [shape((rows, LANES), F32)],
                (half, *weights[:3]),
                flops=flops // (3 * group) * 2,
            )
            outs = [shape((rows, inner))] + [shape((rows, chunk))] * (group - 1)
            scratch = []
            if last:
                outs = [shape((slots, width))] * (group + 1)
                scratch = [pltpu.VMEM((rows, width), F32)] * 2
            outs = call(
                functools.partial(rest_kernel, group, tick, last),
                outs,
                (*halves, *begun, *weights),
                scratch=scratch,
                flops=flops // 2,
            )
        else:
            outs = call(
                functools.partial(whole_kernel, group, tick),
                [shape((rows, inner))] + [shape((rows, chunk))] * (group - 1),
                (whole, *weights),
                flops=flops * 5 // 6,
            )
        terms = [within(outs[m], m) for m in range(1, group)]
        if last:
            terms = [outs[0]] + terms
        else:
            own = call(
                functools.partial(own_kernel, group, tick),
                shape((rows, chunk)),
                (outs[0], w_down),
                flops=flops // 6,
            )
            terms = [own] + terms
        if not last:
            latest, marked = call(
                functools.partial(update_kernel, group),
                [shape((rows, chunk)), shape((rows, chunk + LANES))],
                (*terms, half, table, scale),
            )
            saved.append(latest)
    leaving = call(
        functools.partial(leave_kernel, group),
        [shape((CAP, width))] * EXPERTS,
        (*terms, outs[group], scale, *kept),
        scratch=[pltpu.VMEM((slots, width), F32)],
    )
    back = [across(leaving[i], i) for i in range(EXPERTS)]
    return call(
        functools.partial(home_kernel, group),
        shape((1, count, width)),
        (*back, sent[0][:, width : width + LANES]),
        scratch=[pltpu.VMEM((slots, width), F32)],
    )


def gather_turns(tick):
    far = EXPERTS - 1
    return [0, far, *range(2, far)] if tick in RELAYED else [far, *range(far)]


def solution(mesh):
    return jax.shard_map(
        local,
        mesh=mesh,
        in_specs=(
            P("expert", None),
            P("section", "expert", None),
            P("section", "expert"),
            P("section", None),
            P("section", None, "expert"),
            P("section", None, "expert"),
            P("section", "expert", None),
        ),
        out_specs=P("section", "expert", None),
        check_vma=False,
    )
```

```python
import functools

import jax
import jax.numpy as jnp
from jax import lax
from jax.experimental import pallas as pl
from jax.experimental.pallas import tpu as pltpu
from jax.sharding import PartitionSpec as P


EXPERTS = 4
CAP = 2
LANES = 128
BLOCKS = 4
RELAYED = (0,)
START_FLOPS = 10_000_000_000
F32 = jnp.float32
BF16 = jnp.bfloat16
VMEM = pl.BlockSpec(memory_space=pltpu.VMEM)


def call(kernel, outs, args, limit=4 << 20, scratch=(), flops=1000, specs=None, moved=None):
    if moved is None:
        moved = sum(a.size * a.dtype.itemsize for a in args)
    return pl.pallas_call(
        kernel,
        out_shape=outs,
        in_specs=specs or [VMEM] * len(args),
        out_specs=jax.tree.map(lambda _: VMEM, outs),
        scratch_shapes=scratch,
        compiler_params=pltpu.CompilerParams(vmem_limit_bytes=limit),
        cost_estimate=pl.CostEstimate(flops=flops, bytes_accessed=moved, transcendentals=0),
    )(*args)


def shape(dims, kind=BF16):
    return jax.ShapeDtypeStruct(dims, kind)


def place(group):
    index = lax.axis_index("expert")
    return index // group, lax.rem(index, group)


def iota(dims, axis):
    return lax.broadcasted_iota(jnp.int32, dims, axis)


def code_kernel(group, out):
    expert, _ = place(group)
    index = iota(out.shape, 0)
    out[...] = ((expert ^ (index // CAP)) * CAP + lax.rem(index, CAP)).astype(F32)


def slot_kernel(wanted, tokens, ids, scale, *outs):
    rows = tokens.shape[0]
    width = tokens.shape[1]
    ids_row = ids[...]
    ids_full = jnp.broadcast_to(ids_row, (rows, rows))
    diagonal = iota((rows, rows), 0) == iota((rows, rows), 1)
    ids_column = jnp.sum(jnp.where(diagonal, ids_full, 0), axis=1, keepdims=True)
    earlier = iota((rows, rows), 0) < iota((rows, rows), 1)
    rank = jnp.sum(jnp.where((ids_full == ids_column) & earlier, 1, 0), axis=0, keepdims=True)
    position = (ids_row * CAP + rank).astype(F32)
    chosen = jnp.where(position == wanted[:, 0:rows], 1.0, 0.0).astype(BF16)
    body = jnp.dot(chosen, tokens[...], preferred_element_type=F32)
    value = scale[...]
    first = value.astype(BF16).astype(F32)
    second = (value - first).astype(BF16).astype(F32)
    third = value - first - second
    for i in range(EXPERTS):
        outs[i][:, 0:width] = body[i * CAP : (i + 1) * CAP, :].astype(BF16)
        outs[i][:, width:] = jnp.full((CAP, BLOCKS * LANES), -1.0, BF16)
        for n, piece in enumerate((position, first, second, third)):
            at = width + n * LANES
            outs[i][:, at : at + rows] = jnp.broadcast_to(piece, (CAP, rows)).astype(BF16)


def hidden_of(gate, upward):
    return (gate / (1.0 + jnp.exp(-gate)) * upward).astype(BF16)


def down(hidden, w_down, first, out):
    step = min(512, out.shape[1])
    for n in range(0, out.shape[1], step):
        at = first + n if isinstance(first, int) else pl.multiple_of(first + n, step)
        out[:, n : n + step] = jnp.dot(
            hidden, w_down[0, :, pl.ds(at, step)], preferred_element_type=F32
        ).astype(out.dtype)


def active(tick):
    return pl.when(lax.axis_index("section") == tick)


def deal_rows(source, blocks, own):
    slots = blocks[0].shape[0]
    for m in range(len(blocks)):
        at = pl.multiple_of((own ^ m) * slots, slots)
        blocks[m][...] = source[pl.ds(at, slots), :].astype(BF16)


def assemble(group, pieces, block, rows, width):
    _, own = place(group)
    slots = EXPERTS * CAP
    for m in range(group):
        for i in range(EXPERTS):
            piece = pieces[m * EXPERTS + i]
            block[i * CAP : (i + 1) * CAP, :] = piece[:, 0:width].astype(F32)
        at = pl.multiple_of((own ^ m) * slots, slots)
        rows[pl.ds(at, slots), :] = block[...]


def join_kernel(group, width, *refs):
    count = group * EXPERTS
    half, table, scale = refs[count : count + 3]
    block, rows = refs[count + 3 :]
    expert, own = place(group)
    assemble(group, refs[:count], block, rows, rows.shape[1])
    table[...] = rows[:, width : width + LANES].astype(BF16)
    scale[...] = scales(expert, rows[:, width:])
    at = pl.multiple_of(own * half.shape[1], half.shape[1])
    half[...] = rows[:, pl.ds(at, half.shape[1])].astype(BF16)


def whole_kernel(group, tick, *refs):
    count = group * EXPERTS
    gain, w_gate, w_up, w_down = refs[count : count + 4]
    outs = refs[count + 4 : -2]
    block, rows = refs[-2:]
    _, own = place(group)

    @active(tick)
    def _():
        assemble(group, refs[:count], block, rows, rows.shape[1])
        values = rows[...]
        inverse = lax.rsqrt(jnp.mean(values * values, axis=-1, keepdims=True) + 1e-06)
        normed = (values * inverse * gain[...]).astype(BF16)
        gate = jnp.dot(normed, w_gate[0], preferred_element_type=F32)
        upward = jnp.dot(normed, w_up[0], preferred_element_type=F32)
        hidden = hidden_of(gate, upward)
        outs[0][...] = hidden
        width = outs[1].shape[1]
        for m in range(1, group):
            down(hidden, w_down, pl.multiple_of((own ^ m) * width, width), outs[m])


def products(half, at, gain, w_gate, w_up):
    width = half.shape[1]
    values = half[...].astype(F32)
    scaled = (values * gain[:, pl.ds(at, width)]).astype(BF16)
    gate = jnp.dot(scaled, w_gate[0, pl.ds(at, width), :], preferred_element_type=F32)
    upward = jnp.dot(scaled, w_up[0, pl.ds(at, width), :], preferred_element_type=F32)
    return gate, upward, jnp.sum(values * values, axis=-1, keepdims=True)


def half_kernel(group, tick, half, gain, w_gate, w_up, gate_out, up_out, square_out):
    _, own = place(group)

    @active(tick)
    def _():
        width = half.shape[1]
        at = pl.multiple_of(own * width, width)
        gate, upward, square = products(half, at, gain, w_gate, w_up)
        gate_out[...] = gate
        up_out[...] = upward
        square_out[...] = jnp.broadcast_to(square, square_out.shape)


def rest_kernel(group, tick, last, *refs):
    halves = refs[:group]
    gate_in, up_in, square_in, gain, w_gate, w_up, w_down = refs[group : group + 7]
    outs = refs[group + 7 :]
    _, own = place(group)

    @active(tick)
    def _():
        gate, upward, square = gate_in[...], up_in[...], square_in[:, 0:1]
        width = halves[0].shape[1]
        for m in range(1, group):
            at = pl.multiple_of((own ^ m) * width, width)
            more = products(halves[m], at, gain, w_gate, w_up)
            gate, upward, square = gate + more[0], upward + more[1], square + more[2]
        inverse = lax.rsqrt(square / gain.shape[1] + 1e-06)
        hidden = hidden_of(gate * inverse, upward * inverse)
        if last:
            rows, parts = outs[-2:]
            for m in range(group):
                at = pl.multiple_of((own ^ m) * width, width)
                rows[:, pl.ds(at, width)] = halves[m][...].astype(F32)
            down(hidden, w_down, 0, parts)
            deal_rows(parts, outs[:group], own)
            deal_rows(rows, outs[group : group + 1], own)
        else:
            outs[0][...] = hidden
            for m in range(1, group):
                down(hidden, w_down, pl.multiple_of((own ^ m) * width, width), outs[m])


def own_kernel(group, tick, hidden, w_down, out):
    _, own = place(group)

    @active(tick)
    def _():
        down(hidden[...], w_down, pl.multiple_of(own * out.shape[1], out.shape[1]), out)


def slot_codes(expert, dims):
    return expert * CAP + lax.rem(iota(dims, 0), CAP)


def scales(expert, table):
    rows = table.shape[0]
    mine = table[:, 0:LANES] == slot_codes(expert, (rows, LANES)).astype(F32)
    scale = sum(table[:, n * LANES : (n + 1) * LANES] for n in range(1, BLOCKS))
    scale = jnp.sum(jnp.where(mine, scale, 0.0), axis=1, keepdims=True)
    return jnp.broadcast_to(scale, (rows, LANES))


def updated(pieces, before, scale):
    total = pieces[0][...].astype(F32)
    for piece in pieces[1:]:
        total = total + piece[...].astype(F32)
    return before[...].astype(F32) + scale * total


def update_kernel(group, *refs):
    half, table, scale, out, marked = refs[group : group + 5]
    width = out.shape[1]
    result = updated(refs[:group], half, scale[:, 0:1]).astype(BF16)
    out[...] = result
    marked[:, 0:width] = result
    marked[:, width:] = table[...]


def keep_kernel(group, saved, *refs):
    outs, buffer = refs[saved : saved + group], refs[-1]
    section = lax.axis_index("section")
    _, own = place(group)
    for n in range(saved):

        @pl.when(section == n)
        def _(n=n):
            buffer[...] = refs[n][...].astype(F32)

    deal_rows(buffer, outs, own)


def leave_kernel(group, *refs):
    before, scale = refs[group : group + 2]
    kept = refs[group + 2 : 2 * group + 2]
    outs = refs[2 * group + 2 : 2 * group + 2 + EXPERTS]
    rows = refs[-1]
    slots = EXPERTS * CAP
    final = lax.axis_size("section") - 1
    section = lax.axis_index("section")
    _, own = place(group)

    @pl.when(section == final)
    def _():
        at = pl.multiple_of(own * slots, slots)
        rows[...] = updated(refs[:group], before, scale[pl.ds(at, slots), :][:, 0:1])

    @pl.when(section != final)
    def _():
        width = kept[0].shape[1]
        for m in range(group):
            at = pl.multiple_of((own ^ m) * width, width)
            rows[:, pl.ds(at, width)] = kept[m][...].astype(F32)

    for i in range(EXPERTS):
        outs[i][...] = rows[i * CAP : (i + 1) * CAP, :].astype(BF16)


def choice_kernel(group, current, before, out):
    expert, _ = place(group)
    rows = current.shape[0]
    span = EXPERTS * CAP
    here = current[...].astype(F32)
    there = before[:, before.shape[1] - LANES :].astype(F32)
    mine = jnp.where(here == slot_codes(expert, here.shape).astype(F32), 1.0, 0.0).astype(BF16)
    a, b = iota((rows, rows), 0), iota((rows, rows), 1)
    for i in range(EXPERTS):
        codes = slot_codes(expert ^ i, there.shape).astype(F32)
        theirs = jnp.where(there == codes, 1.0, 0.0).astype(BF16)
        both = lax.dot_general(
            mine, theirs, (((1,), (1,)), ((), ())), preferred_element_type=F32
        )
        both = jnp.where(a // CAP == b // CAP, both, 0.0).astype(BF16)
        moved = (a // span) * span + (((lax.rem(a, span) // CAP) ^ i) * CAP) + lax.rem(a, CAP)
        order = jnp.where(moved == b, 1.0, 0.0).astype(BF16)
        out[i] = jnp.dot(both, order, preferred_element_type=F32).astype(BF16)


def early_kernel(turns, *refs):
    choice, out = refs[-2], refs[-1]
    width = out.shape[1]
    total = 0.0
    for n, i in enumerate(turns):
        total = total + jnp.dot(choice[i], refs[n][:, 0:width], preferred_element_type=F32)
    out[...] = total


def pick_kernel(i, *refs):
    sofar, last, choice, out = refs[0], refs[1], refs[2], refs[-1]
    piece = last[:, 0 : out.shape[1]]
    total = sofar[...] + jnp.dot(choice[i], piece, preferred_element_type=F32)
    out[...] = total.astype(BF16)


def home_kernel(group, *refs):
    table, out, block = refs[EXPERTS:]
    expert, _ = place(group)
    slots = EXPERTS * CAP
    count = out.shape[1]
    for i in range(EXPERTS):
        block[i * CAP : (i + 1) * CAP, :] = refs[i][...].astype(F32)
    lanes = -(-count // 16) * 16
    position = jnp.broadcast_to(table[0:1, 0:lanes].astype(F32), (slots, lanes))
    index = iota((slots, lanes), 0)
    wanted = (expert ^ (index // CAP)) * CAP + lax.rem(index, CAP)
    chosen = jnp.where(position == wanted.astype(F32), 1.0, 0.0).astype(BF16)
    full = lax.dot_general(
        chosen, block[...].astype(BF16), (((0,), (0,)), ((), ())), preferred_element_type=F32
    )
    out[0] = full[0:count, :].astype(BF16)


def local(tokens, expert_ids, gate_scale, norm_gain, w_gate, w_up, w_down):
    peers = lax.axis_size("expert")
    sections = lax.axis_size("section")
    count, width = tokens.shape
    group = peers // EXPERTS
    chunk = width // group
    rows = peers * CAP
    slots = EXPERTS * CAP
    wide = width + BLOCKS * LANES
    weights = (norm_gain, w_gate, w_up, w_down)

    def across(value, i):
        pairs = [(d, (d // group ^ i) * group + d % group) for d in range(peers)]
        if i == 0:
            return value
        return lax.ppermute(value, "expert", pairs)

    def within(value, m):
        return lax.ppermute(value, "expert", [(d, d ^ m) for d in range(peers)])

    def gather(value, marked, tick):
        outs = {}
        turns = gather_turns(tick)
        for i in turns:
            ring = [tick, tick + 1]
            if i == turns[0] and sections > 2:
                ring.append((tick + 2) % sections)
            pairs = []
            for s in range(sections):
                to, move = s, lambda d: d ^ 1
                if s in ring:
                    to = ring[(ring.index(s) + 1) % len(ring)]
                    move = lambda d: d
                if s == tick:
                    move = lambda d: (d // group ^ i) * group + d % group
                pairs += [(s * peers + d, to * peers + move(d)) for d in range(peers)]
            outs[i] = lax.ppermute(value if i else marked, ("section", "expert"), pairs)
        if 1 not in outs:
            pairs = [
                (s * peers + d, s * peers + ((d // group ^ 1) * group + d % group if s == tick + 1 else d ^ 1))
                for s in range(sections)
                for d in range(peers)
            ]
            outs[1] = lax.ppermute(outs[0], ("section", "expert"), pairs)
            turns = [*turns, 1]
        return outs, turns

    wanted = call(
        functools.partial(code_kernel, group), shape((slots, LANES), F32), (), flops=START_FLOPS
    )
    sent = call(
        slot_kernel,
        [shape((CAP, wide))] * EXPERTS,
        (wanted, tokens, expert_ids.reshape(1, count), gate_scale),
    )
    arrived = [across(sent[i], i) for i in range(EXPERTS)]
    pieces = list(arrived)
    for m in range(1, group):
        for i, piece in enumerate(arrived):
            if i == EXPERTS - 2:
                pairs = [
                    (d, (d // group ^ i) * group + (d % group ^ m)) for d in range(peers)
                ]
                pieces.append(lax.ppermute(sent[i], "expert", pairs))
            else:
                pieces.append(within(piece, m))
    flops = 6 * rows * width * w_gate.shape[2]
    half, table, scale = call(
        functools.partial(join_kernel, group, width),
        [shape((rows, chunk)), shape((rows, LANES)), shape((rows, LANES), F32)],
        tuple(pieces),
        scratch=[pltpu.VMEM((slots, wide), F32), pltpu.VMEM((rows, wide), F32)],
    )
    saved = []
    inner = w_gate.shape[2]
    for tick in range(sections):
        last = tick == sections - 1
        if tick:
            gathered, turns = gather(saved[-1], marked, tick - 1)
            choice = call(
                functools.partial(choice_kernel, group),
                shape((EXPERTS, rows, rows)),
                (table, gathered[0]),
            )
            kept = []
            if last:
                kept = call(
                    functools.partial(keep_kernel, group, len(saved)),
                    [shape((slots, chunk))] * group,
                    tuple(saved),
                    scratch=[pltpu.VMEM((rows, chunk), F32)],
                )
                kept = [kept[0]] + [within(kept[m], m) for m in range(1, group)]
            sofar = call(
                functools.partial(early_kernel, turns[:-1]),
                shape((rows, chunk), F32),
                (*[gathered[i] for i in turns[:-1]], choice),
                flops=2 * rows * rows * EXPERTS * chunk,
            )
            half = call(
                functools.partial(pick_kernel, turns[-1]),
                shape((rows, chunk)),
                (sofar, gathered[turns[-1]], choice, *kept),
            )
            halves = [half] + [within(half, m) for m in range(1, group)]
            begun = call(
                functools.partial(half_kernel, group, tick),
                [shape((rows, inner), F32)] * 2 + [shape((rows, LANES), F32)],
                (half, *weights[:3]),
                flops=flops // (3 * group) * 2,
            )
            outs = [shape((rows, inner))] + [shape((rows, chunk))] * (group - 1)
            scratch = []
            if last:
                outs = [shape((slots, width))] * (group + 1)
                scratch = [pltpu.VMEM((rows, width), F32)] * 2
            outs = call(
                functools.partial(rest_kernel, group, tick, last),
                outs,
                (*halves, *begun, *weights),
                scratch=scratch,
                flops=flops // 2,
            )
        else:
            outs = call(
                functools.partial(whole_kernel, group, tick),
                [shape((rows, inner))] + [shape((rows, chunk))] * (group - 1),
                (*pieces, *weights),
                scratch=[pltpu.VMEM((slots, width), F32), pltpu.VMEM((rows, width), F32)],
                flops=flops * 5 // 6,
            )
        terms = [within(outs[m], m) for m in range(1, group)]
        if last:
            terms = [outs[0]] + terms
        else:
            own = call(
                functools.partial(own_kernel, group, tick),
                shape((rows, chunk)),
                (outs[0], w_down),
                flops=flops // 6,
            )
            terms = [own] + terms
        if not last:
            latest, marked = call(
                functools.partial(update_kernel, group),
                [shape((rows, chunk)), shape((rows, chunk + LANES))],
                (*terms, half, table, scale),
            )
            saved.append(latest)
    leaving = call(
        functools.partial(leave_kernel, group),
        [shape((CAP, width))] * EXPERTS,
        (*terms, outs[group], scale, *kept),
        scratch=[pltpu.VMEM((slots, width), F32)],
    )
    back = [across(leaving[i], i) for i in range(EXPERTS)]
    return call(
        functools.partial(home_kernel, group),
        shape((1, count, width)),
        (*back, sent[0][:, width : width + LANES]),
        scratch=[pltpu.VMEM((slots, width), F32)],
    )


def gather_turns(tick):
    far = EXPERTS - 1
    return [0, far, *range(2, far)] if tick in RELAYED else [far, *range(far)]


def solution(mesh):
    return jax.shard_map(
        local,
        mesh=mesh,
        in_specs=(
            P("expert", None),
            P("section", "expert", None),
            P("section", "expert"),
            P("section", None),
            P("section", None, "expert"),
            P("section", None, "expert"),
            P("section", "expert", None),
        ),
        out_specs=P("section", "expert", None),
        check_vma=False,
    )
```
